128 devices in a mesh: row: 8 (over x, core), col: 16 (over y, z).
Axes of the slice: x: 4, y: 4, z: 4, core: 2. Of those that a mesh axis runs over, the one named last changes fastest.
Arguments:
- imu: bfloat16 [32768, 128], P(('row', 'col')), may hold values from -30 to 30
- camera: bfloat16 [16, 2048, 128], P('col', 'row'), may hold values from -30 to 30
- imu_mass: float32 [32768], P('row'), may hold values from 0.3 to 3
- cam_mass: float32 [32768], P('col'), may hold values from 0.3 to 3
Outputs:
- grad_imu: float32 [32768, 128], P(('row', 'col'))
- grad_camera: float32 [16, 2048, 128], P('col', 'row')
The draws below stay inside these ranges and needn't reach their ends.
All inputs are finite; a program needn't handle non-finite values.
Results may differ from the reference program's by a relative error of at most 0.0028.
Values may be sent and summed in bfloat16 or wider, within the bound.
A program may use at most 128 MiB of HBM per device.

```python
import math
import jax
import jax.numpy as jnp
from jax import lax

D = 128
ITERS = 3
COL_DEV = 2048
IMU_TOTAL = 32768
CAM_TOTAL = 32768
CAM_BLOCKS = 16


def embeddings(key):
    imu = jax.random.normal(jax.random.fold_in(key, 101), (IMU_TOTAL, D), jnp.float32)
    cams = jax.random.normal(jax.random.fold_in(key, 102), (CAM_TOTAL, D), jnp.float32)
    return (jnp.clip(imu, -30.0, 30.0), jnp.clip(cams, -30.0, 30.0))


def draw_imu(key, part):
    imu, cams = embeddings(key)
    return imu.astype(jnp.bfloat16)


def draw_camera(key, part):
    imu, cams = embeddings(key)
    return cams.reshape(CAM_BLOCKS, COL_DEV, D).astype(jnp.bfloat16)


def steps_of(own_key, dims, shards, least, top_value):
    loudness, own = 1.0, jax.random.fold_in(own_key, 6)
    for position, blocks in shards:
        heights = jnp.exp(jax.random.uniform(jax.random.fold_in(own, position), (blocks,), jnp.float32, least / len(shards), top_value / len(shards)))
        loudness = loudness * jnp.repeat(heights, dims[position] // blocks).reshape([-1 if axis == position else 1 for axis in range(len(dims))])
    return loudness


def setup_inputs(seed: int = 0) -> dict:
    splits = jax.random.split(jax.random.key(seed), 5)
    return {
        "imu": draw_imu(jax.random.fold_in(splits[4], 71), 0),
        "camera": draw_camera(jax.random.fold_in(splits[4], 71), 0),
        "imu_mass": jnp.clip(jnp.exp(math.log(3.0) - 2.3025851 * jax.random.uniform(splits[2], (IMU_TOTAL,), jnp.float32) ** steps_of(splits[2], (IMU_TOTAL,), ((0, 8),), -0.2, 0.2)), 0.3, 3.0),
        "cam_mass": jnp.clip(jnp.exp(math.log(3.0) - 2.3025851 * jax.random.uniform(splits[3], (CAM_TOTAL,), jnp.float32) ** steps_of(splits[3], (CAM_TOTAL,), ((0, 16),), -0.2, 0.2)), 0.3, 3.0),
    }


def cost_block(rows, cols):
    rows_sq = jnp.sum(jnp.square(rows.astype(jnp.float32)), axis=1)
    cols_sq = jnp.sum(jnp.square(cols.astype(jnp.float32)), axis=1)
    cross = jnp.dot(rows, cols.T, preferred_element_type=jnp.float32)
    return rows_sq[:, None] + cols_sq[None, :] - 2.0 * cross


def reference(imu, camera, imu_mass, cam_mass):
    epsilon = D / 20.0
    cams = camera.reshape(CAM_TOTAL, D)
    block = math.gcd(IMU_TOTAL, 512)
    count = IMU_TOTAL // block
    imu_blocks = imu.reshape(count, block, D)
    log_a = jnp.log(imu_mass)
    log_b = jnp.log(cam_mass)

    def row_lse(g):
        def single(x_blk):
            scores = (g[None, :] - cost_block(x_blk, cams)) / epsilon
            peak = jnp.max(scores, axis=1)
            return peak + jnp.log(jnp.sum(jnp.exp(scores - peak[:, None]), axis=1))
        return lax.map(single, imu_blocks).reshape(IMU_TOTAL)

    def col_lse(f):
        f_blocks = f.reshape(count, block)

        def advance(carry, item):
            peak, total = carry
            x_blk, f_blk = item
            scores = (f_blk[:, None] - cost_block(x_blk, cams)) / epsilon
            new_peak = jnp.maximum(peak, jnp.max(scores, axis=0))
            total = total * jnp.exp(peak - new_peak) + jnp.sum(jnp.exp(scores - new_peak[None, :]), axis=0)
            return (new_peak, total), None

        start = (jnp.full((CAM_TOTAL,), -1e30, jnp.float32), jnp.zeros((CAM_TOTAL,), jnp.float32))
        (peak, total), unused = lax.scan(advance, start, (imu_blocks, f_blocks))
        return peak + jnp.log(total)

    g = jnp.zeros((CAM_TOTAL,), jnp.float32)
    f = jnp.zeros((IMU_TOTAL,), jnp.float32)
    for step in range(ITERS):
        f = epsilon * log_a - epsilon * row_lse(g)
        g = epsilon * log_b - epsilon * col_lse(f)

    def final(carry, item):
        col_total, pulled_cam = carry
        x_blk, f_blk = item
        plan = jnp.exp((f_blk[:, None] + g[None, :] - cost_block(x_blk, cams)) / epsilon).astype(jnp.bfloat16)
        row_total = jnp.sum(plan.astype(jnp.float32), axis=1)
        pulled = jnp.dot(plan, cams, preferred_element_type=jnp.float32)
        grad_rows = 2.0 * (row_total[:, None] * x_blk.astype(jnp.float32) - pulled)
        col_total = col_total + jnp.sum(plan.astype(jnp.float32), axis=0)
        pulled_cam = pulled_cam + jnp.dot(plan.T, x_blk, preferred_element_type=jnp.float32)
        return (col_total, pulled_cam), grad_rows

    start = (jnp.zeros((CAM_TOTAL,), jnp.float32), jnp.zeros((CAM_TOTAL, D), jnp.float32))
    (col_total, pulled_cam), grad_rows = lax.scan(final, start, (imu_blocks, f.reshape(count, block)))
    grad_imu = grad_rows.reshape(IMU_TOTAL, D)
    grad_cam = 2.0 * (col_total[:, None] * cams.astype(jnp.float32) - pulled_cam)
    return grad_imu, grad_cam.reshape(CAM_BLOCKS, COL_DEV, D)
```

```python
import math

import jax
import jax.numpy as jnp
from jax import lax
from jax.sharding import PartitionSpec as P

D = 128
ITERS = 3


def cost_block(rows, rows_sq, cols, cols_sq):
    cross = jnp.dot(rows, cols.T, preferred_element_type=jnp.float32)
    return rows_sq[:, None] + cols_sq[None, :] - 2.0 * cross


def squares(values):
    return jnp.sum(jnp.square(values.astype(jnp.float32)), axis=1)


def combine(part, axis):
    parts = lax.all_gather(part, axis, axis=0)
    top = jnp.max(parts, axis=0)
    return top + jnp.log(jnp.sum(jnp.exp(parts - top[None, :]), axis=0))


def local(imu, camera, imu_mass, cam_mass):
    epsilon = D / 20.0
    imu_rows = lax.all_gather(imu, "col", axis=0, tiled=True)
    cam_rows = lax.all_gather(camera, "row", axis=1, tiled=True)[0]
    rows = imu_rows.shape[0]
    cols = cam_rows.shape[0]
    block = math.gcd(rows, 512)
    count = rows // block
    rows_sq = squares(imu_rows)
    cols_sq = squares(cam_rows)
    log_a = jnp.log(imu_mass)
    log_b = jnp.log(cam_mass)
    stored = cost_block(imu_rows, rows_sq, cam_rows, cols_sq)

    def tile(k):
        return lax.dynamic_slice_in_dim(stored, k * block, block, 0)

    blocks = jnp.arange(count, dtype=jnp.int32)

    def row_lse(g):

        def single(k):
            scores = (g[None, :] - tile(k)) / epsilon
            peak = jnp.max(scores, axis=1)
            return (peak, jnp.sum(jnp.exp(scores - peak[:, None]), axis=1))

        peak, total = lax.map(single, blocks)
        peak = peak.reshape(rows)
        total = total.reshape(rows)
        return combine(peak + jnp.log(total), "col")

    def col_lse(f):

        def advance(k, carry):
            peak, total = carry
            f_blk = lax.dynamic_slice_in_dim(f, k * block, block, 0)
            scores = (f_blk[:, None] - tile(k)) / epsilon
            new_peak = jnp.maximum(peak, jnp.max(scores, axis=0))
            total = total * jnp.exp(peak - new_peak) + jnp.sum(
                jnp.exp(scores - new_peak[None, :]), axis=0
            )
            return (new_peak, total)

        start = (jnp.full((cols,), -1e30, jnp.float32), jnp.zeros((cols,), jnp.float32))
        peak, total = lax.fori_loop(0, count, advance, start)
        return combine(peak + jnp.log(total), "row")

    g = jnp.zeros((cols,), jnp.float32)
    f = jnp.zeros((rows,), jnp.float32)
    for step in range(ITERS):
        f = epsilon * log_a - epsilon * row_lse(g)
        g = epsilon * log_b - epsilon * col_lse(f)

    def plan_rows(k):
        f_blk = lax.dynamic_slice_in_dim(f, k * block, block, 0)
        return jnp.exp((f_blk[:, None] + g[None, :] - tile(k)) / epsilon).astype(jnp.bfloat16)

    plan = lax.map(plan_rows, blocks).reshape(rows, cols)
    row_total = jnp.sum(plan, axis=1, dtype=jnp.float32)
    col_total = jnp.sum(plan, axis=0, dtype=jnp.float32)
    imu_share = rows // lax.axis_size("col")
    cam_share = cols // lax.axis_size("row")
    plan_part = plan
    own = imu_rows.astype(jnp.float32)
    weight = row_total
    pulled = jnp.dot(plan_part, cam_rows, preferred_element_type=jnp.float32)
    grad_imu = lax.psum_scatter(2.0 * (weight[:, None] * own - pulled), "col", scatter_dimension=0, tiled=True)
    plan_part = plan
    own = cam_rows.astype(jnp.float32)
    weight = col_total
    pulled = lax.dot_general(
        plan_part, imu_rows, (((0,), (0,)), ((), ())), preferred_element_type=jnp.float32
    )
    grad_cam = lax.psum_scatter(2.0 * (weight[:, None] * own - pulled), "row", scatter_dimension=0, tiled=True)
    return (grad_imu, grad_cam[None])


def solution(mesh):
    in_specs = (P(("row", "col"), None), P("col", "row", None), P("row"), P("col"))
    out_specs = (P(("row", "col"), None), P("col", "row", None))
    return jax.shard_map(local, mesh=mesh, in_specs=in_specs, out_specs=out_specs, check_vma=False)
```

```python
import jax
import jax.numpy as jnp
from jax import lax
from jax.experimental import pallas as pl
from jax.experimental.pallas import tpu as pltpu
from jax.sharding import PartitionSpec as P

D = 128
ITERS = 3
EPS = D / 20.0
INV = 1.0 / EPS
TWO_INV = 2.0 / EPS
ROW_TILE = 512
COL_TILE = 256
VMEM_LIMIT = 60 * 1024 * 1024
NT = (((1,), (1,)), ((), ()))
TN = (((0,), (0,)), ((), ()))


def _params(semantics):
    return pltpu.CompilerParams(dimension_semantics=semantics, vmem_limit_bytes=VMEM_LIMIT)


def _row_kernel(x_ref, y_ref, b_ref, a_ref, o_ref):
    cross = lax.dot_general(x_ref[...], y_ref[...], NT, preferred_element_type=jnp.float32)
    t = a_ref[...] + TWO_INV * cross
    top = jnp.max(t, axis=1, keepdims=True)
    total = jnp.sum(jnp.exp(t - top), axis=1, keepdims=True)
    o_ref[...] = top + jnp.log(total) - b_ref[...]


def row_lse(x, y, b, a):
    rows, cols = x.shape[0], y.shape[0]
    return pl.pallas_call(
        _row_kernel,
        out_shape=jax.ShapeDtypeStruct((rows, 1), jnp.float32),
        grid=(rows // ROW_TILE,),
        in_specs=[
            pl.BlockSpec((ROW_TILE, D), lambda i: (i, 0)),
            pl.BlockSpec((cols, D), lambda i: (0, 0)),
            pl.BlockSpec((ROW_TILE, 1), lambda i: (i, 0)),
            pl.BlockSpec((1, cols), lambda i: (0, 0)),
        ],
        out_specs=pl.BlockSpec((ROW_TILE, 1), lambda i: (i, 0)),
        compiler_params=_params(("arbitrary",)),
    )(x, y, b, a)


def _col_kernel(x_ref, y_ref, u_ref, b_ref, o_ref):
    cross = lax.dot_general(x_ref[...], y_ref[...], NT, preferred_element_type=jnp.float32)
    t = u_ref[...] + TWO_INV * cross
    top = jnp.max(t, axis=0, keepdims=True)
    total = jnp.sum(jnp.exp(t - top), axis=0, keepdims=True)
    o_ref[...] = top + jnp.log(total) - b_ref[...]


def col_lse(x, y, u, b):
    rows, cols = x.shape[0], y.shape[0]
    return pl.pallas_call(
        _col_kernel,
        out_shape=jax.ShapeDtypeStruct((1, cols), jnp.float32),
        grid=(cols // COL_TILE,),
        in_specs=[
            pl.BlockSpec((rows, D), lambda j: (0, 0)),
            pl.BlockSpec((COL_TILE, D), lambda j: (j, 0)),
            pl.BlockSpec((rows, 1), lambda j: (0, 0)),
            pl.BlockSpec((1, COL_TILE), lambda j: (0, j)),
        ],
        out_specs=pl.BlockSpec((1, COL_TILE), lambda j: (0, j)),
        compiler_params=_params(("arbitrary",)),
    )(x, y, u, b)


def _plan_kernel(x_ref, y_ref, u_ref, a_ref, gi_ref, pc_ref, c_ref):
    @pl.when(pl.program_id(0) == 0)
    def _():
        pc_ref[...] = jnp.zeros_like(pc_ref)
        c_ref[...] = jnp.zeros_like(c_ref)

    x = x_ref[...]
    cross = lax.dot_general(x, y_ref[...], NT, preferred_element_type=jnp.float32)
    plan = jnp.exp(u_ref[...] + a_ref[...] + TWO_INV * cross).astype(jnp.bfloat16)
    wide = plan.astype(jnp.float32)
    r = jnp.sum(wide, axis=1, keepdims=True)
    c_ref[...] += jnp.sum(wide, axis=0, keepdims=True)
    pulled = jnp.dot(plan, y_ref[...], preferred_element_type=jnp.float32)
    gi_ref[...] = 2.0 * (r * x.astype(jnp.float32) - pulled)
    pc_ref[...] += lax.dot_general(plan, x, TN, preferred_element_type=jnp.float32)


def plan_grads(x, y, u, a):
    rows, cols = x.shape[0], y.shape[0]
    return pl.pallas_call(
        _plan_kernel,
        out_shape=(
            jax.ShapeDtypeStruct((rows, D), jnp.float32),
            jax.ShapeDtypeStruct((cols, D), jnp.float32),
            jax.ShapeDtypeStruct((1, cols), jnp.float32),
        ),
        grid=(rows // ROW_TILE,),
        in_specs=[
            pl.BlockSpec((ROW_TILE, D), lambda i: (i, 0)),
            pl.BlockSpec((cols, D), lambda i: (0, 0)),
            pl.BlockSpec((ROW_TILE, 1), lambda i: (i, 0)),
            pl.BlockSpec((1, cols), lambda i: (0, 0)),
        ],
        out_specs=(
            pl.BlockSpec((ROW_TILE, D), lambda i: (i, 0)),
            pl.BlockSpec((cols, D), lambda i: (0, 0)),
            pl.BlockSpec((1, cols), lambda i: (0, 0)),
        ),
        compiler_params=_params(("arbitrary",)),
    )(x, y, u, a)


def squares(values):
    return jnp.sum(jnp.square(values.astype(jnp.float32)), axis=1)


def combine(part, axis):
    parts = lax.all_gather(part, axis, axis=0)
    top = jnp.max(parts, axis=0)
    return top + jnp.log(jnp.sum(jnp.exp(parts - top[None, :]), axis=0))


def local(imu, camera, imu_mass, cam_mass):
    imu_rows = lax.all_gather(imu, "col", axis=0, tiled=True)
    cam_rows = lax.all_gather(camera, "row", axis=1, tiled=True)[0]
    rows_sq = squares(imu_rows)
    cols_sq = squares(cam_rows)
    log_a = jnp.log(imu_mass)
    log_b = jnp.log(cam_mass)
    row_b = (rows_sq * INV)[:, None]
    col_b = (cols_sq * INV)[None, :]

    g = jnp.zeros_like(cols_sq)
    f = jnp.zeros_like(rows_sq)
    for step in range(ITERS):
        a = (g[None, :] - cols_sq[None, :]) * INV
        lse = combine(row_lse(imu_rows, cam_rows, row_b, a)[:, 0], "col")
        f = EPS * log_a - EPS * lse
        u = ((f - rows_sq) * INV)[:, None]
        lse = combine(col_lse(imu_rows, cam_rows, u, col_b)[0], "row")
        g = EPS * log_b - EPS * lse

    a = (g[None, :] - cols_sq[None, :]) * INV
    u = ((f - rows_sq) * INV)[:, None]
    grad_rows, pulled_cam, col_total = plan_grads(imu_rows, cam_rows, u, a)
    grad_cols = 2.0 * (col_total[0][:, None] * cam_rows.astype(jnp.float32) - pulled_cam)
    grad_imu = lax.psum_scatter(grad_rows, "col", scatter_dimension=0, tiled=True)
    grad_cam = lax.psum_scatter(grad_cols, "row", scatter_dimension=0, tiled=True)
    return (grad_imu, grad_cam[None])


def solution(mesh):
    in_specs = (P(("row", "col"), None), P("col", "row", None), P("row"), P("col"))
    out_specs = (P(("row", "col"), None), P("col", "row", None))
    return jax.shard_map(local, mesh=mesh, in_specs=in_specs, out_specs=out_specs, check_vma=False)
```

```python
import jax
import jax.numpy as jnp
from jax import lax
from jax.experimental import pallas as pl
from jax.experimental.pallas import tpu as pltpu
from jax.sharding import PartitionSpec as P

D = 128
ITERS = 3
EPS = D / 20.0
INV = 1.0 / EPS
TWO_INV = 2.0 / EPS
ROW_TILE = 512
COL_TILE = 256
VMEM_LIMIT = 60 * 1024 * 1024
NT = (((1,), (1,)), ((), ()))
TN = (((0,), (0,)), ((), ()))


def _params(semantics):
    return pltpu.CompilerParams(dimension_semantics=semantics, vmem_limit_bytes=VMEM_LIMIT)


def _to_row(col):
    return jnp.transpose(jnp.broadcast_to(col, (col.shape[0], D)))[0:1, :]


def _to_col(row):
    return jnp.transpose(jnp.broadcast_to(row, (D, row.shape[1])))[:, 0:1]


def _lse_kernel(p_ref, q_ref, a_ref, b_ref, o_ref):
    cross = lax.dot_general(p_ref[...], q_ref[...], NT, preferred_element_type=jnp.float32)
    t = a_ref[...] + TWO_INV * cross
    top = jnp.max(t, axis=1, keepdims=True)
    total = jnp.sum(jnp.exp(t - top), axis=1, keepdims=True)
    o_ref[...] = _to_row(top + jnp.log(total)) - b_ref[...]


def lse(p, q, a, b, tile):
    rows, cols = p.shape[0], q.shape[0]
    return pl.pallas_call(
        _lse_kernel,
        out_shape=jax.ShapeDtypeStruct((1, rows), jnp.float32),
        grid=(rows // tile,),
        in_specs=[
            pl.BlockSpec((tile, D), lambda i: (i, 0)),
            pl.BlockSpec((cols, D), lambda i: (0, 0)),
            pl.BlockSpec((1, cols), lambda i: (0, 0)),
            pl.BlockSpec((1, tile), lambda i: (0, i)),
        ],
        out_specs=pl.BlockSpec((1, tile), lambda i: (0, i)),
        compiler_params=_params(("arbitrary",)),
    )(p, q, a, b)


def _plan_kernel(x_ref, y_ref, u_ref, a_ref, gi_ref, pc_ref, c_ref):
    @pl.when(pl.program_id(0) == 0)
    def _():
        pc_ref[...] = jnp.zeros_like(pc_ref)
        c_ref[...] = jnp.zeros_like(c_ref)

    x = x_ref[...]
    cross = lax.dot_general(x, y_ref[...], NT, preferred_element_type=jnp.float32)
    plan = jnp.exp(_to_col(u_ref[...]) + a_ref[...] + TWO_INV * cross).astype(jnp.bfloat16)
    wide = plan.astype(jnp.float32)
    r = jnp.sum(wide, axis=1, keepdims=True)
    c_ref[...] += jnp.sum(wide, axis=0, keepdims=True)
    pulled = jnp.dot(plan, y_ref[...], preferred_element_type=jnp.float32)
    gi_ref[...] = 2.0 * (r * x.astype(jnp.float32) - pulled)
    pc_ref[...] += lax.dot_general(plan, x, TN, preferred_element_type=jnp.float32)


def plan_grads(x, y, u, a):
    rows, cols = x.shape[0], y.shape[0]
    return pl.pallas_call(
        _plan_kernel,
        out_shape=(
            jax.ShapeDtypeStruct((rows, D), jnp.float32),
            jax.ShapeDtypeStruct((cols, D), jnp.float32),
            jax.ShapeDtypeStruct((1, cols), jnp.float32),
        ),
        grid=(rows // ROW_TILE,),
        in_specs=[
            pl.BlockSpec((ROW_TILE, D), lambda i: (i, 0)),
            pl.BlockSpec((cols, D), lambda i: (0, 0)),
            pl.BlockSpec((1, ROW_TILE), lambda i: (0, i)),
            pl.BlockSpec((1, cols), lambda i: (0, 0)),
        ],
        out_specs=(
            pl.BlockSpec((ROW_TILE, D), lambda i: (i, 0)),
            pl.BlockSpec((cols, D), lambda i: (0, 0)),
            pl.BlockSpec((1, cols), lambda i: (0, 0)),
        ),
        compiler_params=_params(("arbitrary",)),
    )(x, y, u, a)


def squares(values):
    return jnp.sum(jnp.square(values.astype(jnp.float32)), axis=1)


def combine(part, axis):
    parts = lax.all_gather(part, axis, axis=0)
    top = jnp.max(parts, axis=0)
    return top + jnp.log(jnp.sum(jnp.exp(parts - top[None, :]), axis=0))


def local(imu, camera, imu_mass, cam_mass):
    imu_rows = lax.all_gather(imu, "col", axis=0, tiled=True)
    cam_rows = lax.all_gather(camera, "row", axis=1, tiled=True)[0]
    rows_sq = squares(imu_rows)
    cols_sq = squares(cam_rows)
    log_a = jnp.log(imu_mass)
    log_b = jnp.log(cam_mass)
    row_b = (rows_sq * INV)[None, :]
    col_b = (cols_sq * INV)[None, :]

    g = jnp.zeros_like(cols_sq)
    f = jnp.zeros_like(rows_sq)
    for step in range(ITERS):
        a = (g[None, :] - cols_sq[None, :]) * INV
        lse_f = combine(lse(imu_rows, cam_rows, a, row_b, ROW_TILE)[0], "col")
        f = EPS * log_a - EPS * lse_f
        u = ((f - rows_sq) * INV)[None, :]
        lse_g = combine(lse(cam_rows, imu_rows, u, col_b, COL_TILE)[0], "row")
        g = EPS * log_b - EPS * lse_g

    a = (g[None, :] - cols_sq[None, :]) * INV
    u = ((f - rows_sq) * INV)[None, :]
    grad_rows, pulled_cam, col_total = plan_grads(imu_rows, cam_rows, u, a)
    grad_cols = 2.0 * (col_total[0][:, None] * cam_rows.astype(jnp.float32) - pulled_cam)
    grad_imu = lax.psum_scatter(grad_rows, "col", scatter_dimension=0, tiled=True)
    grad_cam = lax.psum_scatter(grad_cols, "row", scatter_dimension=0, tiled=True)
    return (grad_imu, grad_cam[None])


def solution(mesh):
    in_specs = (P(("row", "col"), None), P("col", "row", None), P("row"), P("col"))
    out_specs = (P(("row", "col"), None), P("col", "row", None))
    return jax.shard_map(local, mesh=mesh, in_specs=in_specs, out_specs=out_specs, check_vma=False)
```

```python
import functools

import jax
import jax.numpy as jnp
from jax import lax
from jax.experimental import pallas as pl
from jax.experimental.pallas import tpu as pltpu
from jax.sharding import PartitionSpec as P

D = 128
ITERS = 3
EPS = D / 20.0
INV = 1.0 / EPS
TWO_INV = 2.0 / EPS
ROW_TILE = 512
COL_TILE = 256
VMEM_LIMIT = 60 * 1024 * 1024
NT = (((1,), (1,)), ((), ()))
TN = (((0,), (0,)), ((), ()))


def _params(semantics):
    return pltpu.CompilerParams(dimension_semantics=semantics, vmem_limit_bytes=VMEM_LIMIT)


def _to_row(col):
    return jnp.transpose(jnp.broadcast_to(col, (col.shape[0], D)))[0:1, :]


def _to_col(row):
    return jnp.transpose(jnp.broadcast_to(row, (D, row.shape[1])))[:, 0:1]


def _lse_kernel(p_ref, q_ref, a_ref, b_ref, o_ref):
    cross = lax.dot_general(p_ref[...], q_ref[...], NT, preferred_element_type=jnp.float32)
    t = a_ref[...] + TWO_INV * cross
    top = jnp.max(t, axis=1, keepdims=True)
    total = jnp.sum(jnp.exp(t - top), axis=1, keepdims=True)
    o_ref[...] = _to_row(top + jnp.log(total)) - b_ref[...]


def lse(p, q, a, b, tile):
    rows, cols = p.shape[0], q.shape[0]
    return pl.pallas_call(
        _lse_kernel,
        out_shape=jax.ShapeDtypeStruct((1, rows), jnp.float32),
        grid=(rows // tile,),
        in_specs=[
            pl.BlockSpec((tile, D), lambda i: (i, 0)),
            pl.BlockSpec((cols, D), lambda i: (0, 0)),
            pl.BlockSpec((1, cols), lambda i: (0, 0)),
            pl.BlockSpec((1, tile), lambda i: (0, i)),
        ],
        out_specs=pl.BlockSpec((1, tile), lambda i: (0, i)),
        compiler_params=_params(("arbitrary",)),
    )(p, q, a, b)


def _plan_kernel(x_ref, y_ref, u_ref, a_ref, gi_ref, pc_ref, c_ref):
    @pl.when(pl.program_id(0) == 0)
    def _():
        pc_ref[...] = jnp.zeros_like(pc_ref)
        c_ref[...] = jnp.zeros_like(c_ref)

    x = x_ref[...]
    cross = lax.dot_general(x, y_ref[...], NT, preferred_element_type=jnp.float32)
    plan = jnp.exp(_to_col(u_ref[...]) + a_ref[...] + TWO_INV * cross).astype(jnp.bfloat16)
    wide = plan.astype(jnp.float32)
    r = jnp.sum(wide, axis=1, keepdims=True)
    c_ref[...] += jnp.sum(wide, axis=0, keepdims=True)
    pulled = jnp.dot(plan, y_ref[...], preferred_element_type=jnp.float32)
    gi_ref[...] = 2.0 * (r * x.astype(jnp.float32) - pulled)
    pc_ref[...] += lax.dot_general(plan, x, TN, preferred_element_type=jnp.float32)


def plan_grads(x, y, u, a):
    rows, cols = x.shape[0], y.shape[0]
    return pl.pallas_call(
        _plan_kernel,
        out_shape=(
            jax.ShapeDtypeStruct((rows, D), jnp.float32),
            jax.ShapeDtypeStruct((cols, D), jnp.float32),
            jax.ShapeDtypeStruct((1, cols), jnp.float32),
        ),
        grid=(rows // ROW_TILE,),
        in_specs=[
            pl.BlockSpec((ROW_TILE, D), lambda i: (i, 0)),
            pl.BlockSpec((cols, D), lambda i: (0, 0)),
            pl.BlockSpec((1, ROW_TILE), lambda i: (0, i)),
            pl.BlockSpec((1, cols), lambda i: (0, 0)),
        ],
        out_specs=(
            pl.BlockSpec((ROW_TILE, D), lambda i: (i, 0)),
            pl.BlockSpec((cols, D), lambda i: (0, 0)),
            pl.BlockSpec((1, cols), lambda i: (0, 0)),
        ),
        compiler_params=_params(("arbitrary",)),
    )(x, y, u, a)


def squares(values):
    return jnp.sum(jnp.square(values.astype(jnp.float32)), axis=1)


def _peer(axis, k):
    if axis == "col":
        return (lax.axis_index("row"), k)
    return (k, lax.axis_index("col"))


def _gather_lse_kernel(axis, n, x_ref, o_ref, buf, send, recv):
    me = lax.axis_index(axis)
    barrier = pltpu.get_barrier_semaphore()
    for d in range(1, n):
        pl.semaphore_signal(barrier, inc=1, device_id=_peer(axis, lax.rem(me + d, n)),
                            device_id_type=pl.DeviceIdType.MESH)
    pl.semaphore_wait(barrier, n - 1)
    copies = []
    for d in range(1, n):
        copy = pltpu.make_async_remote_copy(
            src_ref=x_ref, dst_ref=buf.at[me], send_sem=send.at[d], recv_sem=recv.at[me],
            device_id=_peer(axis, lax.rem(me + d, n)), device_id_type=pl.DeviceIdType.MESH)
        copy.start()
        copies.append(copy)
    for copy in copies:
        copy.wait_send()
    for d in range(1, n):
        src = lax.rem(me + n - d, n)
        pltpu.make_async_remote_copy(
            src_ref=x_ref, dst_ref=buf.at[src], send_sem=send.at[d], recv_sem=recv.at[src],
            device_id=_peer(axis, src), device_id_type=pl.DeviceIdType.MESH).wait_recv()
    buf[me] = x_ref[...]
    parts = buf[...]
    top = jnp.max(parts, axis=0)
    o_ref[...] = top + jnp.log(jnp.sum(jnp.exp(parts - top[None]), axis=0))


def combine(part, axis):
    n = lax.axis_size(axis)
    block = part.reshape(8, part.shape[0] // 8)
    out = pl.pallas_call(
        functools.partial(_gather_lse_kernel, axis, n),
        out_shape=jax.ShapeDtypeStruct(block.shape, jnp.float32),
        in_specs=[pl.BlockSpec(memory_space=pltpu.VMEM)],
        out_specs=pl.BlockSpec(memory_space=pltpu.VMEM),
        scratch_shapes=[
            pltpu.VMEM((n,) + block.shape, jnp.float32),
            pltpu.SemaphoreType.DMA((n,)),
            pltpu.SemaphoreType.DMA((n,)),
        ],
        compiler_params=pltpu.CompilerParams(
            collective_id=0 if axis == "col" else 1, has_side_effects=True),
    )(block)
    return out.reshape(part.shape)


def local(imu, camera, imu_mass, cam_mass):
    imu_rows = lax.all_gather(imu, "col", axis=0, tiled=True)
    cam_rows = lax.all_gather(camera, "row", axis=1, tiled=True)[0]
    rows_sq = squares(imu_rows)
    cols_sq = squares(cam_rows)
    log_a = jnp.log(imu_mass)
    log_b = jnp.log(cam_mass)
    row_b = (rows_sq * INV)[None, :]
    col_b = (cols_sq * INV)[None, :]

    g = jnp.zeros_like(cols_sq)
    f = jnp.zeros_like(rows_sq)
    for step in range(ITERS):
        a = (g[None, :] - cols_sq[None, :]) * INV
        lse_f = combine(lse(imu_rows, cam_rows, a, row_b, ROW_TILE)[0], "col")
        f = EPS * log_a - EPS * lse_f
        u = ((f - rows_sq) * INV)[None, :]
        lse_g = combine(lse(cam_rows, imu_rows, u, col_b, COL_TILE)[0], "row")
        g = EPS * log_b - EPS * lse_g

    a = (g[None, :] - cols_sq[None, :]) * INV
    u = ((f - rows_sq) * INV)[None, :]
    grad_rows, pulled_cam, col_total = plan_grads(imu_rows, cam_rows, u, a)
    grad_cols = 2.0 * (col_total[0][:, None] * cam_rows.astype(jnp.float32) - pulled_cam)
    grad_imu = lax.psum_scatter(grad_rows, "col", scatter_dimension=0, tiled=True)
    grad_cam = lax.psum_scatter(grad_cols, "row", scatter_dimension=0, tiled=True)
    return (grad_imu, grad_cam[None])


def solution(mesh):
    in_specs = (P(("row", "col"), None), P("col", "row", None), P("row"), P("col"))
    out_specs = (P(("row", "col"), None), P("col", "row", None))
    return jax.shard_map(local, mesh=mesh, in_specs=in_specs, out_specs=out_specs, check_vma=False)
```

```python
import functools

import jax
import jax.numpy as jnp
from jax import lax
from jax.experimental import pallas as pl
from jax.experimental.pallas import tpu as pltpu
from jax.sharding import PartitionSpec as P

D = 128
ITERS = 3
EPS = D / 20.0
INV = 1.0 / EPS
TWO_INV = 2.0 / EPS
ROW_TILE = 512
COL_TILE = 256
VMEM_LIMIT = 60 * 1024 * 1024
NT = (((1,), (1,)), ((), ()))
TN = (((0,), (0,)), ((), ()))


def _params(semantics):
    return pltpu.CompilerParams(dimension_semantics=semantics, vmem_limit_bytes=VMEM_LIMIT)


def _to_row(col):
    return jnp.transpose(jnp.broadcast_to(col, (col.shape[0], D)))[0:1, :]


def _to_col(row):
    return jnp.transpose(jnp.broadcast_to(row, (D, row.shape[1])))[:, 0:1]


def _lse_kernel(p_ref, q_ref, a_ref, b_ref, o_ref):
    cross = lax.dot_general(p_ref[...], q_ref[...], NT, preferred_element_type=jnp.float32)
    t = a_ref[...] + TWO_INV * cross
    top = jnp.max(t, axis=1, keepdims=True)
    total = jnp.sum(jnp.exp(t - top), axis=1, keepdims=True)
    o_ref[...] = _to_row(top + jnp.log(total)) - b_ref[...]


def lse(p, q, a, b, tile):
    rows, cols = p.shape[0], q.shape[0]
    return pl.pallas_call(
        _lse_kernel,
        out_shape=jax.ShapeDtypeStruct((1, rows), jnp.float32),
        grid=(rows // tile,),
        in_specs=[
            pl.BlockSpec((tile, D), lambda i: (i, 0)),
            pl.BlockSpec((cols, D), lambda i: (0, 0)),
            pl.BlockSpec((1, cols), lambda i: (0, 0)),
            pl.BlockSpec((1, tile), lambda i: (0, i)),
        ],
        out_specs=pl.BlockSpec((1, tile), lambda i: (0, i)),
        compiler_params=_params(("arbitrary",)),
    )(p, q, a, b)


def _plan_kernel(x_ref, y_ref, u_ref, a_ref, gi_ref, pc_ref, c_ref):
    @pl.when(pl.program_id(0) == 0)
    def _():
        pc_ref[...] = jnp.zeros_like(pc_ref)
        c_ref[...] = jnp.zeros_like(c_ref)

    x = x_ref[...]
    cross = lax.dot_general(x, y_ref[...], NT, preferred_element_type=jnp.float32)
    plan = jnp.exp(_to_col(u_ref[...]) + a_ref[...] + TWO_INV * cross).astype(jnp.bfloat16)
    wide = plan.astype(jnp.float32)
    r = jnp.sum(wide, axis=1, keepdims=True)
    c_ref[...] += jnp.sum(wide, axis=0, keepdims=True)
    pulled = jnp.dot(plan, y_ref[...], preferred_element_type=jnp.float32)
    gi_ref[...] = 2.0 * (r * x.astype(jnp.float32) - pulled)
    pc_ref[...] += lax.dot_general(plan, x, TN, preferred_element_type=jnp.float32)


def plan_grads(x, y, u, a):
    rows, cols = x.shape[0], y.shape[0]
    return pl.pallas_call(
        _plan_kernel,
        out_shape=(
            jax.ShapeDtypeStruct((rows, D), jnp.float32),
            jax.ShapeDtypeStruct((cols, D), jnp.float32),
            jax.ShapeDtypeStruct((1, cols), jnp.float32),
        ),
        grid=(rows // ROW_TILE,),
        in_specs=[
            pl.BlockSpec((ROW_TILE, D), lambda i: (i, 0)),
            pl.BlockSpec((cols, D), lambda i: (0, 0)),
            pl.BlockSpec((1, ROW_TILE), lambda i: (0, i)),
            pl.BlockSpec((1, cols), lambda i: (0, 0)),
        ],
        out_specs=(
            pl.BlockSpec((ROW_TILE, D), lambda i: (i, 0)),
            pl.BlockSpec((cols, D), lambda i: (0, 0)),
            pl.BlockSpec((1, cols), lambda i: (0, 0)),
        ),
        compiler_params=_params(("arbitrary",)),
    )(x, y, u, a)


def squares(values):
    return jnp.sum(jnp.square(values.astype(jnp.float32)), axis=1)


def _peer(axis, k):
    if axis == "col":
        return (lax.axis_index("row"), k)
    return (k, lax.axis_index("col"))


def _gather_lse_kernel(axis, n, x_ref, o_ref, buf, send, recv):
    me = lax.axis_index(axis)
    barrier = pltpu.get_barrier_semaphore()
    for d in range(1, n):
        pl.semaphore_signal(barrier, inc=1, device_id=_peer(axis, lax.rem(me + d, n)),
                            device_id_type=pl.DeviceIdType.MESH)
    pl.semaphore_wait(barrier, n - 1)
    copies = []
    for d in range(1, n):
        copy = pltpu.make_async_remote_copy(
            src_ref=x_ref, dst_ref=buf.at[me], send_sem=send.at[d], recv_sem=recv.at[me],
            device_id=_peer(axis, lax.rem(me + d, n)), device_id_type=pl.DeviceIdType.MESH)
        copy.start()
        copies.append(copy)
    for copy in copies:
        copy.wait_send()
    for d in range(1, n):
        src = lax.rem(me + n - d, n)
        pltpu.make_async_remote_copy(
            src_ref=x_ref, dst_ref=buf.at[src], send_sem=send.at[d], recv_sem=recv.at[src],
            device_id=_peer(axis, src), device_id_type=pl.DeviceIdType.MESH).wait_recv()
    buf[me] = x_ref[...]
    parts = buf[...]
    top = jnp.max(parts, axis=0)
    o_ref[...] = top + jnp.log(jnp.sum(jnp.exp(parts - top[None]), axis=0))


def _exchange_kernel(jobs, *refs):
    count = len(jobs)
    ins, outs = refs[:count], refs[count:2 * count]
    bufs, sends, recvs = refs[2 * count::3], refs[2 * count + 1::3], refs[2 * count + 2::3]
    barrier = pltpu.get_barrier_semaphore()
    for axis, n, kind in jobs:
        me = lax.axis_index(axis)
        for d in range(1, n):
            pl.semaphore_signal(barrier, inc=1, device_id=_peer(axis, lax.rem(me + d, n)),
                                device_id_type=pl.DeviceIdType.MESH)
    pl.semaphore_wait(barrier, sum(n - 1 for _, n, _ in jobs))

    def copy(job, d, peer, slot):
        axis, n, kind = jobs[job]
        src = ins[job] if kind == "gather" else ins[job].at[peer]
        return pltpu.make_async_remote_copy(
            src_ref=src, dst_ref=bufs[job].at[slot], send_sem=sends[job].at[d],
            recv_sem=recvs[job].at[slot], device_id=_peer(axis, peer),
            device_id_type=pl.DeviceIdType.MESH)

    started = []
    for job, (axis, n, kind) in enumerate(jobs):
        me = lax.axis_index(axis)
        for d in range(1, n):
            started.append(copy(job, d, lax.rem(me + d, n), me))
            started[-1].start()
    for c in started:
        c.wait_send()
    for job, (axis, n, kind) in enumerate(jobs):
        me = lax.axis_index(axis)
        for d in range(1, n):
            src = lax.rem(me + n - d, n)
            copy(job, d, src, src).wait_recv()
        if kind == "gather":
            bufs[job][me] = ins[job][...]
            outs[job][...] = bufs[job][...]
        else:
            bufs[job][me] = ins[job][me]
            outs[job][...] = jnp.sum(bufs[job][...], axis=0)


def exchange(jobs, arrays, collective_id):
    shapes, scratch = [], []
    for (axis, n, kind), x in zip(jobs, arrays):
        block = x.shape if kind == "gather" else x.shape[1:]
        shapes.append(jax.ShapeDtypeStruct((n,) + block if kind == "gather" else block, x.dtype))
        scratch += [pltpu.VMEM((n,) + block, x.dtype), pltpu.SemaphoreType.DMA((n,)),
                    pltpu.SemaphoreType.DMA((n,))]
    return pl.pallas_call(
        functools.partial(_exchange_kernel, tuple(jobs)),
        out_shape=tuple(shapes),
        in_specs=[pl.BlockSpec(memory_space=pltpu.VMEM)] * len(jobs),
        out_specs=tuple(pl.BlockSpec(memory_space=pltpu.VMEM) for _ in jobs),
        scratch_shapes=scratch,
        compiler_params=pltpu.CompilerParams(
            collective_id=collective_id, has_side_effects=True, vmem_limit_bytes=VMEM_LIMIT),
    )(*arrays)


def combine(part, axis):
    n = lax.axis_size(axis)
    block = part.reshape(8, part.shape[0] // 8)
    out = pl.pallas_call(
        functools.partial(_gather_lse_kernel, axis, n),
        out_shape=jax.ShapeDtypeStruct(block.shape, jnp.float32),
        in_specs=[pl.BlockSpec(memory_space=pltpu.VMEM)],
        out_specs=pl.BlockSpec(memory_space=pltpu.VMEM),
        scratch_shapes=[
            pltpu.VMEM((n,) + block.shape, jnp.float32),
            pltpu.SemaphoreType.DMA((n,)),
            pltpu.SemaphoreType.DMA((n,)),
        ],
        compiler_params=pltpu.CompilerParams(
            collective_id=0 if axis == "col" else 1, has_side_effects=True),
    )(block)
    return out.reshape(part.shape)


def local(imu, camera, imu_mass, cam_mass):
    imu_rows = lax.all_gather(imu, "col", axis=0, tiled=True)
    cam_rows = lax.all_gather(camera, "row", axis=1, tiled=True)[0]
    rows_sq = squares(imu_rows)
    cols_sq = squares(cam_rows)
    log_a = jnp.log(imu_mass)
    log_b = jnp.log(cam_mass)
    row_b = (rows_sq * INV)[None, :]
    col_b = (cols_sq * INV)[None, :]

    g = jnp.zeros_like(cols_sq)
    f = jnp.zeros_like(rows_sq)
    for step in range(ITERS):
        a = (g[None, :] - cols_sq[None, :]) * INV
        lse_f = combine(lse(imu_rows, cam_rows, a, row_b, ROW_TILE)[0], "col")
        f = EPS * log_a - EPS * lse_f
        u = ((f - rows_sq) * INV)[None, :]
        lse_g = combine(lse(cam_rows, imu_rows, u, col_b, COL_TILE)[0], "row")
        g = EPS * log_b - EPS * lse_g

    a = (g[None, :] - cols_sq[None, :]) * INV
    u = ((f - rows_sq) * INV)[None, :]
    grad_rows, pulled_cam, col_total = plan_grads(imu_rows, cam_rows, u, a)
    grad_cols = 2.0 * (col_total[0][:, None] * cam_rows.astype(jnp.float32) - pulled_cam)
    n_col, n_row = lax.axis_size("col"), lax.axis_size("row")
    grad_imu, grad_cam = exchange(
        [("col", n_col, "scatter"), ("row", n_row, "scatter")],
        [grad_rows.reshape(n_col, -1, D), grad_cols.reshape(n_row, -1, D)], 2)
    return (grad_imu, grad_cam[None])


def solution(mesh):
    in_specs = (P(("row", "col"), None), P("col", "row", None), P("row"), P("col"))
    out_specs = (P(("row", "col"), None), P("col", "row", None))
    return jax.shard_map(local, mesh=mesh, in_specs=in_specs, out_specs=out_specs, check_vma=False)
```

```python
import functools

import jax
import jax.numpy as jnp
from jax import lax
from jax.experimental import pallas as pl
from jax.experimental.pallas import tpu as pltpu
from jax.sharding import PartitionSpec as P

D = 128
ITERS = 3
EPS = D / 20.0
INV = 1.0 / EPS
TWO_INV = 2.0 / EPS
ROW_TILE = 512
COL_TILE = 256
VMEM_LIMIT = 60 * 1024 * 1024
NT = (((1,), (1,)), ((), ()))
TN = (((0,), (0,)), ((), ()))


def _params(semantics):
    return pltpu.CompilerParams(dimension_semantics=semantics, vmem_limit_bytes=VMEM_LIMIT)


def _to_row(col):
    return jnp.transpose(jnp.broadcast_to(col, (col.shape[0], D)))[0:1, :]


def _to_col(row):
    return jnp.transpose(jnp.broadcast_to(row, (D, row.shape[1])))[:, 0:1]


def _lse_kernel(p_ref, q_ref, a_ref, b_ref, o_ref):
    cross = lax.dot_general(p_ref[...], q_ref[...], NT, preferred_element_type=jnp.float32)
    t = a_ref[...] + TWO_INV * cross
    top = jnp.max(t, axis=1, keepdims=True)
    total = jnp.sum(jnp.exp(t - top), axis=1, keepdims=True)
    o_ref[...] = _to_row(top + jnp.log(total)) - b_ref[...]


def lse(p, q, a, b, tile):
    rows, cols = p.shape[0], q.shape[0]
    return pl.pallas_call(
        _lse_kernel,
        out_shape=jax.ShapeDtypeStruct((1, rows), jnp.float32),
        grid=(rows // tile,),
        in_specs=[
            pl.BlockSpec((tile, D), lambda i: (i, 0)),
            pl.BlockSpec((cols, D), lambda i: (0, 0)),
            pl.BlockSpec((1, cols), lambda i: (0, 0)),
            pl.BlockSpec((1, tile), lambda i: (0, i)),
        ],
        out_specs=pl.BlockSpec((1, tile), lambda i: (0, i)),
        compiler_params=_params(("arbitrary",)),
    )(p, q, a, b)


def _plan_kernel(x_ref, y_ref, u_ref, a_ref, gi_ref, pc_ref, c_ref):
    @pl.when(pl.program_id(0) == 0)
    def _():
        pc_ref[...] = jnp.zeros_like(pc_ref)
        c_ref[...] = jnp.zeros_like(c_ref)

    x = x_ref[...]
    cross = lax.dot_general(x, y_ref[...], NT, preferred_element_type=jnp.float32)
    plan = jnp.exp(_to_col(u_ref[...]) + a_ref[...] + TWO_INV * cross).astype(jnp.bfloat16)
    wide = plan.astype(jnp.float32)
    r = jnp.sum(wide, axis=1, keepdims=True)
    c_ref[...] += jnp.sum(wide, axis=0, keepdims=True)
    pulled = jnp.dot(plan, y_ref[...], preferred_element_type=jnp.float32)
    gi_ref[...] = 2.0 * (r * x.astype(jnp.float32) - pulled)
    pc_ref[...] += lax.dot_general(plan, x, TN, preferred_element_type=jnp.float32)


def plan_grads(x, y, u, a):
    rows, cols = x.shape[0], y.shape[0]
    return pl.pallas_call(
        _plan_kernel,
        out_shape=(
            jax.ShapeDtypeStruct((rows, D), jnp.float32),
            jax.ShapeDtypeStruct((cols, D), jnp.float32),
            jax.ShapeDtypeStruct((1, cols), jnp.float32),
        ),
        grid=(rows // ROW_TILE,),
        in_specs=[
            pl.BlockSpec((ROW_TILE, D), lambda i: (i, 0)),
            pl.BlockSpec((cols, D), lambda i: (0, 0)),
            pl.BlockSpec((1, ROW_TILE), lambda i: (0, i)),
            pl.BlockSpec((1, cols), lambda i: (0, 0)),
        ],
        out_specs=(
            pl.BlockSpec((ROW_TILE, D), lambda i: (i, 0)),
            pl.BlockSpec((cols, D), lambda i: (0, 0)),
            pl.BlockSpec((1, cols), lambda i: (0, 0)),
        ),
        compiler_params=_params(("arbitrary",)),
    )(x, y, u, a)


def squares(values):
    return jnp.sum(jnp.square(values.astype(jnp.float32)), axis=1)


def _peer(axis, k):
    if axis == "col":
        return (lax.axis_index("row"), k)
    return (k, lax.axis_index("col"))


def _gather_lse_kernel(axis, n, x_ref, o_ref, buf, send, recv):
    me = lax.axis_index(axis)
    barrier = pltpu.get_barrier_semaphore()
    for d in range(1, n):
        pl.semaphore_signal(barrier, inc=1, device_id=_peer(axis, lax.rem(me + d, n)),
                            device_id_type=pl.DeviceIdType.MESH)
    pl.semaphore_wait(barrier, n - 1)
    copies = []
    for d in range(1, n):
        copy = pltpu.make_async_remote_copy(
            src_ref=x_ref, dst_ref=buf.at[me], send_sem=send.at[d], recv_sem=recv.at[me],
            device_id=_peer(axis, lax.rem(me + d, n)), device_id_type=pl.DeviceIdType.MESH)
        copy.start()
        copies.append(copy)
    for copy in copies:
        copy.wait_send()
    for d in range(1, n):
        src = lax.rem(me + n - d, n)
        pltpu.make_async_remote_copy(
            src_ref=x_ref, dst_ref=buf.at[src], send_sem=send.at[d], recv_sem=recv.at[src],
            device_id=_peer(axis, src), device_id_type=pl.DeviceIdType.MESH).wait_recv()
    buf[me] = x_ref[...]
    parts = buf[...]
    top = jnp.max(parts, axis=0)
    o_ref[...] = top + jnp.log(jnp.sum(jnp.exp(parts - top[None]), axis=0))


def _exchange_kernel(jobs, *refs):
    count = len(jobs)
    ins, outs = refs[:count], refs[count:2 * count]
    bufs, sends, recvs = refs[2 * count::3], refs[2 * count + 1::3], refs[2 * count + 2::3]
    barrier = pltpu.get_barrier_semaphore()
    for axis, n, kind in jobs:
        me = lax.axis_index(axis)
        for d in range(1, n):
            pl.semaphore_signal(barrier, inc=1, device_id=_peer(axis, lax.rem(me + d, n)),
                                device_id_type=pl.DeviceIdType.MESH)
    pl.semaphore_wait(barrier, sum(n - 1 for _, n, _ in jobs))

    def copy(job, d, peer, slot):
        axis, n, kind = jobs[job]
        src = ins[job] if kind == "gather" else ins[job].at[peer]
        return pltpu.make_async_remote_copy(
            src_ref=src, dst_ref=bufs[job].at[slot], send_sem=sends[job].at[d],
            recv_sem=recvs[job].at[slot], device_id=_peer(axis, peer),
            device_id_type=pl.DeviceIdType.MESH)

    started = []
    for job, (axis, n, kind) in enumerate(jobs):
        me = lax.axis_index(axis)
        for d in range(1, n):
            started.append(copy(job, d, lax.rem(me + d, n), me))
            started[-1].start()
    for c in started:
        c.wait_send()
    for job, (axis, n, kind) in enumerate(jobs):
        me = lax.axis_index(axis)
        for d in range(1, n):
            src = lax.rem(me + n - d, n)
            copy(job, d, src, src).wait_recv()
        if kind == "gather":
            bufs[job][me] = ins[job][...]
            outs[job][...] = bufs[job][...]
        else:
            bufs[job][me] = ins[job][me]
            outs[job][...] = jnp.sum(bufs[job][...], axis=0)


def exchange(jobs, arrays, collective_id):
    shapes, scratch = [], []
    for (axis, n, kind), x in zip(jobs, arrays):
        block = x.shape if kind == "gather" else x.shape[1:]
        shapes.append(jax.ShapeDtypeStruct((n,) + block if kind == "gather" else block, x.dtype))
        scratch += [pltpu.VMEM((n,) + block, x.dtype), pltpu.SemaphoreType.DMA((n,)),
                    pltpu.SemaphoreType.DMA((n,))]
    return pl.pallas_call(
        functools.partial(_exchange_kernel, tuple(jobs)),
        out_shape=tuple(shapes),
        in_specs=[pl.BlockSpec(memory_space=pltpu.VMEM)] * len(jobs),
        out_specs=tuple(pl.BlockSpec(memory_space=pltpu.VMEM) for _ in jobs),
        scratch_shapes=scratch,
        compiler_params=pltpu.CompilerParams(
            collective_id=collective_id, has_side_effects=True, vmem_limit_bytes=VMEM_LIMIT),
    )(*arrays)


def combine(part, axis):
    n = lax.axis_size(axis)
    block = part.reshape(8, part.shape[0] // 8)
    out = pl.pallas_call(
        functools.partial(_gather_lse_kernel, axis, n),
        out_shape=jax.ShapeDtypeStruct(block.shape, jnp.float32),
        in_specs=[pl.BlockSpec(memory_space=pltpu.VMEM)],
        out_specs=pl.BlockSpec(memory_space=pltpu.VMEM),
        scratch_shapes=[
            pltpu.VMEM((n,) + block.shape, jnp.float32),
            pltpu.SemaphoreType.DMA((n,)),
            pltpu.SemaphoreType.DMA((n,)),
        ],
        compiler_params=pltpu.CompilerParams(
            collective_id=0 if axis == "col" else 1, has_side_effects=True),
    )(block)
    return out.reshape(part.shape)


def local(imu, camera, imu_mass, cam_mass):
    n_col, n_row = lax.axis_size("col"), lax.axis_size("row")
    imu_rows, cam_rows = exchange(
        [("col", n_col, "gather"), ("row", n_row, "gather")], [imu, camera[0]], 3)
    imu_rows = imu_rows.reshape(-1, D)
    cam_rows = cam_rows.reshape(-1, D)
    rows_sq = squares(imu_rows)
    cols_sq = squares(cam_rows)
    log_a = jnp.log(imu_mass)
    log_b = jnp.log(cam_mass)
    row_b = (rows_sq * INV)[None, :]
    col_b = (cols_sq * INV)[None, :]

    g = jnp.zeros_like(cols_sq)
    f = jnp.zeros_like(rows_sq)
    for step in range(ITERS):
        a = (g[None, :] - cols_sq[None, :]) * INV
        lse_f = combine(lse(imu_rows, cam_rows, a, row_b, ROW_TILE)[0], "col")
        f = EPS * log_a - EPS * lse_f
        u = ((f - rows_sq) * INV)[None, :]
        lse_g = combine(lse(cam_rows, imu_rows, u, col_b, COL_TILE)[0], "row")
        g = EPS * log_b - EPS * lse_g

    a = (g[None, :] - cols_sq[None, :]) * INV
    u = ((f - rows_sq) * INV)[None, :]
    grad_rows, pulled_cam, col_total = plan_grads(imu_rows, cam_rows, u, a)
    grad_cols = 2.0 * (col_total[0][:, None] * cam_rows.astype(jnp.float32) - pulled_cam)
    grad_imu, grad_cam = exchange(
        [("col", n_col, "scatter"), ("row", n_row, "scatter")],
        [grad_rows.reshape(n_col, -1, D), grad_cols.reshape(n_row, -1, D)], 2)
    return (grad_imu, grad_cam[None])


def solution(mesh):
    in_specs = (P(("row", "col"), None), P("col", "row", None), P("row"), P("col"))
    out_specs = (P(("row", "col"), None), P("col", "row", None))
    return jax.shard_map(local, mesh=mesh, in_specs=in_specs, out_specs=out_specs, check_vma=False)
```

```python
import functools

import jax
import jax.numpy as jnp
from jax import lax
from jax.experimental import pallas as pl
from jax.experimental.pallas import tpu as pltpu
from jax.sharding import PartitionSpec as P

D = 128
ITERS = 3
EPS = D / 20.0
INV = 1.0 / EPS
TWO_INV = 2.0 / EPS
VMEM_LIMIT = 60 * 1024 * 1024
LOG2E = 1.4426950408889634
LN2 = 0.6931471805599453
SCALE2 = TWO_INV * LOG2E
NT = (((1,), (1,)), ((), ()))
TN = (((0,), (0,)), ((), ()))


def _params(semantics):
    return pltpu.CompilerParams(dimension_semantics=semantics, vmem_limit_bytes=VMEM_LIMIT)


def _to_row(col):
    return jnp.transpose(jnp.broadcast_to(col, (col.shape[0], D)))[0:1, :]


def _to_col(row):
    return jnp.transpose(jnp.broadcast_to(row, (D, row.shape[1])))[:, 0:1]


def _row_of(v):
    return jnp.concatenate([v[k:k + 1, :] for k in range(v.shape[0])], axis=1)


def _lse_kernel(p_ref, q_ref, a_ref, b_ref, o_ref):
    i = pl.program_id(0)
    cross = lax.dot_general(p_ref[...], q_ref[...], NT, preferred_element_type=jnp.float32)
    t = _row_of(a_ref[...]) * LOG2E + SCALE2 * cross
    top = jnp.max(t, axis=1, keepdims=True)
    total = jnp.sum(jnp.exp2(t - top), axis=1, keepdims=True)
    o_ref[pl.ds(i, 1), :] = _to_row(top * LN2 + jnp.log(total)) - b_ref[pl.ds(i, 1), :]


def lse(p, q, a, b):
    rows, cols = p.shape[0], q.shape[0]
    tile = rows // 8
    return pl.pallas_call(
        _lse_kernel,
        out_shape=jax.ShapeDtypeStruct((8, tile), jnp.float32),
        grid=(8,),
        in_specs=[
            pl.BlockSpec((tile, D), lambda i: (i, 0)),
            pl.BlockSpec((cols, D), lambda i: (0, 0)),
            pl.BlockSpec((8, cols // 8), lambda i: (0, 0)),
            pl.BlockSpec((8, tile), lambda i: (0, 0)),
        ],
        out_specs=pl.BlockSpec((8, tile), lambda i: (0, 0)),
        compiler_params=_params(("arbitrary",)),
    )(p, q, a, b)


def _plan_kernel(x_ref, y_ref, u_ref, a_ref, gi_ref, pc_ref, c_ref):
    @pl.when(pl.program_id(0) == 0)
    def _():
        pc_ref[...] = jnp.zeros_like(pc_ref)
        c_ref[...] = jnp.zeros_like(c_ref)

    i = pl.program_id(0)
    x = x_ref[...]
    cross = lax.dot_general(x, y_ref[...], NT, preferred_element_type=jnp.float32)
    u = _to_col(u_ref[pl.ds(i, 1), :] * LOG2E)
    plan = jnp.exp2(u + _row_of(a_ref[...]) * LOG2E + SCALE2 * cross).astype(jnp.bfloat16)
    wide = plan.astype(jnp.float32)
    r = jnp.sum(wide, axis=1, keepdims=True)
    c_ref[...] += jnp.sum(wide, axis=0, keepdims=True)
    pulled = jnp.dot(plan, y_ref[...], preferred_element_type=jnp.float32)
    gi_ref[...] = 2.0 * (r * x.astype(jnp.float32) - pulled)
    pc_ref[...] += lax.dot_general(plan, x, TN, preferred_element_type=jnp.float32)


def plan_grads(x, y, u, a):
    rows, cols = x.shape[0], y.shape[0]
    return pl.pallas_call(
        _plan_kernel,
        out_shape=(
            jax.ShapeDtypeStruct((rows, D), jnp.float32),
            jax.ShapeDtypeStruct((cols, D), jnp.float32),
            jax.ShapeDtypeStruct((1, cols), jnp.float32),
        ),
        grid=(8,),
        in_specs=[
            pl.BlockSpec((rows // 8, D), lambda i: (i, 0)),
            pl.BlockSpec((cols, D), lambda i: (0, 0)),
            pl.BlockSpec((8, rows // 8), lambda i: (0, 0)),
            pl.BlockSpec((8, cols // 8), lambda i: (0, 0)),
        ],
        out_specs=(
            pl.BlockSpec((rows // 8, D), lambda i: (i, 0)),
            pl.BlockSpec((cols, D), lambda i: (0, 0)),
            pl.BlockSpec((1, cols), lambda i: (0, 0)),
        ),
        compiler_params=_params(("arbitrary",)),
    )(x, y, u, a)


def squares(values):
    return jnp.sum(jnp.square(values.astype(jnp.float32)), axis=1)


def _peer(axis, k):
    if axis == "col":
        return (lax.axis_index("row"), k)
    return (k, lax.axis_index("col"))


def _gather_lse_kernel(axis, n, x_ref, m_ref, q_ref, o_ref, buf, send, recv):
    me = lax.axis_index(axis)
    barrier = pltpu.get_barrier_semaphore()
    for d in range(1, n):
        pl.semaphore_signal(barrier, inc=1, device_id=_peer(axis, lax.rem(me + d, n)),
                            device_id_type=pl.DeviceIdType.MESH)
    pl.semaphore_wait(barrier, n - 1)
    copies = []
    for d in range(1, n):
        copy = pltpu.make_async_remote_copy(
            src_ref=x_ref, dst_ref=buf.at[me], send_sem=send.at[d], recv_sem=recv.at[me],
            device_id=_peer(axis, lax.rem(me + d, n)), device_id_type=pl.DeviceIdType.MESH)
        copy.start()
        copies.append(copy)
    for copy in copies:
        copy.wait_send()
    for d in range(1, n):
        src = lax.rem(me + n - d, n)
        pltpu.make_async_remote_copy(
            src_ref=x_ref, dst_ref=buf.at[src], send_sem=send.at[d], recv_sem=recv.at[src],
            device_id=_peer(axis, src), device_id_type=pl.DeviceIdType.MESH).wait_recv()
    buf[me] = x_ref[...]
    parts = buf[...]
    top = jnp.max(parts, axis=0)
    total = top + jnp.log(jnp.sum(jnp.exp(parts - top[None]), axis=0))
    o_ref[...] = (EPS * (m_ref[...] - total) - q_ref[...]) * INV


def _exchange_kernel(jobs, *refs):
    count = len(jobs)
    ins, outs = refs[:count], refs[count:2 * count]
    bufs, sends, recvs = refs[2 * count::3], refs[2 * count + 1::3], refs[2 * count + 2::3]
    barrier = pltpu.get_barrier_semaphore()
    for axis, n, kind in jobs:
        me = lax.axis_index(axis)
        for d in range(1, n):
            pl.semaphore_signal(barrier, inc=1, device_id=_peer(axis, lax.rem(me + d, n)),
                                device_id_type=pl.DeviceIdType.MESH)
    pl.semaphore_wait(barrier, sum(n - 1 for _, n, _ in jobs))

    def copy(job, d, peer, slot):
        axis, n, kind = jobs[job]
        src = ins[job] if kind == "gather" else ins[job].at[peer]
        return pltpu.make_async_remote_copy(
            src_ref=src, dst_ref=bufs[job].at[slot], send_sem=sends[job].at[d],
            recv_sem=recvs[job].at[slot], device_id=_peer(axis, peer),
            device_id_type=pl.DeviceIdType.MESH)

    started = []
    for job, (axis, n, kind) in enumerate(jobs):
        me = lax.axis_index(axis)
        for d in range(1, n):
            started.append(copy(job, d, lax.rem(me + d, n), me))
            started[-1].start()
    for c in started:
        c.wait_send()
    for job, (axis, n, kind) in enumerate(jobs):
        me = lax.axis_index(axis)
        for d in range(1, n):
            src = lax.rem(me + n - d, n)
            copy(job, d, src, src).wait_recv()
        if kind == "gather":
            bufs[job][me] = ins[job][...]
            outs[job][...] = bufs[job][...]
        else:
            bufs[job][me] = ins[job][me]
            outs[job][...] = jnp.sum(bufs[job][...], axis=0)


def exchange(jobs, arrays, collective_id):
    shapes, scratch = [], []
    for (axis, n, kind), x in zip(jobs, arrays):
        block = x.shape if kind == "gather" else x.shape[1:]
        shapes.append(jax.ShapeDtypeStruct((n,) + block if kind == "gather" else block, x.dtype))
        scratch += [pltpu.VMEM((n,) + block, x.dtype), pltpu.SemaphoreType.DMA((n,)),
                    pltpu.SemaphoreType.DMA((n,))]
    return pl.pallas_call(
        functools.partial(_exchange_kernel, tuple(jobs)),
        out_shape=tuple(shapes),
        in_specs=[pl.BlockSpec(memory_space=pltpu.VMEM)] * len(jobs),
        out_specs=tuple(pl.BlockSpec(memory_space=pltpu.VMEM) for _ in jobs),
        scratch_shapes=scratch,
        compiler_params=pltpu.CompilerParams(
            collective_id=collective_id, has_side_effects=True, vmem_limit_bytes=VMEM_LIMIT),
    )(*arrays)


def combine(block, axis, log_mass, sq):
    n = lax.axis_size(axis)
    return pl.pallas_call(
        functools.partial(_gather_lse_kernel, axis, n),
        out_shape=jax.ShapeDtypeStruct(block.shape, jnp.float32),
        in_specs=[pl.BlockSpec(memory_space=pltpu.VMEM)] * 3,
        out_specs=pl.BlockSpec(memory_space=pltpu.VMEM),
        scratch_shapes=[
            pltpu.VMEM((n,) + block.shape, jnp.float32),
            pltpu.SemaphoreType.DMA((n,)),
            pltpu.SemaphoreType.DMA((n,)),
        ],
        compiler_params=pltpu.CompilerParams(
            collective_id=0 if axis == "col" else 1, has_side_effects=True),
    )(block, log_mass, sq)


def local(imu, camera, imu_mass, cam_mass):
    n_col, n_row = lax.axis_size("col"), lax.axis_size("row")
    imu_rows, cam_rows = exchange(
        [("col", n_col, "gather"), ("row", n_row, "gather")], [imu, camera[0]], 3)
    imu_rows = imu_rows.reshape(-1, D)
    cam_rows = cam_rows.reshape(-1, D)
    rows_sq = squares(imu_rows).reshape(8, -1)
    cols_sq = squares(cam_rows).reshape(8, -1)
    log_a = jnp.log(imu_mass).reshape(8, -1)
    log_b = jnp.log(cam_mass).reshape(8, -1)
    row_b = rows_sq * INV
    col_b = cols_sq * INV

    a = -col_b
    for step in range(ITERS):
        u = combine(lse(imu_rows, cam_rows, a, row_b), "col", log_a, rows_sq)
        a = combine(lse(cam_rows, imu_rows, u, col_b), "row", log_b, cols_sq)

    grad_rows, pulled_cam, col_total = plan_grads(imu_rows, cam_rows, u, a)
    grad_cols = 2.0 * (col_total[0][:, None] * cam_rows.astype(jnp.float32) - pulled_cam)
    grad_imu, grad_cam = exchange(
        [("col", n_col, "scatter"), ("row", n_row, "scatter")],
        [grad_rows.reshape(n_col, -1, D), grad_cols.reshape(n_row, -1, D)], 2)
    return (grad_imu, grad_cam[None])


def solution(mesh):
    in_specs = (P(("row", "col"), None), P("col", "row", None), P("row"), P("col"))
    out_specs = (P(("row", "col"), None), P("col", "row", None))
    return jax.shard_map(local, mesh=mesh, in_specs=in_specs, out_specs=out_specs, check_vma=False)
```

```python
import functools

import jax
import jax.numpy as jnp
from jax import lax
from jax.experimental import pallas as pl
from jax.experimental.pallas import tpu as pltpu
from jax.sharding import PartitionSpec as P

D = 128
ITERS = 3
EPS = D / 20.0
INV = 1.0 / EPS
TWO_INV = 2.0 / EPS
VMEM_LIMIT = 60 * 1024 * 1024
LOG2E = 1.4426950408889634
LN2 = 0.6931471805599453
SCALE2 = TWO_INV * LOG2E
NT = (((1,), (1,)), ((), ()))
TN = (((0,), (0,)), ((), ()))


def _params(semantics):
    return pltpu.CompilerParams(dimension_semantics=semantics, vmem_limit_bytes=VMEM_LIMIT)


def _to_row(col):
    return jnp.transpose(jnp.broadcast_to(col, (col.shape[0], D)))[0:1, :]


def _to_col(row):
    return jnp.transpose(jnp.broadcast_to(row, (D, row.shape[1])))[:, 0:1]


def _row_of(v):
    return jnp.concatenate([v[k:k + 1, :] for k in range(v.shape[0])], axis=1)


def _lse_kernel(p_ref, q_ref, a_ref, b_ref, o_ref):
    i = pl.program_id(0)
    cross = lax.dot_general(p_ref[...], q_ref[...], NT, preferred_element_type=jnp.float32)
    t = _row_of(a_ref[...]) * LOG2E + SCALE2 * cross
    top = jnp.max(t, axis=1, keepdims=True)
    total = jnp.sum(jnp.exp2(t - top), axis=1, keepdims=True)
    o_ref[pl.ds(i, 1), :] = _to_row(top * LN2 + jnp.log(total)) - b_ref[pl.ds(i, 1), :]


def lse(p, q, a, b):
    rows, cols = p.shape[0], q.shape[0]
    tile = rows // 8
    return pl.pallas_call(
        _lse_kernel,
        out_shape=jax.ShapeDtypeStruct((8, tile), jnp.float32),
        grid=(8,),
        in_specs=[
            pl.BlockSpec((tile, D), lambda i: (i, 0)),
            pl.BlockSpec((cols, D), lambda i: (0, 0)),
            pl.BlockSpec((8, cols // 8), lambda i: (0, 0)),
            pl.BlockSpec((8, tile), lambda i: (0, 0)),
        ],
        out_specs=pl.BlockSpec((8, tile), lambda i: (0, 0)),
        compiler_params=_params(("arbitrary",)),
    )(p, q, a, b)


def _plan_kernel(x_ref, y_ref, u_ref, a_ref, gi_ref, pc_ref, c_ref):
    @pl.when(pl.program_id(0) == 0)
    def _():
        pc_ref[...] = jnp.zeros_like(pc_ref)
        c_ref[...] = jnp.zeros_like(c_ref)

    i = pl.program_id(0)
    x = x_ref[...]
    cross = lax.dot_general(x, y_ref[...], NT, preferred_element_type=jnp.float32)
    u = _to_col(u_ref[pl.ds(i, 1), :] * LOG2E)
    plan = jnp.exp2(u + _row_of(a_ref[...]) * LOG2E + SCALE2 * cross).astype(jnp.bfloat16)
    wide = plan.astype(jnp.float32)
    r = jnp.sum(wide, axis=1, keepdims=True)
    c_ref[...] += jnp.sum(wide, axis=0, keepdims=True)
    pulled = jnp.dot(plan, y_ref[...], preferred_element_type=jnp.float32)
    gi_ref[...] = 2.0 * (r * x.astype(jnp.float32) - pulled)
    pc_ref[...] += lax.dot_general(plan, x, TN, preferred_element_type=jnp.float32)


def plan_grads(x, y, u, a):
    rows, cols = x.shape[0], y.shape[0]
    return pl.pallas_call(
        _plan_kernel,
        out_shape=(
            jax.ShapeDtypeStruct((rows, D), jnp.float32),
            jax.ShapeDtypeStruct((cols, D), jnp.float32),
            jax.ShapeDtypeStruct((1, cols), jnp.float32),
        ),
        grid=(8,),
        in_specs=[
            pl.BlockSpec((rows // 8, D), lambda i: (i, 0)),
            pl.BlockSpec((cols, D), lambda i: (0, 0)),
            pl.BlockSpec((8, rows // 8), lambda i: (0, 0)),
            pl.BlockSpec((8, cols // 8), lambda i: (0, 0)),
        ],
        out_specs=(
            pl.BlockSpec((rows // 8, D), lambda i: (i, 0)),
            pl.BlockSpec((cols, D), lambda i: (0, 0)),
            pl.BlockSpec((1, cols), lambda i: (0, 0)),
        ),
        compiler_params=_params(("arbitrary",)),
    )(x, y, u, a)


def _plan_scatter_kernel(n_col, n_row, x_ref, y_ref, u_ref, a_ref, gi_out, gc_out,
                         gi, pc, csum, gcs, bufi, bufc, sendi, recvi, sendc, recvc):
    me_c, me_r = lax.axis_index("col"), lax.axis_index("row")
    barrier = pltpu.get_barrier_semaphore()
    for d in range(1, n_col):
        pl.semaphore_signal(barrier, inc=1, device_id=_peer("col", lax.rem(me_c + d, n_col)),
                            device_id_type=pl.DeviceIdType.MESH)
    for d in range(1, n_row):
        pl.semaphore_signal(barrier, inc=1, device_id=_peer("row", lax.rem(me_r + d, n_row)),
                            device_id_type=pl.DeviceIdType.MESH)
    pl.semaphore_wait(barrier, n_col + n_row - 2)

    def to_col_dev(k, slot):
        return pltpu.make_async_remote_copy(
            src_ref=gi.at[k], dst_ref=bufi.at[slot], send_sem=sendi.at[k], recv_sem=recvi.at[slot],
            device_id=_peer("col", k), device_id_type=pl.DeviceIdType.MESH)

    def to_row_dev(k, slot):
        return pltpu.make_async_remote_copy(
            src_ref=gcs.at[k], dst_ref=bufc.at[slot], send_sem=sendc.at[k], recv_sem=recvc.at[slot],
            device_id=_peer("row", k), device_id_type=pl.DeviceIdType.MESH)

    def each(n, me, body):
        for k in range(n):
            pl.when(me != k)(functools.partial(body, k))

    rows, cols = x_ref.shape[0], y_ref.shape[0]
    tiles = u_ref.shape[0]
    tile, m, mc = rows // tiles, rows // n_col, cols // n_row
    per = tile // m
    y = y_ref[...]
    a2 = _row_of(a_ref[...]) * LOG2E
    pc[...] = jnp.zeros_like(pc)
    csum[...] = jnp.zeros_like(csum)
    for i in range(tiles):
        x = x_ref[i * tile:(i + 1) * tile, :]
        cross = lax.dot_general(x, y, NT, preferred_element_type=jnp.float32)
        u = _to_col(u_ref[i:i + 1, :] * LOG2E)
        plan = jnp.exp2(u + a2 + SCALE2 * cross).astype(jnp.bfloat16)
        wide = plan.astype(jnp.float32)
        r = jnp.sum(wide, axis=1, keepdims=True)
        csum[...] += jnp.sum(wide, axis=0, keepdims=True)
        pulled = jnp.dot(plan, y, preferred_element_type=jnp.float32)
        g = 2.0 * (r * x.astype(jnp.float32) - pulled)
        for s in range(per):
            gi[i * per + s] = g[s * m:(s + 1) * m]
        pc[...] += lax.dot_general(plan, x, TN, preferred_element_type=jnp.float32)
        if i >= 1:
            for s in range((i - 1) * per, i * per):
                pl.when(me_c != s)(functools.partial(lambda k: to_col_dev(k, me_c).start(), s))
    for s in range((tiles - 1) * per, tiles * per):
        pl.when(me_c != s)(functools.partial(lambda k: to_col_dev(k, me_c).start(), s))
    gcv = 2.0 * (_to_col(csum[...]) * y.astype(jnp.float32) - pc[...])
    for k in range(n_row):
        gcs[k] = gcv[k * mc:(k + 1) * mc]
    each(n_row, me_r, lambda k: to_row_dev(k, me_r).start())
    each(n_col, me_c, lambda k: to_col_dev(k, me_c).wait_send())
    each(n_row, me_r, lambda k: to_row_dev(k, me_r).wait_send())
    each(n_col, me_c, lambda k: to_col_dev(k, k).wait_recv())
    each(n_row, me_r, lambda k: to_row_dev(k, k).wait_recv())
    bufi[me_c] = gi[me_c]
    bufc[me_r] = gcs[me_r]
    gi_out[...] = jnp.sum(bufi[...], axis=0)
    gc_out[...] = jnp.sum(bufc[...], axis=0)


def plan_scatter(x, y, u, a, n_col, n_row):
    rows, cols = x.shape[0], y.shape[0]
    m, mc = rows // n_col, cols // n_row
    return pl.pallas_call(
        functools.partial(_plan_scatter_kernel, n_col, n_row),
        out_shape=(jax.ShapeDtypeStruct((m, D), jnp.float32),
                   jax.ShapeDtypeStruct((mc, D), jnp.float32)),
        in_specs=[pl.BlockSpec(memory_space=pltpu.VMEM)] * 4,
        out_specs=(pl.BlockSpec(memory_space=pltpu.VMEM),) * 2,
        scratch_shapes=[
            pltpu.VMEM((n_col, m, D), jnp.float32),
            pltpu.VMEM((cols, D), jnp.float32),
            pltpu.VMEM((1, cols), jnp.float32),
            pltpu.VMEM((n_row, mc, D), jnp.float32),
            pltpu.VMEM((n_col, m, D), jnp.float32),
            pltpu.VMEM((n_row, mc, D), jnp.float32),
            pltpu.SemaphoreType.DMA((n_col,)),
            pltpu.SemaphoreType.DMA((n_col,)),
            pltpu.SemaphoreType.DMA((n_row,)),
            pltpu.SemaphoreType.DMA((n_row,)),
        ],
        compiler_params=pltpu.CompilerParams(
            collective_id=4, has_side_effects=True, vmem_limit_bytes=VMEM_LIMIT),
    )(x, y, u, a)


def squares(values):
    return jnp.sum(jnp.square(values.astype(jnp.float32)), axis=1)


def _peer(axis, k):
    if axis == "col":
        return (lax.axis_index("row"), k)
    return (k, lax.axis_index("col"))


def _gather_lse_kernel(axis, n, x_ref, m_ref, q_ref, o_ref, buf, send, recv):
    me = lax.axis_index(axis)
    barrier = pltpu.get_barrier_semaphore()
    for d in range(1, n):
        pl.semaphore_signal(barrier, inc=1, device_id=_peer(axis, lax.rem(me + d, n)),
                            device_id_type=pl.DeviceIdType.MESH)
    pl.semaphore_wait(barrier, n - 1)
    copies = []
    for d in range(1, n):
        copy = pltpu.make_async_remote_copy(
            src_ref=x_ref, dst_ref=buf.at[me], send_sem=send.at[d], recv_sem=recv.at[me],
            device_id=_peer(axis, lax.rem(me + d, n)), device_id_type=pl.DeviceIdType.MESH)
        copy.start()
        copies.append(copy)
    for copy in copies:
        copy.wait_send()
    for d in range(1, n):
        src = lax.rem(me + n - d, n)
        pltpu.make_async_remote_copy(
            src_ref=x_ref, dst_ref=buf.at[src], send_sem=send.at[d], recv_sem=recv.at[src],
            device_id=_peer(axis, src), device_id_type=pl.DeviceIdType.MESH).wait_recv()
    buf[me] = x_ref[...]
    parts = buf[...]
    top = jnp.max(parts, axis=0)
    total = top + jnp.log(jnp.sum(jnp.exp(parts - top[None]), axis=0))
    o_ref[...] = (EPS * (m_ref[...] - total) - q_ref[...]) * INV


def _exchange_kernel(jobs, *refs):
    count = len(jobs)
    ins, outs = refs[:count], refs[count:2 * count]
    bufs, sends, recvs = refs[2 * count::3], refs[2 * count + 1::3], refs[2 * count + 2::3]
    barrier = pltpu.get_barrier_semaphore()
    for axis, n, kind in jobs:
        me = lax.axis_index(axis)
        for d in range(1, n):
            pl.semaphore_signal(barrier, inc=1, device_id=_peer(axis, lax.rem(me + d, n)),
                                device_id_type=pl.DeviceIdType.MESH)
    pl.semaphore_wait(barrier, sum(n - 1 for _, n, _ in jobs))

    def copy(job, d, peer, slot):
        axis, n, kind = jobs[job]
        src = ins[job] if kind == "gather" else ins[job].at[peer]
        return pltpu.make_async_remote_copy(
            src_ref=src, dst_ref=bufs[job].at[slot], send_sem=sends[job].at[d],
            recv_sem=recvs[job].at[slot], device_id=_peer(axis, peer),
            device_id_type=pl.DeviceIdType.MESH)

    started = []
    for job, (axis, n, kind) in enumerate(jobs):
        me = lax.axis_index(axis)
        for d in range(1, n):
            started.append(copy(job, d, lax.rem(me + d, n), me))
            started[-1].start()
    for c in started:
        c.wait_send()
    for job, (axis, n, kind) in enumerate(jobs):
        me = lax.axis_index(axis)
        for d in range(1, n):
            src = lax.rem(me + n - d, n)
            copy(job, d, src, src).wait_recv()
        if kind == "gather":
            bufs[job][me] = ins[job][...]
            outs[job][...] = bufs[job][...]
        else:
            bufs[job][me] = ins[job][me]
            outs[job][...] = jnp.sum(bufs[job][...], axis=0)


def exchange(jobs, arrays, collective_id):
    shapes, scratch = [], []
    for (axis, n, kind), x in zip(jobs, arrays):
        block = x.shape if kind == "gather" else x.shape[1:]
        shapes.append(jax.ShapeDtypeStruct((n,) + block if kind == "gather" else block, x.dtype))
        scratch += [pltpu.VMEM((n,) + block, x.dtype), pltpu.SemaphoreType.DMA((n,)),
                    pltpu.SemaphoreType.DMA((n,))]
    return pl.pallas_call(
        functools.partial(_exchange_kernel, tuple(jobs)),
        out_shape=tuple(shapes),
        in_specs=[pl.BlockSpec(memory_space=pltpu.VMEM)] * len(jobs),
        out_specs=tuple(pl.BlockSpec(memory_space=pltpu.VMEM) for _ in jobs),
        scratch_shapes=scratch,
        compiler_params=pltpu.CompilerParams(
            collective_id=collective_id, has_side_effects=True, vmem_limit_bytes=VMEM_LIMIT),
    )(*arrays)


def combine(block, axis, log_mass, sq):
    n = lax.axis_size(axis)
    return pl.pallas_call(
        functools.partial(_gather_lse_kernel, axis, n),
        out_shape=jax.ShapeDtypeStruct(block.shape, jnp.float32),
        in_specs=[pl.BlockSpec(memory_space=pltpu.VMEM)] * 3,
        out_specs=pl.BlockSpec(memory_space=pltpu.VMEM),
        scratch_shapes=[
            pltpu.VMEM((n,) + block.shape, jnp.float32),
            pltpu.SemaphoreType.DMA((n,)),
            pltpu.SemaphoreType.DMA((n,)),
        ],
        compiler_params=pltpu.CompilerParams(
            collective_id=0 if axis == "col" else 1, has_side_effects=True),
    )(block, log_mass, sq)


def local(imu, camera, imu_mass, cam_mass):
    n_col, n_row = lax.axis_size("col"), lax.axis_size("row")
    imu_rows, cam_rows = exchange(
        [("col", n_col, "gather"), ("row", n_row, "gather")], [imu, camera[0]], 3)
    imu_rows = imu_rows.reshape(-1, D)
    cam_rows = cam_rows.reshape(-1, D)
    rows_sq = squares(imu_rows).reshape(8, -1)
    cols_sq = squares(cam_rows).reshape(8, -1)
    log_a = jnp.log(imu_mass).reshape(8, -1)
    log_b = jnp.log(cam_mass).reshape(8, -1)
    row_b = rows_sq * INV
    col_b = cols_sq * INV

    a = -col_b
    for step in range(ITERS):
        u = combine(lse(imu_rows, cam_rows, a, row_b), "col", log_a, rows_sq)
        a = combine(lse(cam_rows, imu_rows, u, col_b), "row", log_b, cols_sq)

    grad_imu, grad_cam = plan_scatter(imu_rows, cam_rows, u, a, n_col, n_row)
    return (grad_imu, grad_cam[None])


def solution(mesh):
    in_specs = (P(("row", "col"), None), P("col", "row", None), P("row"), P("col"))
    out_specs = (P(("row", "col"), None), P("col", "row", None))
    return jax.shard_map(local, mesh=mesh, in_specs=in_specs, out_specs=out_specs, check_vma=False)
```

```python
import functools

import jax
import jax.numpy as jnp
from jax import lax
from jax.experimental import pallas as pl
from jax.experimental.pallas import tpu as pltpu
from jax.sharding import PartitionSpec as P

D = 128
ITERS = 3
EPS = D / 20.0
INV = 1.0 / EPS
TWO_INV = 2.0 / EPS
VMEM_LIMIT = 60 * 1024 * 1024
LOG2E = 1.4426950408889634
LN2 = 0.6931471805599453
SCALE2 = TWO_INV * LOG2E
NT = (((1,), (1,)), ((), ()))
TN = (((0,), (0,)), ((), ()))


def _params(semantics):
    return pltpu.CompilerParams(dimension_semantics=semantics, vmem_limit_bytes=VMEM_LIMIT)


def _to_row(col):
    return jnp.transpose(jnp.broadcast_to(col, (col.shape[0], D)))[0:1, :]


def _to_col(row):
    return jnp.transpose(jnp.broadcast_to(row, (D, row.shape[1])))[:, 0:1]


def _row_of(v):
    return jnp.concatenate([v[k:k + 1, :] for k in range(v.shape[0])], axis=1)


def _lse_kernel(p_ref, q_ref, a_ref, b_ref, o_ref):
    i = pl.program_id(0)
    cross = lax.dot_general(p_ref[...], q_ref[...], NT, preferred_element_type=jnp.float32)
    t = _row_of(a_ref[...]) * LOG2E + SCALE2 * cross
    top = jnp.max(t, axis=1, keepdims=True)
    total = jnp.sum(jnp.exp2(t - top), axis=1, keepdims=True)
    o_ref[pl.ds(i, 1), :] = _to_row(top * LN2 + jnp.log(total)) - b_ref[pl.ds(i, 1), :]


def lse(p, q, a, b):
    rows, cols = p.shape[0], q.shape[0]
    tile = rows // 8
    return pl.pallas_call(
        _lse_kernel,
        out_shape=jax.ShapeDtypeStruct((8, tile), jnp.float32),
        grid=(8,),
        in_specs=[
            pl.BlockSpec((tile, D), lambda i: (i, 0)),
            pl.BlockSpec((cols, D), lambda i: (0, 0)),
            pl.BlockSpec((8, cols // 8), lambda i: (0, 0)),
            pl.BlockSpec((8, tile), lambda i: (0, 0)),
        ],
        out_specs=pl.BlockSpec((8, tile), lambda i: (0, 0)),
        compiler_params=_params(("arbitrary",)),
    )(p, q, a, b)


def _plan_kernel(x_ref, y_ref, u_ref, a_ref, gi_ref, pc_ref, c_ref):
    @pl.when(pl.program_id(0) == 0)
    def _():
        pc_ref[...] = jnp.zeros_like(pc_ref)
        c_ref[...] = jnp.zeros_like(c_ref)

    i = pl.program_id(0)
    x = x_ref[...]
    cross = lax.dot_general(x, y_ref[...], NT, preferred_element_type=jnp.float32)
    u = _to_col(u_ref[pl.ds(i, 1), :] * LOG2E)
    plan = jnp.exp2(u + _row_of(a_ref[...]) * LOG2E + SCALE2 * cross).astype(jnp.bfloat16)
    wide = plan.astype(jnp.float32)
    r = jnp.sum(wide, axis=1, keepdims=True)
    c_ref[...] += jnp.sum(wide, axis=0, keepdims=True)
    pulled = jnp.dot(plan, y_ref[...], preferred_element_type=jnp.float32)
    gi_ref[...] = 2.0 * (r * x.astype(jnp.float32) - pulled)
    pc_ref[...] += lax.dot_general(plan, x, TN, preferred_element_type=jnp.float32)


def plan_grads(x, y, u, a):
    rows, cols = x.shape[0], y.shape[0]
    return pl.pallas_call(
        _plan_kernel,
        out_shape=(
            jax.ShapeDtypeStruct((rows, D), jnp.float32),
            jax.ShapeDtypeStruct((cols, D), jnp.float32),
            jax.ShapeDtypeStruct((1, cols), jnp.float32),
        ),
        grid=(8,),
        in_specs=[
            pl.BlockSpec((rows // 8, D), lambda i: (i, 0)),
            pl.BlockSpec((cols, D), lambda i: (0, 0)),
            pl.BlockSpec((8, rows // 8), lambda i: (0, 0)),
            pl.BlockSpec((8, cols // 8), lambda i: (0, 0)),
        ],
        out_specs=(
            pl.BlockSpec((rows // 8, D), lambda i: (i, 0)),
            pl.BlockSpec((cols, D), lambda i: (0, 0)),
            pl.BlockSpec((1, cols), lambda i: (0, 0)),
        ),
        compiler_params=_params(("arbitrary",)),
    )(x, y, u, a)


def _plan_scatter_kernel(n_col, n_row, x_ref, y_ref, u_ref, a_ref, gi_out, gc_out,
                         gi, pc, csum, gcs, bufi, bufc, sendi, recvi, sendc, recvc):
    me_c, me_r = lax.axis_index("col"), lax.axis_index("row")
    barrier = pltpu.get_barrier_semaphore()
    for d in range(1, n_col):
        pl.semaphore_signal(barrier, inc=1, device_id=_peer("col", lax.rem(me_c + d, n_col)),
                            device_id_type=pl.DeviceIdType.MESH)
    for d in range(1, n_row):
        pl.semaphore_signal(barrier, inc=1, device_id=_peer("row", lax.rem(me_r + d, n_row)),
                            device_id_type=pl.DeviceIdType.MESH)
    pl.semaphore_wait(barrier, n_col + n_row - 2)

    def to_col_dev(k, slot):
        return pltpu.make_async_remote_copy(
            src_ref=gi.at[k], dst_ref=bufi.at[slot], send_sem=sendi.at[k], recv_sem=recvi.at[slot],
            device_id=_peer("col", k), device_id_type=pl.DeviceIdType.MESH)

    def to_row_dev(k, slot):
        return pltpu.make_async_remote_copy(
            src_ref=gcs.at[k], dst_ref=bufc.at[slot], send_sem=sendc.at[k], recv_sem=recvc.at[slot],
            device_id=_peer("row", k), device_id_type=pl.DeviceIdType.MESH)

    def each(n, me, body):
        for k in range(n):
            pl.when(me != k)(functools.partial(body, k))

    rows, cols = x_ref.shape[0], y_ref.shape[0]
    tiles = u_ref.shape[0]
    tile, m, mc = rows // tiles, rows // n_col, cols // n_row
    per = tile // m
    y = y_ref[...]
    a2 = _row_of(a_ref[...]) * LOG2E
    pc[...] = jnp.zeros_like(pc)
    csum[...] = jnp.zeros_like(csum)
    for i in range(tiles):
        x = x_ref[i * tile:(i + 1) * tile, :]
        cross = lax.dot_general(x, y, NT, preferred_element_type=jnp.float32)
        u = _to_col(u_ref[i:i + 1, :] * LOG2E)
        plan = jnp.exp2(u + a2 + SCALE2 * cross).astype(jnp.bfloat16)
        wide = plan.astype(jnp.float32)
        r = jnp.sum(wide, axis=1, keepdims=True)
        csum[...] += jnp.sum(wide, axis=0, keepdims=True)
        pulled = jnp.dot(plan, y, preferred_element_type=jnp.float32)
        g = 2.0 * (r * x.astype(jnp.float32) - pulled)
        for s in range(per):
            gi[i * per + s] = g[s * m:(s + 1) * m]
        pc[...] += lax.dot_general(plan, x, TN, preferred_element_type=jnp.float32)
        if i >= 1:
            for s in range((i - 1) * per, i * per):
                pl.when(me_c != s)(functools.partial(lambda k: to_col_dev(k, me_c).start(), s))
    for s in range((tiles - 1) * per, tiles * per):
        pl.when(me_c != s)(functools.partial(lambda k: to_col_dev(k, me_c).start(), s))
    gcv = 2.0 * (_to_col(csum[...]) * y.astype(jnp.float32) - pc[...])
    for k in range(n_row):
        gcs[k] = gcv[k * mc:(k + 1) * mc]
    each(n_row, me_r, lambda k: to_row_dev(k, me_r).start())
    each(n_col, me_c, lambda k: to_col_dev(k, me_c).wait_send())
    each(n_row, me_r, lambda k: to_row_dev(k, me_r).wait_send())
    each(n_col, me_c, lambda k: to_col_dev(k, k).wait_recv())
    each(n_row, me_r, lambda k: to_row_dev(k, k).wait_recv())
    bufi[me_c] = gi[me_c]
    bufc[me_r] = gcs[me_r]
    gi_out[...] = jnp.sum(bufi[...], axis=0)
    gc_out[...] = jnp.sum(bufc[...], axis=0)


def plan_scatter(x, y, u, a, n_col, n_row):
    rows, cols = x.shape[0], y.shape[0]
    m, mc = rows // n_col, cols // n_row
    return pl.pallas_call(
        functools.partial(_plan_scatter_kernel, n_col, n_row),
        out_shape=(jax.ShapeDtypeStruct((m, D), jnp.float32),
                   jax.ShapeDtypeStruct((mc, D), jnp.float32)),
        in_specs=[pl.BlockSpec(memory_space=pltpu.VMEM)] * 4,
        out_specs=(pl.BlockSpec(memory_space=pltpu.VMEM),) * 2,
        scratch_shapes=[
            pltpu.VMEM((n_col, m, D), jnp.float32),
            pltpu.VMEM((cols, D), jnp.float32),
            pltpu.VMEM((1, cols), jnp.float32),
            pltpu.VMEM((n_row, mc, D), jnp.float32),
            pltpu.VMEM((n_col, m, D), jnp.float32),
            pltpu.VMEM((n_row, mc, D), jnp.float32),
            pltpu.SemaphoreType.DMA((n_col,)),
            pltpu.SemaphoreType.DMA((n_col,)),
            pltpu.SemaphoreType.DMA((n_row,)),
            pltpu.SemaphoreType.DMA((n_row,)),
        ],
        compiler_params=pltpu.CompilerParams(
            collective_id=4, has_side_effects=True, vmem_limit_bytes=VMEM_LIMIT),
    )(x, y, u, a)


def _lse_combine_kernel(axis, n, p_ref, q_ref, a_ref, b_ref, m_ref, s_ref, o_ref,
                        part, buf, send, recv):
    me = lax.axis_index(axis)
    barrier = pltpu.get_barrier_semaphore()
    for d in range(1, n):
        pl.semaphore_signal(barrier, inc=1, device_id=_peer(axis, lax.rem(me + d, n)),
                            device_id_type=pl.DeviceIdType.MESH)
    pl.semaphore_wait(barrier, n - 1)

    def out_copy(c, d):
        return pltpu.make_async_remote_copy(
            src_ref=part.at[c], dst_ref=buf.at[me, c], send_sem=send.at[c, d],
            recv_sem=recv.at[c, me], device_id=_peer(axis, lax.rem(me + d, n)),
            device_id_type=pl.DeviceIdType.MESH)

    def in_copy(c, d):
        src = lax.rem(me + n - d, n)
        return pltpu.make_async_remote_copy(
            src_ref=part.at[c], dst_ref=buf.at[src, c], send_sem=send.at[c, d],
            recv_sem=recv.at[c, src], device_id=_peer(axis, src),
            device_id_type=pl.DeviceIdType.MESH)

    def send_half(c):
        for d in range(1, n):
            out_copy(c, d).start()

    half = part.shape[1]
    tile = p_ref.shape[0] // (2 * half)
    q = q_ref[...]
    a2 = _row_of(a_ref[...]) * LOG2E

    def body(i, carry):
        start = pl.multiple_of(i * tile, tile)
        cross = lax.dot_general(p_ref[pl.ds(start, tile), :], q, NT,
                                preferred_element_type=jnp.float32)
        t = a2 + SCALE2 * cross
        top = jnp.max(t, axis=1, keepdims=True)
        total = jnp.sum(jnp.exp2(t - top), axis=1, keepdims=True)
        row = _to_row(top * LN2 + jnp.log(total)) - b_ref[pl.ds(i, 1), :]
        part.at[i // half][pl.ds(i % half, 1), :] = row

        @pl.when(i == half)
        def _():
            send_half(0)

        return carry

    lax.fori_loop(0, 2 * half, body, 0)

    def finish(c):
        for d in range(1, n):
            out_copy(c, d).wait_send()
        for d in range(1, n):
            in_copy(c, d).wait_recv()
        buf[me, c] = part[c]
        parts = buf[:, c]
        top = jnp.max(parts, axis=0)
        total = top + jnp.log(jnp.sum(jnp.exp(parts - top[None]), axis=0))
        rows = slice(c * half, (c + 1) * half)
        o_ref[rows, :] = (EPS * (m_ref[rows, :] - total) - s_ref[rows, :]) * INV

    finish(0)
    send_half(1)
    finish(1)


def lse_combine(p, q, a, b, log_mass, sq, axis):
    n = lax.axis_size(axis)
    m = p.shape[0] // 8
    return pl.pallas_call(
        functools.partial(_lse_combine_kernel, axis, n),
        out_shape=jax.ShapeDtypeStruct((8, m), jnp.float32),
        in_specs=[pl.BlockSpec(memory_space=pltpu.VMEM)] * 6,
        out_specs=pl.BlockSpec(memory_space=pltpu.VMEM),
        scratch_shapes=[
            pltpu.VMEM((2, 4, m), jnp.float32),
            pltpu.VMEM((n, 2, 4, m), jnp.float32),
            pltpu.SemaphoreType.DMA((2, n)),
            pltpu.SemaphoreType.DMA((2, n)),
        ],
        compiler_params=pltpu.CompilerParams(
            collective_id=5 if axis == "col" else 6, has_side_effects=True,
            vmem_limit_bytes=VMEM_LIMIT),
    )(p, q, a, b, log_mass, sq)


def squares(values):
    return jnp.sum(jnp.square(values.astype(jnp.float32)), axis=1)


def _peer(axis, k):
    if axis == "col":
        return (lax.axis_index("row"), k)
    return (k, lax.axis_index("col"))


def _gather_lse_kernel(axis, n, x_ref, m_ref, q_ref, o_ref, buf, send, recv):
    me = lax.axis_index(axis)
    barrier = pltpu.get_barrier_semaphore()
    for d in range(1, n):
        pl.semaphore_signal(barrier, inc=1, device_id=_peer(axis, lax.rem(me + d, n)),
                            device_id_type=pl.DeviceIdType.MESH)
    pl.semaphore_wait(barrier, n - 1)
    copies = []
    for d in range(1, n):
        copy = pltpu.make_async_remote_copy(
            src_ref=x_ref, dst_ref=buf.at[me], send_sem=send.at[d], recv_sem=recv.at[me],
            device_id=_peer(axis, lax.rem(me + d, n)), device_id_type=pl.DeviceIdType.MESH)
        copy.start()
        copies.append(copy)
    for copy in copies:
        copy.wait_send()
    for d in range(1, n):
        src = lax.rem(me + n - d, n)
        pltpu.make_async_remote_copy(
            src_ref=x_ref, dst_ref=buf.at[src], send_sem=send.at[d], recv_sem=recv.at[src],
            device_id=_peer(axis, src), device_id_type=pl.DeviceIdType.MESH).wait_recv()
    buf[me] = x_ref[...]
    parts = buf[...]
    top = jnp.max(parts, axis=0)
    total = top + jnp.log(jnp.sum(jnp.exp(parts - top[None]), axis=0))
    o_ref[...] = (EPS * (m_ref[...] - total) - q_ref[...]) * INV


def _exchange_kernel(jobs, *refs):
    count = len(jobs)
    ins, outs = refs[:count], refs[count:2 * count]
    bufs, sends, recvs = refs[2 * count::3], refs[2 * count + 1::3], refs[2 * count + 2::3]
    barrier = pltpu.get_barrier_semaphore()
    for axis, n, kind in jobs:
        me = lax.axis_index(axis)
        for d in range(1, n):
            pl.semaphore_signal(barrier, inc=1, device_id=_peer(axis, lax.rem(me + d, n)),
                                device_id_type=pl.DeviceIdType.MESH)
    pl.semaphore_wait(barrier, sum(n - 1 for _, n, _ in jobs))

    def copy(job, d, peer, slot):
        axis, n, kind = jobs[job]
        src = ins[job] if kind == "gather" else ins[job].at[peer]
        return pltpu.make_async_remote_copy(
            src_ref=src, dst_ref=bufs[job].at[slot], send_sem=sends[job].at[d],
            recv_sem=recvs[job].at[slot], device_id=_peer(axis, peer),
            device_id_type=pl.DeviceIdType.MESH)

    started = []
    for job, (axis, n, kind) in enumerate(jobs):
        me = lax.axis_index(axis)
        for d in range(1, n):
            started.append(copy(job, d, lax.rem(me + d, n), me))
            started[-1].start()
    for c in started:
        c.wait_send()
    for job, (axis, n, kind) in enumerate(jobs):
        me = lax.axis_index(axis)
        for d in range(1, n):
            src = lax.rem(me + n - d, n)
            copy(job, d, src, src).wait_recv()
        if kind == "gather":
            bufs[job][me] = ins[job][...]
            outs[job][...] = bufs[job][...]
        else:
            bufs[job][me] = ins[job][me]
            outs[job][...] = jnp.sum(bufs[job][...], axis=0)


def exchange(jobs, arrays, collective_id):
    shapes, scratch = [], []
    for (axis, n, kind), x in zip(jobs, arrays):
        block = x.shape if kind == "gather" else x.shape[1:]
        shapes.append(jax.ShapeDtypeStruct((n,) + block if kind == "gather" else block, x.dtype))
        scratch += [pltpu.VMEM((n,) + block, x.dtype), pltpu.SemaphoreType.DMA((n,)),
                    pltpu.SemaphoreType.DMA((n,))]
    return pl.pallas_call(
        functools.partial(_exchange_kernel, tuple(jobs)),
        out_shape=tuple(shapes),
        in_specs=[pl.BlockSpec(memory_space=pltpu.VMEM)] * len(jobs),
        out_specs=tuple(pl.BlockSpec(memory_space=pltpu.VMEM) for _ in jobs),
        scratch_shapes=scratch,
        compiler_params=pltpu.CompilerParams(
            collective_id=collective_id, has_side_effects=True, vmem_limit_bytes=VMEM_LIMIT),
    )(*arrays)


def combine(block, axis, log_mass, sq):
    n = lax.axis_size(axis)
    return pl.pallas_call(
        functools.partial(_gather_lse_kernel, axis, n),
        out_shape=jax.ShapeDtypeStruct(block.shape, jnp.float32),
        in_specs=[pl.BlockSpec(memory_space=pltpu.VMEM)] * 3,
        out_specs=pl.BlockSpec(memory_space=pltpu.VMEM),
        scratch_shapes=[
            pltpu.VMEM((n,) + block.shape, jnp.float32),
            pltpu.SemaphoreType.DMA((n,)),
            pltpu.SemaphoreType.DMA((n,)),
        ],
        compiler_params=pltpu.CompilerParams(
            collective_id=0 if axis == "col" else 1, has_side_effects=True),
    )(block, log_mass, sq)


def local(imu, camera, imu_mass, cam_mass):
    n_col, n_row = lax.axis_size("col"), lax.axis_size("row")
    imu_rows, cam_rows = exchange(
        [("col", n_col, "gather"), ("row", n_row, "gather")], [imu, camera[0]], 3)
    imu_rows = imu_rows.reshape(-1, D)
    cam_rows = cam_rows.reshape(-1, D)
    rows_sq = squares(imu_rows).reshape(8, -1)
    cols_sq = squares(cam_rows).reshape(8, -1)
    log_a = jnp.log(imu_mass).reshape(8, -1)
    log_b = jnp.log(cam_mass).reshape(8, -1)
    row_b = rows_sq * INV
    col_b = cols_sq * INV

    a = -col_b
    for step in range(ITERS):
        u = lse_combine(imu_rows, cam_rows, a, row_b, log_a, rows_sq, "col")
        a = lse_combine(cam_rows, imu_rows, u, col_b, log_b, cols_sq, "row")

    grad_imu, grad_cam = plan_scatter(imu_rows, cam_rows, u, a, n_col, n_row)
    return (grad_imu, grad_cam[None])


def solution(mesh):
    in_specs = (P(("row", "col"), None), P("col", "row", None), P("row"), P("col"))
    out_specs = (P(("row", "col"), None), P("col", "row", None))
    return jax.shard_map(local, mesh=mesh, in_specs=in_specs, out_specs=out_specs, check_vma=False)
```

```python
import functools

import jax
import jax.numpy as jnp
from jax import lax
from jax.experimental import pallas as pl
from jax.experimental.pallas import tpu as pltpu
from jax.sharding import PartitionSpec as P

D = 128
ITERS = 3
EPS = D / 20.0
INV = 1.0 / EPS
TWO_INV = 2.0 / EPS
VMEM_LIMIT = 60 * 1024 * 1024
LOG2E = 1.4426950408889634
LN2 = 0.6931471805599453
SCALE2 = TWO_INV * LOG2E
NT = (((1,), (1,)), ((), ()))
TN = (((0,), (0,)), ((), ()))


def _params(semantics):
    return pltpu.CompilerParams(dimension_semantics=semantics, vmem_limit_bytes=VMEM_LIMIT)


def _to_row(col):
    return jnp.transpose(jnp.broadcast_to(col, (col.shape[0], D)))[0:1, :]


def _to_col(row):
    return jnp.transpose(jnp.broadcast_to(row, (D, row.shape[1])))[:, 0:1]


def _row_of(v):
    return jnp.concatenate([v[k:k + 1, :] for k in range(v.shape[0])], axis=1)


def _lse_kernel(p_ref, q_ref, a_ref, b_ref, o_ref):
    i = pl.program_id(0)
    cross = lax.dot_general(p_ref[...], q_ref[...], NT, preferred_element_type=jnp.float32)
    t = _row_of(a_ref[...]) * LOG2E + SCALE2 * cross
    top = jnp.max(t, axis=1, keepdims=True)
    total = jnp.sum(jnp.exp2(t - top), axis=1, keepdims=True)
    o_ref[pl.ds(i, 1), :] = _to_row(top * LN2 + jnp.log(total)) - b_ref[pl.ds(i, 1), :]


def lse(p, q, a, b):
    rows, cols = p.shape[0], q.shape[0]
    tile = rows // 8
    return pl.pallas_call(
        _lse_kernel,
        out_shape=jax.ShapeDtypeStruct((8, tile), jnp.float32),
        grid=(8,),
        in_specs=[
            pl.BlockSpec((tile, D), lambda i: (i, 0)),
            pl.BlockSpec((cols, D), lambda i: (0, 0)),
            pl.BlockSpec((8, cols // 8), lambda i: (0, 0)),
            pl.BlockSpec((8, tile), lambda i: (0, 0)),
        ],
        out_specs=pl.BlockSpec((8, tile), lambda i: (0, 0)),
        compiler_params=_params(("arbitrary",)),
    )(p, q, a, b)


def _plan_kernel(x_ref, y_ref, u_ref, a_ref, gi_ref, pc_ref, c_ref):
    @pl.when(pl.program_id(0) == 0)
    def _():
        pc_ref[...] = jnp.zeros_like(pc_ref)
        c_ref[...] = jnp.zeros_like(c_ref)

    i = pl.program_id(0)
    x = x_ref[...]
    cross = lax.dot_general(x, y_ref[...], NT, preferred_element_type=jnp.float32)
    u = _to_col(u_ref[pl.ds(i, 1), :] * LOG2E)
    plan = jnp.exp2(u + _row_of(a_ref[...]) * LOG2E + SCALE2 * cross).astype(jnp.bfloat16)
    wide = plan.astype(jnp.float32)
    r = jnp.sum(wide, axis=1, keepdims=True)
    c_ref[...] += jnp.sum(wide, axis=0, keepdims=True)
    pulled = jnp.dot(plan, y_ref[...], preferred_element_type=jnp.float32)
    gi_ref[...] = 2.0 * (r * x.astype(jnp.float32) - pulled)
    pc_ref[...] += lax.dot_general(plan, x, TN, preferred_element_type=jnp.float32)


def plan_grads(x, y, u, a):
    rows, cols = x.shape[0], y.shape[0]
    return pl.pallas_call(
        _plan_kernel,
        out_shape=(
            jax.ShapeDtypeStruct((rows, D), jnp.float32),
            jax.ShapeDtypeStruct((cols, D), jnp.float32),
            jax.ShapeDtypeStruct((1, cols), jnp.float32),
        ),
        grid=(8,),
        in_specs=[
            pl.BlockSpec((rows // 8, D), lambda i: (i, 0)),
            pl.BlockSpec((cols, D), lambda i: (0, 0)),
            pl.BlockSpec((8, rows // 8), lambda i: (0, 0)),
            pl.BlockSpec((8, cols // 8), lambda i: (0, 0)),
        ],
        out_specs=(
            pl.BlockSpec((rows // 8, D), lambda i: (i, 0)),
            pl.BlockSpec((cols, D), lambda i: (0, 0)),
            pl.BlockSpec((1, cols), lambda i: (0, 0)),
        ),
        compiler_params=_params(("arbitrary",)),
    )(x, y, u, a)


def _plan_scatter_kernel(n_col, n_row, x_ref, y_ref, u_ref, a_ref, gi_out, gc_out,
                         gi, pc, csum, gcs, bufi, bufc, sendi, recvi, sendc, recvc):
    me_c, me_r = lax.axis_index("col"), lax.axis_index("row")
    barrier = pltpu.get_barrier_semaphore()
    for d in range(1, n_col):
        pl.semaphore_signal(barrier, inc=1, device_id=_peer("col", lax.rem(me_c + d, n_col)),
                            device_id_type=pl.DeviceIdType.MESH)
    for d in range(1, n_row):
        pl.semaphore_signal(barrier, inc=1, device_id=_peer("row", lax.rem(me_r + d, n_row)),
                            device_id_type=pl.DeviceIdType.MESH)

    def to_col_dev(k, slot):
        return pltpu.make_async_remote_copy(
            src_ref=gi.at[k], dst_ref=bufi.at[slot], send_sem=sendi.at[k], recv_sem=recvi.at[slot],
            device_id=_peer("col", k), device_id_type=pl.DeviceIdType.MESH)

    def to_row_dev(k, slot):
        return pltpu.make_async_remote_copy(
            src_ref=gcs.at[k], dst_ref=bufc.at[slot], send_sem=sendc.at[k], recv_sem=recvc.at[slot],
            device_id=_peer("row", k), device_id_type=pl.DeviceIdType.MESH)

    def each(n, me, body):
        for k in range(n):
            pl.when(me != k)(functools.partial(body, k))

    rows, cols = x_ref.shape[0], y_ref.shape[0]
    tiles = u_ref.shape[0]
    tile, m, mc = rows // tiles, rows // n_col, cols // n_row
    per = tile // m
    y = y_ref[...]
    a2 = _row_of(a_ref[...]) * LOG2E
    pc[...] = jnp.zeros_like(pc)
    csum[...] = jnp.zeros_like(csum)
    for i in range(tiles):
        x = x_ref[i * tile:(i + 1) * tile, :]
        cross = lax.dot_general(x, y, NT, preferred_element_type=jnp.float32)
        u = _to_col(u_ref[i:i + 1, :] * LOG2E)
        plan = jnp.exp2(u + a2 + SCALE2 * cross).astype(jnp.bfloat16)
        wide = plan.astype(jnp.float32)
        r = jnp.sum(wide, axis=1, keepdims=True)
        csum[...] += jnp.sum(wide, axis=0, keepdims=True)
        pulled = jnp.dot(plan, y, preferred_element_type=jnp.float32)
        g = 2.0 * (r * x.astype(jnp.float32) - pulled)
        for s in range(per):
            gi[i * per + s] = g[s * m:(s + 1) * m]
        pc[...] += lax.dot_general(plan, x, TN, preferred_element_type=jnp.float32)
        if i == 1:
            pl.semaphore_wait(barrier, n_col + n_row - 2)
        if i >= 1:
            for s in range((i - 1) * per, i * per):
                pl.when(me_c != s)(functools.partial(lambda k: to_col_dev(k, me_c).start(), s))
    for s in range((tiles - 1) * per, tiles * per):
        pl.when(me_c != s)(functools.partial(lambda k: to_col_dev(k, me_c).start(), s))
    gcv = 2.0 * (_to_col(csum[...]) * y.astype(jnp.float32) - pc[...])
    for k in range(n_row):
        gcs[k] = gcv[k * mc:(k + 1) * mc]
    each(n_row, me_r, lambda k: to_row_dev(k, me_r).start())
    each(n_col, me_c, lambda k: to_col_dev(k, me_c).wait_send())
    each(n_row, me_r, lambda k: to_row_dev(k, me_r).wait_send())
    each(n_col, me_c, lambda k: to_col_dev(k, k).wait_recv())
    each(n_row, me_r, lambda k: to_row_dev(k, k).wait_recv())
    bufi[me_c] = gi[me_c]
    bufc[me_r] = gcs[me_r]
    gi_out[...] = jnp.sum(bufi[...], axis=0)
    gc_out[...] = jnp.sum(bufc[...], axis=0)


def plan_scatter(x, y, u, a, n_col, n_row):
    rows, cols = x.shape[0], y.shape[0]
    m, mc = rows // n_col, cols // n_row
    return pl.pallas_call(
        functools.partial(_plan_scatter_kernel, n_col, n_row),
        out_shape=(jax.ShapeDtypeStruct((m, D), jnp.float32),
                   jax.ShapeDtypeStruct((mc, D), jnp.float32)),
        in_specs=[pl.BlockSpec(memory_space=pltpu.VMEM)] * 4,
        out_specs=(pl.BlockSpec(memory_space=pltpu.VMEM),) * 2,
        scratch_shapes=[
            pltpu.VMEM((n_col, m, D), jnp.float32),
            pltpu.VMEM((cols, D), jnp.float32),
            pltpu.VMEM((1, cols), jnp.float32),
            pltpu.VMEM((n_row, mc, D), jnp.float32),
            pltpu.VMEM((n_col, m, D), jnp.float32),
            pltpu.VMEM((n_row, mc, D), jnp.float32),
            pltpu.SemaphoreType.DMA((n_col,)),
            pltpu.SemaphoreType.DMA((n_col,)),
            pltpu.SemaphoreType.DMA((n_row,)),
            pltpu.SemaphoreType.DMA((n_row,)),
        ],
        compiler_params=pltpu.CompilerParams(
            collective_id=4, has_side_effects=True, vmem_limit_bytes=VMEM_LIMIT),
    )(x, y, u, a)


def _lse_combine_kernel(axis, n, p_ref, q_ref, a_ref, b_ref, m_ref, s_ref, o_ref,
                        part, buf, send, recv):
    me = lax.axis_index(axis)
    barrier = pltpu.get_barrier_semaphore()
    for d in range(1, n):
        pl.semaphore_signal(barrier, inc=1, device_id=_peer(axis, lax.rem(me + d, n)),
                            device_id_type=pl.DeviceIdType.MESH)

    def out_copy(c, d):
        return pltpu.make_async_remote_copy(
            src_ref=part.at[c], dst_ref=buf.at[me, c], send_sem=send.at[c, d],
            recv_sem=recv.at[c, me], device_id=_peer(axis, lax.rem(me + d, n)),
            device_id_type=pl.DeviceIdType.MESH)

    def in_copy(c, d):
        src = lax.rem(me + n - d, n)
        return pltpu.make_async_remote_copy(
            src_ref=part.at[c], dst_ref=buf.at[src, c], send_sem=send.at[c, d],
            recv_sem=recv.at[c, src], device_id=_peer(axis, src),
            device_id_type=pl.DeviceIdType.MESH)

    def send_half(c):
        for d in range(1, n):
            out_copy(c, d).start()

    half = part.shape[1]
    tile = p_ref.shape[0] // (2 * half)
    q = q_ref[...]
    a2 = _row_of(a_ref[...]) * LOG2E

    def body(i, carry):
        start = pl.multiple_of(i * tile, tile)
        cross = lax.dot_general(p_ref[pl.ds(start, tile), :], q, NT,
                                preferred_element_type=jnp.float32)
        t = a2 + SCALE2 * cross
        top = jnp.max(t, axis=1, keepdims=True)
        total = jnp.sum(jnp.exp2(t - top), axis=1, keepdims=True)
        row = _to_row(top * LN2 + jnp.log(total)) - b_ref[pl.ds(i, 1), :]
        part.at[i // half][pl.ds(i % half, 1), :] = row

        @pl.when(i == half)
        def _():
            pl.semaphore_wait(barrier, n - 1)
            send_half(0)

        return carry

    lax.fori_loop(0, 2 * half, body, 0)

    def finish(c):
        for d in range(1, n):
            out_copy(c, d).wait_send()
        for d in range(1, n):
            in_copy(c, d).wait_recv()
        buf[me, c] = part[c]
        parts = buf[:, c]
        top = jnp.max(parts, axis=0)
        total = top + jnp.log(jnp.sum(jnp.exp(parts - top[None]), axis=0))
        rows = slice(c * half, (c + 1) * half)
        o_ref[rows, :] = (EPS * (m_ref[rows, :] - total) - s_ref[rows, :]) * INV

    finish(0)
    send_half(1)
    finish(1)


def lse_combine(p, q, a, b, log_mass, sq, axis):
    n = lax.axis_size(axis)
    m = p.shape[0] // 8
    return pl.pallas_call(
        functools.partial(_lse_combine_kernel, axis, n),
        out_shape=jax.ShapeDtypeStruct((8, m), jnp.float32),
        in_specs=[pl.BlockSpec(memory_space=pltpu.VMEM)] * 6,
        out_specs=pl.BlockSpec(memory_space=pltpu.VMEM),
        scratch_shapes=[
            pltpu.VMEM((2, 4, m), jnp.float32),
            pltpu.VMEM((n, 2, 4, m), jnp.float32),
            pltpu.SemaphoreType.DMA((2, n)),
            pltpu.SemaphoreType.DMA((2, n)),
        ],
        compiler_params=pltpu.CompilerParams(
            collective_id=5 if axis == "col" else 6, has_side_effects=True,
            vmem_limit_bytes=VMEM_LIMIT),
    )(p, q, a, b, log_mass, sq)


def squares(values):
    return jnp.sum(jnp.square(values.astype(jnp.float32)), axis=1)


def _peer(axis, k):
    if axis == "col":
        return (lax.axis_index("row"), k)
    return (k, lax.axis_index("col"))


def _gather_lse_kernel(axis, n, x_ref, m_ref, q_ref, o_ref, buf, send, recv):
    me = lax.axis_index(axis)
    barrier = pltpu.get_barrier_semaphore()
    for d in range(1, n):
        pl.semaphore_signal(barrier, inc=1, device_id=_peer(axis, lax.rem(me + d, n)),
                            device_id_type=pl.DeviceIdType.MESH)
    pl.semaphore_wait(barrier, n - 1)
    copies = []
    for d in range(1, n):
        copy = pltpu.make_async_remote_copy(
            src_ref=x_ref, dst_ref=buf.at[me], send_sem=send.at[d], recv_sem=recv.at[me],
            device_id=_peer(axis, lax.rem(me + d, n)), device_id_type=pl.DeviceIdType.MESH)
        copy.start()
        copies.append(copy)
    for copy in copies:
        copy.wait_send()
    for d in range(1, n):
        src = lax.rem(me + n - d, n)
        pltpu.make_async_remote_copy(
            src_ref=x_ref, dst_ref=buf.at[src], send_sem=send.at[d], recv_sem=recv.at[src],
            device_id=_peer(axis, src), device_id_type=pl.DeviceIdType.MESH).wait_recv()
    buf[me] = x_ref[...]
    parts = buf[...]
    top = jnp.max(parts, axis=0)
    total = top + jnp.log(jnp.sum(jnp.exp(parts - top[None]), axis=0))
    o_ref[...] = (EPS * (m_ref[...] - total) - q_ref[...]) * INV


def _exchange_kernel(jobs, *refs):
    count = len(jobs)
    ins, outs = refs[:count], refs[count:2 * count]
    bufs, sends, recvs = refs[2 * count::3], refs[2 * count + 1::3], refs[2 * count + 2::3]
    barrier = pltpu.get_barrier_semaphore()
    for axis, n, kind in jobs:
        me = lax.axis_index(axis)
        for d in range(1, n):
            pl.semaphore_signal(barrier, inc=1, device_id=_peer(axis, lax.rem(me + d, n)),
                                device_id_type=pl.DeviceIdType.MESH)
    pl.semaphore_wait(barrier, sum(n - 1 for _, n, _ in jobs))

    def copy(job, d, peer, slot):
        axis, n, kind = jobs[job]
        src = ins[job] if kind == "gather" else ins[job].at[peer]
        return pltpu.make_async_remote_copy(
            src_ref=src, dst_ref=bufs[job].at[slot], send_sem=sends[job].at[d],
            recv_sem=recvs[job].at[slot], device_id=_peer(axis, peer),
            device_id_type=pl.DeviceIdType.MESH)

    started = []
    for job, (axis, n, kind) in enumerate(jobs):
        me = lax.axis_index(axis)
        for d in range(1, n):
            started.append(copy(job, d, lax.rem(me + d, n), me))
            started[-1].start()
    for c in started:
        c.wait_send()
    for job, (axis, n, kind) in enumerate(jobs):
        me = lax.axis_index(axis)
        for d in range(1, n):
            src = lax.rem(me + n - d, n)
            copy(job, d, src, src).wait_recv()
        if kind == "gather":
            bufs[job][me] = ins[job][...]
            outs[job][...] = bufs[job][...]
        else:
            bufs[job][me] = ins[job][me]
            outs[job][...] = jnp.sum(bufs[job][...], axis=0)


def exchange(jobs, arrays, collective_id):
    shapes, scratch = [], []
    for (axis, n, kind), x in zip(jobs, arrays):
        block = x.shape if kind == "gather" else x.shape[1:]
        shapes.append(jax.ShapeDtypeStruct((n,) + block if kind == "gather" else block, x.dtype))
        scratch += [pltpu.VMEM((n,) + block, x.dtype), pltpu.SemaphoreType.DMA((n,)),
                    pltpu.SemaphoreType.DMA((n,))]
    return pl.pallas_call(
        functools.partial(_exchange_kernel, tuple(jobs)),
        out_shape=tuple(shapes),
        in_specs=[pl.BlockSpec(memory_space=pltpu.VMEM)] * len(jobs),
        out_specs=tuple(pl.BlockSpec(memory_space=pltpu.VMEM) for _ in jobs),
        scratch_shapes=scratch,
        compiler_params=pltpu.CompilerParams(
            collective_id=collective_id, has_side_effects=True, vmem_limit_bytes=VMEM_LIMIT),
    )(*arrays)


def combine(block, axis, log_mass, sq):
    n = lax.axis_size(axis)
    return pl.pallas_call(
        functools.partial(_gather_lse_kernel, axis, n),
        out_shape=jax.ShapeDtypeStruct(block.shape, jnp.float32),
        in_specs=[pl.BlockSpec(memory_space=pltpu.VMEM)] * 3,
        out_specs=pl.BlockSpec(memory_space=pltpu.VMEM),
        scratch_shapes=[
            pltpu.VMEM((n,) + block.shape, jnp.float32),
            pltpu.SemaphoreType.DMA((n,)),
            pltpu.SemaphoreType.DMA((n,)),
        ],
        compiler_params=pltpu.CompilerParams(
            collective_id=0 if axis == "col" else 1, has_side_effects=True),
    )(block, log_mass, sq)


def local(imu, camera, imu_mass, cam_mass):
    n_col, n_row = lax.axis_size("col"), lax.axis_size("row")
    imu_rows, cam_rows = exchange(
        [("col", n_col, "gather"), ("row", n_row, "gather")], [imu, camera[0]], 3)
    imu_rows = imu_rows.reshape(-1, D)
    cam_rows = cam_rows.reshape(-1, D)
    rows_sq = squares(imu_rows).reshape(8, -1)
    cols_sq = squares(cam_rows).reshape(8, -1)
    log_a = jnp.log(imu_mass).reshape(8, -1)
    log_b = jnp.log(cam_mass).reshape(8, -1)
    row_b = rows_sq * INV
    col_b = cols_sq * INV

    a = -col_b
    for step in range(ITERS):
        u = lse_combine(imu_rows, cam_rows, a, row_b, log_a, rows_sq, "col")
        a = lse_combine(cam_rows, imu_rows, u, col_b, log_b, cols_sq, "row")

    grad_imu, grad_cam = plan_scatter(imu_rows, cam_rows, u, a, n_col, n_row)
    return (grad_imu, grad_cam[None])


def solution(mesh):
    in_specs = (P(("row", "col"), None), P("col", "row", None), P("row"), P("col"))
    out_specs = (P(("row", "col"), None), P("col", "row", None))
    return jax.shard_map(local, mesh=mesh, in_specs=in_specs, out_specs=out_specs, check_vma=False)
```

```python
import functools

import jax
import jax.numpy as jnp
from jax import lax
from jax.experimental import pallas as pl
from jax.experimental.pallas import tpu as pltpu
from jax.sharding import PartitionSpec as P

D = 128
ITERS = 3
EPS = D / 20.0
INV = 1.0 / EPS
TWO_INV = 2.0 / EPS
VMEM_LIMIT = 60 * 1024 * 1024
LOG2E = 1.4426950408889634
LN2 = 0.6931471805599453
SCALE2 = TWO_INV * LOG2E
NT = (((1,), (1,)), ((), ()))
TN = (((0,), (0,)), ((), ()))


def _params(semantics):
    return pltpu.CompilerParams(dimension_semantics=semantics, vmem_limit_bytes=VMEM_LIMIT)


def _to_row(col):
    return jnp.transpose(jnp.broadcast_to(col, (col.shape[0], D)))[0:1, :]


def _to_col(row):
    return jnp.transpose(jnp.broadcast_to(row, (D, row.shape[1])))[:, 0:1]


def _row_of(v):
    return jnp.concatenate([v[k:k + 1, :] for k in range(v.shape[0])], axis=1)


def _lse_kernel(p_ref, q_ref, a_ref, b_ref, o_ref):
    i = pl.program_id(0)
    cross = lax.dot_general(p_ref[...], q_ref[...], NT, preferred_element_type=jnp.float32)
    t = _row_of(a_ref[...]) * LOG2E + SCALE2 * cross
    top = jnp.max(t, axis=1, keepdims=True)
    total = jnp.sum(jnp.exp2(t - top), axis=1, keepdims=True)
    o_ref[pl.ds(i, 1), :] = _to_row(top * LN2 + jnp.log(total)) - b_ref[pl.ds(i, 1), :]


def lse(p, q, a, b):
    rows, cols = p.shape[0], q.shape[0]
    tile = rows // 8
    return pl.pallas_call(
        _lse_kernel,
        out_shape=jax.ShapeDtypeStruct((8, tile), jnp.float32),
        grid=(8,),
        in_specs=[
            pl.BlockSpec((tile, D), lambda i: (i, 0)),
            pl.BlockSpec((cols, D), lambda i: (0, 0)),
            pl.BlockSpec((8, cols // 8), lambda i: (0, 0)),
            pl.BlockSpec((8, tile), lambda i: (0, 0)),
        ],
        out_specs=pl.BlockSpec((8, tile), lambda i: (0, 0)),
        compiler_params=_params(("arbitrary",)),
    )(p, q, a, b)


def _plan_kernel(x_ref, y_ref, u_ref, a_ref, gi_ref, pc_ref, c_ref):
    @pl.when(pl.program_id(0) == 0)
    def _():
        pc_ref[...] = jnp.zeros_like(pc_ref)
        c_ref[...] = jnp.zeros_like(c_ref)

    i = pl.program_id(0)
    x = x_ref[...]
    cross = lax.dot_general(x, y_ref[...], NT, preferred_element_type=jnp.float32)
    u = _to_col(u_ref[pl.ds(i, 1), :] * LOG2E)
    plan = jnp.exp2(u + _row_of(a_ref[...]) * LOG2E + SCALE2 * cross).astype(jnp.bfloat16)
    wide = plan.astype(jnp.float32)
    r = jnp.sum(wide, axis=1, keepdims=True)
    c_ref[...] += jnp.sum(wide, axis=0, keepdims=True)
    pulled = jnp.dot(plan, y_ref[...], preferred_element_type=jnp.float32)
    gi_ref[...] = 2.0 * (r * x.astype(jnp.float32) - pulled)
    pc_ref[...] += lax.dot_general(plan, x, TN, preferred_element_type=jnp.float32)


def plan_grads(x, y, u, a):
    rows, cols = x.shape[0], y.shape[0]
    return pl.pallas_call(
        _plan_kernel,
        out_shape=(
            jax.ShapeDtypeStruct((rows, D), jnp.float32),
            jax.ShapeDtypeStruct((cols, D), jnp.float32),
            jax.ShapeDtypeStruct((1, cols), jnp.float32),
        ),
        grid=(8,),
        in_specs=[
            pl.BlockSpec((rows // 8, D), lambda i: (i, 0)),
            pl.BlockSpec((cols, D), lambda i: (0, 0)),
            pl.BlockSpec((8, rows // 8), lambda i: (0, 0)),
            pl.BlockSpec((8, cols // 8), lambda i: (0, 0)),
        ],
        out_specs=(
            pl.BlockSpec((rows // 8, D), lambda i: (i, 0)),
            pl.BlockSpec((cols, D), lambda i: (0, 0)),
            pl.BlockSpec((1, cols), lambda i: (0, 0)),
        ),
        compiler_params=_params(("arbitrary",)),
    )(x, y, u, a)


def _plan_scatter_kernel(n_col, n_row, x_ref, y_ref, u_ref, a_ref, gi_out, gc_out,
                         gi, pc, csum, gcs, bufi, bufc, sendi, recvi, sendc, recvc):
    me_c, me_r = lax.axis_index("col"), lax.axis_index("row")
    barrier = pltpu.get_barrier_semaphore()
    for d in range(1, n_col):
        pl.semaphore_signal(barrier, inc=1, device_id=_peer("col", lax.rem(me_c + d, n_col)),
                            device_id_type=pl.DeviceIdType.MESH)
    for d in range(1, n_row):
        pl.semaphore_signal(barrier, inc=1, device_id=_peer("row", lax.rem(me_r + d, n_row)),
                            device_id_type=pl.DeviceIdType.MESH)

    def to_col_dev(k, slot):
        return pltpu.make_async_remote_copy(
            src_ref=gi.at[k], dst_ref=bufi.at[slot], send_sem=sendi.at[k], recv_sem=recvi.at[slot],
            device_id=_peer("col", k), device_id_type=pl.DeviceIdType.MESH)

    def to_row_dev(k, slot):
        return pltpu.make_async_remote_copy(
            src_ref=gcs.at[k], dst_ref=bufc.at[slot], send_sem=sendc.at[k], recv_sem=recvc.at[slot],
            device_id=_peer("row", k), device_id_type=pl.DeviceIdType.MESH)

    def each(n, me, body):
        for k in range(n):
            pl.when(me != k)(functools.partial(body, k))

    rows, cols = x_ref.shape[0], y_ref.shape[0]
    tiles = u_ref.shape[0]
    tile, m, mc = rows // tiles, rows // n_col, cols // n_row
    per = tile // m
    y = y_ref[...]
    a2 = _row_of(a_ref[...]) * LOG2E
    pc[...] = jnp.zeros_like(pc)
    csum[...] = jnp.zeros_like(csum)
    for i in range(tiles):
        x = x_ref[i * tile:(i + 1) * tile, :]
        cross = lax.dot_general(x, y, NT, preferred_element_type=jnp.float32)
        u = _to_col(u_ref[i:i + 1, :] * LOG2E)
        plan = jnp.exp2(u + a2 + SCALE2 * cross).astype(jnp.bfloat16)
        wide = plan.astype(jnp.float32)
        r = jnp.sum(wide, axis=1, keepdims=True)
        csum[...] += jnp.sum(wide, axis=0, keepdims=True)
        pulled = jnp.dot(plan, y, preferred_element_type=jnp.float32)
        g = 2.0 * (r * x.astype(jnp.float32) - pulled)
        for s in range(per):
            gi[i * per + s] = g[s * m:(s + 1) * m]
        pc[...] += lax.dot_general(plan, x, TN, preferred_element_type=jnp.float32)
        if i == 1:
            pl.semaphore_wait(barrier, n_col + n_row - 2)
        if i >= 1:
            for s in range((i - 1) * per, i * per):
                pl.when(me_c != s)(functools.partial(lambda k: to_col_dev(k, me_c).start(), s))
    for s in range((tiles - 1) * per, tiles * per):
        pl.when(me_c != s)(functools.partial(lambda k: to_col_dev(k, me_c).start(), s))
    gcv = 2.0 * (_to_col(csum[...]) * y.astype(jnp.float32) - pc[...])
    for k in range(n_row):
        gcs[k] = gcv[k * mc:(k + 1) * mc]
    each(n_row, me_r, lambda k: to_row_dev(k, me_r).start())
    each(n_col, me_c, lambda k: to_col_dev(k, me_c).wait_send())
    each(n_row, me_r, lambda k: to_row_dev(k, me_r).wait_send())
    each(n_col, me_c, lambda k: to_col_dev(k, k).wait_recv())
    each(n_row, me_r, lambda k: to_row_dev(k, k).wait_recv())
    bufi[me_c] = gi[me_c]
    bufc[me_r] = gcs[me_r]
    gi_out[...] = jnp.sum(bufi[...], axis=0)
    gc_out[...] = jnp.sum(bufc[...], axis=0)


def plan_scatter(x, y, u, a, n_col, n_row):
    rows, cols = x.shape[0], y.shape[0]
    m, mc = rows // n_col, cols // n_row
    return pl.pallas_call(
        functools.partial(_plan_scatter_kernel, n_col, n_row),
        out_shape=(jax.ShapeDtypeStruct((m, D), jnp.float32),
                   jax.ShapeDtypeStruct((mc, D), jnp.float32)),
        in_specs=[pl.BlockSpec(memory_space=pltpu.VMEM)] * 4,
        out_specs=(pl.BlockSpec(memory_space=pltpu.VMEM),) * 2,
        scratch_shapes=[
            pltpu.VMEM((n_col, m, D), jnp.float32),
            pltpu.VMEM((cols, D), jnp.float32),
            pltpu.VMEM((1, cols), jnp.float32),
            pltpu.VMEM((n_row, mc, D), jnp.float32),
            pltpu.VMEM((n_col, m, D), jnp.float32),
            pltpu.VMEM((n_row, mc, D), jnp.float32),
            pltpu.SemaphoreType.DMA((n_col,)),
            pltpu.SemaphoreType.DMA((n_col,)),
            pltpu.SemaphoreType.DMA((n_row,)),
            pltpu.SemaphoreType.DMA((n_row,)),
        ],
        compiler_params=pltpu.CompilerParams(
            collective_id=4, has_side_effects=True, vmem_limit_bytes=VMEM_LIMIT),
    )(x, y, u, a)


def _lse_combine_kernel(axis, n, p_ref, q_ref, a_ref, m_ref, s_ref, o_ref,
                        part, buf, send, recv):
    me = lax.axis_index(axis)
    barrier = pltpu.get_barrier_semaphore()
    for d in range(1, n):
        pl.semaphore_signal(barrier, inc=1, device_id=_peer(axis, lax.rem(me + d, n)),
                            device_id_type=pl.DeviceIdType.MESH)

    def out_copy(c, d):
        return pltpu.make_async_remote_copy(
            src_ref=part.at[c], dst_ref=buf.at[me, c], send_sem=send.at[c, d],
            recv_sem=recv.at[c, me], device_id=_peer(axis, lax.rem(me + d, n)),
            device_id_type=pl.DeviceIdType.MESH)

    def in_copy(c, d):
        src = lax.rem(me + n - d, n)
        return pltpu.make_async_remote_copy(
            src_ref=part.at[c], dst_ref=buf.at[src, c], send_sem=send.at[c, d],
            recv_sem=recv.at[c, src], device_id=_peer(axis, src),
            device_id_type=pl.DeviceIdType.MESH)

    def send_half(c):
        for d in range(1, n):
            out_copy(c, d).start()

    half = part.shape[1]
    tile = p_ref.shape[0] // (2 * half)
    q = q_ref[...]
    a2 = _row_of(a_ref[...]) * LOG2E

    def body(i, carry):
        start = pl.multiple_of(i * tile, tile)
        cross = lax.dot_general(p_ref[pl.ds(start, tile), :], q, NT,
                                preferred_element_type=jnp.float32)
        t = a2 + SCALE2 * cross
        top = jnp.max(t, axis=1, keepdims=True)
        total = jnp.sum(jnp.exp2(t - top), axis=1, keepdims=True)
        row = _to_row(top * LN2 + jnp.log(total)) - s_ref[pl.ds(i, 1), :] * INV
        part.at[i // half][pl.ds(i % half, 1), :] = row

        @pl.when(i == half)
        def _():
            pl.semaphore_wait(barrier, n - 1)
            send_half(0)

        return carry

    lax.fori_loop(0, 2 * half, body, 0)

    def finish(c):
        for d in range(1, n):
            out_copy(c, d).wait_send()
        for d in range(1, n):
            in_copy(c, d).wait_recv()
        buf[me, c] = part[c]
        parts = buf[:, c]
        top = jnp.max(parts, axis=0)
        total = top + jnp.log(jnp.sum(jnp.exp(parts - top[None]), axis=0))
        rows = slice(c * half, (c + 1) * half)
        o_ref[rows, :] = (EPS * (m_ref[rows, :] - total) - s_ref[rows, :]) * INV

    finish(0)
    send_half(1)
    finish(1)


def lse_combine(p, q, a, log_mass, sq, axis):
    n = lax.axis_size(axis)
    m = p.shape[0] // 8
    return pl.pallas_call(
        functools.partial(_lse_combine_kernel, axis, n),
        out_shape=jax.ShapeDtypeStruct((8, m), jnp.float32),
        in_specs=[pl.BlockSpec(memory_space=pltpu.VMEM)] * 5,
        out_specs=pl.BlockSpec(memory_space=pltpu.VMEM),
        scratch_shapes=[
            pltpu.VMEM((2, 4, m), jnp.float32),
            pltpu.VMEM((n, 2, 4, m), jnp.float32),
            pltpu.SemaphoreType.DMA((2, n)),
            pltpu.SemaphoreType.DMA((2, n)),
        ],
        compiler_params=pltpu.CompilerParams(
            collective_id=5 if axis == "col" else 6, has_side_effects=True,
            vmem_limit_bytes=VMEM_LIMIT),
    )(p, q, a, log_mass, sq)


def squares(values):
    return jnp.sum(jnp.square(values.astype(jnp.float32)), axis=1)


def _peer(axis, k):
    if axis == "col":
        return (lax.axis_index("row"), k)
    return (k, lax.axis_index("col"))


def _gather_lse_kernel(axis, n, x_ref, m_ref, q_ref, o_ref, buf, send, recv):
    me = lax.axis_index(axis)
    barrier = pltpu.get_barrier_semaphore()
    for d in range(1, n):
        pl.semaphore_signal(barrier, inc=1, device_id=_peer(axis, lax.rem(me + d, n)),
                            device_id_type=pl.DeviceIdType.MESH)
    pl.semaphore_wait(barrier, n - 1)
    copies = []
    for d in range(1, n):
        copy = pltpu.make_async_remote_copy(
            src_ref=x_ref, dst_ref=buf.at[me], send_sem=send.at[d], recv_sem=recv.at[me],
            device_id=_peer(axis, lax.rem(me + d, n)), device_id_type=pl.DeviceIdType.MESH)
        copy.start()
        copies.append(copy)
    for copy in copies:
        copy.wait_send()
    for d in range(1, n):
        src = lax.rem(me + n - d, n)
        pltpu.make_async_remote_copy(
            src_ref=x_ref, dst_ref=buf.at[src], send_sem=send.at[d], recv_sem=recv.at[src],
            device_id=_peer(axis, src), device_id_type=pl.DeviceIdType.MESH).wait_recv()
    buf[me] = x_ref[...]
    parts = buf[...]
    top = jnp.max(parts, axis=0)
    total = top + jnp.log(jnp.sum(jnp.exp(parts - top[None]), axis=0))
    o_ref[...] = (EPS * (m_ref[...] - total) - q_ref[...]) * INV


def _exchange_kernel(jobs, *refs):
    count = len(jobs)
    ins, outs = refs[:count], refs[count:2 * count]
    gathers = sum(kind == "gather" for _, _, kind in jobs)
    sqs = refs[2 * count:2 * count + gathers]
    rest = refs[2 * count + gathers:]
    bufs, sends, recvs = rest[0::3], rest[1::3], rest[2::3]
    barrier = pltpu.get_barrier_semaphore()
    for axis, n, kind in jobs:
        me = lax.axis_index(axis)
        for d in range(1, n):
            pl.semaphore_signal(barrier, inc=1, device_id=_peer(axis, lax.rem(me + d, n)),
                                device_id_type=pl.DeviceIdType.MESH)
    pl.semaphore_wait(barrier, sum(n - 1 for _, n, _ in jobs))

    def copy(job, d, peer, slot):
        axis, n, kind = jobs[job]
        src = ins[job] if kind == "gather" else ins[job].at[peer]
        return pltpu.make_async_remote_copy(
            src_ref=src, dst_ref=bufs[job].at[slot], send_sem=sends[job].at[d],
            recv_sem=recvs[job].at[slot], device_id=_peer(axis, peer),
            device_id_type=pl.DeviceIdType.MESH)

    started = []
    for job, (axis, n, kind) in enumerate(jobs):
        me = lax.axis_index(axis)
        for d in range(1, n):
            started.append(copy(job, d, lax.rem(me + d, n), me))
            started[-1].start()
    for c in started:
        c.wait_send()
    for job, (axis, n, kind) in enumerate(jobs):
        me = lax.axis_index(axis)
        for d in range(1, n):
            src = lax.rem(me + n - d, n)
            copy(job, d, src, src).wait_recv()
        if kind == "gather":
            bufs[job][me] = ins[job][...]
            outs[job][...] = bufs[job][...]
            sq = sqs[job]
            m = bufs[job].shape[1]
            per = sq.shape[1] // m
            for j in range(n):
                v = bufs[job][j].astype(jnp.float32)
                row = _to_row(jnp.sum(v * v, axis=1, keepdims=True))
                sq[j // per:j // per + 1, (j % per) * m:(j % per + 1) * m] = row
        else:
            bufs[job][me] = ins[job][me]
            outs[job][...] = jnp.sum(bufs[job][...], axis=0)


def exchange(jobs, arrays, collective_id):
    shapes, scratch = [], []
    for (axis, n, kind), x in zip(jobs, arrays):
        block = x.shape if kind == "gather" else x.shape[1:]
        shapes.append(jax.ShapeDtypeStruct((n,) + block if kind == "gather" else block, x.dtype))
        scratch += [pltpu.VMEM((n,) + block, x.dtype), pltpu.SemaphoreType.DMA((n,)),
                    pltpu.SemaphoreType.DMA((n,))]
    for (axis, n, kind), x in zip(jobs, arrays):
        if kind == "gather":
            shapes.append(jax.ShapeDtypeStruct((8, n * x.shape[0] // 8), jnp.float32))
    return pl.pallas_call(
        functools.partial(_exchange_kernel, tuple(jobs)),
        out_shape=tuple(shapes),
        in_specs=[pl.BlockSpec(memory_space=pltpu.VMEM)] * len(jobs),
        out_specs=tuple(pl.BlockSpec(memory_space=pltpu.VMEM) for _ in shapes),
        scratch_shapes=scratch,
        compiler_params=pltpu.CompilerParams(
            collective_id=collective_id, has_side_effects=True, vmem_limit_bytes=VMEM_LIMIT),
    )(*arrays)


def combine(block, axis, log_mass, sq):
    n = lax.axis_size(axis)
    return pl.pallas_call(
        functools.partial(_gather_lse_kernel, axis, n),
        out_shape=jax.ShapeDtypeStruct(block.shape, jnp.float32),
        in_specs=[pl.BlockSpec(memory_space=pltpu.VMEM)] * 3,
        out_specs=pl.BlockSpec(memory_space=pltpu.VMEM),
        scratch_shapes=[
            pltpu.VMEM((n,) + block.shape, jnp.float32),
            pltpu.SemaphoreType.DMA((n,)),
            pltpu.SemaphoreType.DMA((n,)),
        ],
        compiler_params=pltpu.CompilerParams(
            collective_id=0 if axis == "col" else 1, has_side_effects=True),
    )(block, log_mass, sq)


def local(imu, camera, imu_mass, cam_mass):
    n_col, n_row = lax.axis_size("col"), lax.axis_size("row")
    imu_rows, cam_rows, rows_sq, cols_sq = exchange(
        [("col", n_col, "gather"), ("row", n_row, "gather")], [imu, camera[0]], 3)
    imu_rows = imu_rows.reshape(-1, D)
    cam_rows = cam_rows.reshape(-1, D)
    log_a = jnp.log(imu_mass).reshape(8, -1)
    log_b = jnp.log(cam_mass).reshape(8, -1)

    a = -cols_sq * INV
    for step in range(ITERS):
        u = lse_combine(imu_rows, cam_rows, a, log_a, rows_sq, "col")
        a = lse_combine(cam_rows, imu_rows, u, log_b, cols_sq, "row")

    grad_imu, grad_cam = plan_scatter(imu_rows, cam_rows, u, a, n_col, n_row)
    return (grad_imu, grad_cam[None])


def solution(mesh):
    in_specs = (P(("row", "col"), None), P("col", "row", None), P("row"), P("col"))
    out_specs = (P(("row", "col"), None), P("col", "row", None))
    return jax.shard_map(local, mesh=mesh, in_specs=in_specs, out_specs=out_specs, check_vma=False)
```

```python
import functools

import jax
import jax.numpy as jnp
from jax import lax
from jax.experimental import pallas as pl
from jax.experimental.pallas import tpu as pltpu
from jax.sharding import PartitionSpec as P

D = 128
ITERS = 3
EPS = D / 20.0
INV = 1.0 / EPS
TWO_INV = 2.0 / EPS
VMEM_LIMIT = 60 * 1024 * 1024
LOG2E = 1.4426950408889634
LN2 = 0.6931471805599453
SCALE2 = TWO_INV * LOG2E
NT = (((1,), (1,)), ((), ()))
TN = (((0,), (0,)), ((), ()))


def _params(semantics):
    return pltpu.CompilerParams(dimension_semantics=semantics, vmem_limit_bytes=VMEM_LIMIT)


def _to_row(col):
    return jnp.transpose(jnp.broadcast_to(col, (col.shape[0], D)))[0:1, :]


def _to_col(row):
    return jnp.transpose(jnp.broadcast_to(row, (D, row.shape[1])))[:, 0:1]


def _row_of(v):
    return jnp.concatenate([v[k:k + 1, :] for k in range(v.shape[0])], axis=1)


def _lse_kernel(p_ref, q_ref, a_ref, b_ref, o_ref):
    i = pl.program_id(0)
    cross = lax.dot_general(p_ref[...], q_ref[...], NT, preferred_element_type=jnp.float32)
    t = _row_of(a_ref[...]) * LOG2E + SCALE2 * cross
    top = jnp.max(t, axis=1, keepdims=True)
    total = jnp.sum(jnp.exp2(t - top), axis=1, keepdims=True)
    o_ref[pl.ds(i, 1), :] = _to_row(top * LN2 + jnp.log(total)) - b_ref[pl.ds(i, 1), :]


def lse(p, q, a, b):
    rows, cols = p.shape[0], q.shape[0]
    tile = rows // 8
    return pl.pallas_call(
        _lse_kernel,
        out_shape=jax.ShapeDtypeStruct((8, tile), jnp.float32),
        grid=(8,),
        in_specs=[
            pl.BlockSpec((tile, D), lambda i: (i, 0)),
            pl.BlockSpec((cols, D), lambda i: (0, 0)),
            pl.BlockSpec((8, cols // 8), lambda i: (0, 0)),
            pl.BlockSpec((8, tile), lambda i: (0, 0)),
        ],
        out_specs=pl.BlockSpec((8, tile), lambda i: (0, 0)),
        compiler_params=_params(("arbitrary",)),
    )(p, q, a, b)


def _plan_kernel(x_ref, y_ref, u_ref, a_ref, gi_ref, pc_ref, c_ref):
    @pl.when(pl.program_id(0) == 0)
    def _():
        pc_ref[...] = jnp.zeros_like(pc_ref)
        c_ref[...] = jnp.zeros_like(c_ref)

    i = pl.program_id(0)
    x = x_ref[...]
    cross = lax.dot_general(x, y_ref[...], NT, preferred_element_type=jnp.float32)
    u = _to_col(u_ref[pl.ds(i, 1), :] * LOG2E)
    plan = jnp.exp2(u + _row_of(a_ref[...]) * LOG2E + SCALE2 * cross).astype(jnp.bfloat16)
    wide = plan.astype(jnp.float32)
    r = jnp.sum(wide, axis=1, keepdims=True)
    c_ref[...] += jnp.sum(wide, axis=0, keepdims=True)
    pulled = jnp.dot(plan, y_ref[...], preferred_element_type=jnp.float32)
    gi_ref[...] = 2.0 * (r * x.astype(jnp.float32) - pulled)
    pc_ref[...] += lax.dot_general(plan, x, TN, preferred_element_type=jnp.float32)


def plan_grads(x, y, u, a):
    rows, cols = x.shape[0], y.shape[0]
    return pl.pallas_call(
        _plan_kernel,
        out_shape=(
            jax.ShapeDtypeStruct((rows, D), jnp.float32),
            jax.ShapeDtypeStruct((cols, D), jnp.float32),
            jax.ShapeDtypeStruct((1, cols), jnp.float32),
        ),
        grid=(8,),
        in_specs=[
            pl.BlockSpec((rows // 8, D), lambda i: (i, 0)),
            pl.BlockSpec((cols, D), lambda i: (0, 0)),
            pl.BlockSpec((8, rows // 8), lambda i: (0, 0)),
            pl.BlockSpec((8, cols // 8), lambda i: (0, 0)),
        ],
        out_specs=(
            pl.BlockSpec((rows // 8, D), lambda i: (i, 0)),
            pl.BlockSpec((cols, D), lambda i: (0, 0)),
            pl.BlockSpec((1, cols), lambda i: (0, 0)),
        ),
        compiler_params=_params(("arbitrary",)),
    )(x, y, u, a)


def _plan_scatter_kernel(n_col, n_row, x_ref, y_ref, u_ref, a_ref, gi_out, gc_out,
                         gi, pc, csum, gcs, bufi, bufc, sendi, recvi, sendc, recvc):
    me_c, me_r = lax.axis_index("col"), lax.axis_index("row")
    barrier = pltpu.get_barrier_semaphore()
    for d in range(1, n_col):
        pl.semaphore_signal(barrier, inc=1, device_id=_peer("col", lax.rem(me_c + d, n_col)),
                            device_id_type=pl.DeviceIdType.MESH)
    for d in range(1, n_row):
        pl.semaphore_signal(barrier, inc=1, device_id=_peer("row", lax.rem(me_r + d, n_row)),
                            device_id_type=pl.DeviceIdType.MESH)

    def to_col_dev(k, slot):
        return pltpu.make_async_remote_copy(
            src_ref=gi.at[k], dst_ref=bufi.at[slot], send_sem=sendi.at[k], recv_sem=recvi.at[slot],
            device_id=_peer("col", k), device_id_type=pl.DeviceIdType.MESH)

    def to_row_dev(k, slot):
        return pltpu.make_async_remote_copy(
            src_ref=gcs.at[k], dst_ref=bufc.at[slot], send_sem=sendc.at[k], recv_sem=recvc.at[slot],
            device_id=_peer("row", k), device_id_type=pl.DeviceIdType.MESH)

    def each(n, me, body):
        for k in range(n):
            pl.when(me != k)(functools.partial(body, k))

    rows, cols = x_ref.shape[0], y_ref.shape[0]
    tiles = u_ref.shape[0]
    tile, m, mc = rows // tiles, rows // n_col, cols // n_row
    per = tile // m
    y = y_ref[...]
    a2 = _row_of(a_ref[...]) * LOG2E
    pc[...] = jnp.zeros_like(pc)
    csum[...] = jnp.zeros_like(csum)
    for i in range(tiles):
        x = x_ref[i * tile:(i + 1) * tile, :]
        cross = lax.dot_general(x, y, NT, preferred_element_type=jnp.float32)
        u = _to_col(u_ref[i:i + 1, :] * LOG2E)
        plan = jnp.exp2(u + a2 + SCALE2 * cross).astype(jnp.bfloat16)
        wide = plan.astype(jnp.float32)
        r = jnp.sum(wide, axis=1, keepdims=True)
        csum[...] += jnp.sum(wide, axis=0, keepdims=True)
        pulled = jnp.dot(plan, y, preferred_element_type=jnp.float32)
        g = 2.0 * (r * x.astype(jnp.float32) - pulled)
        for s in range(per):
            gi[i * per + s] = g[s * m:(s + 1) * m]
        pc[...] += lax.dot_general(plan, x, TN, preferred_element_type=jnp.float32)
        if i == 1:
            pl.semaphore_wait(barrier, n_col + n_row - 2)
        if i >= 1:
            for s in range((i - 1) * per, i * per):
                pl.when(me_c != s)(functools.partial(lambda k: to_col_dev(k, me_c).start(), s))
    for s in range((tiles - 1) * per, tiles * per):
        pl.when(me_c != s)(functools.partial(lambda k: to_col_dev(k, me_c).start(), s))
    gcv = 2.0 * (_to_col(csum[...]) * y.astype(jnp.float32) - pc[...])
    for k in range(n_row):
        gcs[k] = gcv[k * mc:(k + 1) * mc]
    each(n_row, me_r, lambda k: to_row_dev(k, me_r).start())
    each(n_col, me_c, lambda k: to_col_dev(k, me_c).wait_send())
    each(n_row, me_r, lambda k: to_row_dev(k, me_r).wait_send())
    each(n_col, me_c, lambda k: to_col_dev(k, k).wait_recv())
    each(n_row, me_r, lambda k: to_row_dev(k, k).wait_recv())
    bufi[me_c] = gi[me_c]
    bufc[me_r] = gcs[me_r]
    gi_out[...] = jnp.sum(bufi[...], axis=0)
    gc_out[...] = jnp.sum(bufc[...], axis=0)


def plan_scatter(x, y, u, a, n_col, n_row):
    rows, cols = x.shape[0], y.shape[0]
    m, mc = rows // n_col, cols // n_row
    return pl.pallas_call(
        functools.partial(_plan_scatter_kernel, n_col, n_row),
        out_shape=(jax.ShapeDtypeStruct((m, D), jnp.float32),
                   jax.ShapeDtypeStruct((mc, D), jnp.float32)),
        in_specs=[pl.BlockSpec(memory_space=pltpu.VMEM)] * 4,
        out_specs=(pl.BlockSpec(memory_space=pltpu.VMEM),) * 2,
        scratch_shapes=[
            pltpu.VMEM((n_col, m, D), jnp.float32),
            pltpu.VMEM((cols, D), jnp.float32),
            pltpu.VMEM((1, cols), jnp.float32),
            pltpu.VMEM((n_row, mc, D), jnp.float32),
            pltpu.VMEM((n_col, m, D), jnp.float32),
            pltpu.VMEM((n_row, mc, D), jnp.float32),
            pltpu.SemaphoreType.DMA((n_col,)),
            pltpu.SemaphoreType.DMA((n_col,)),
            pltpu.SemaphoreType.DMA((n_row,)),
            pltpu.SemaphoreType.DMA((n_row,)),
        ],
        compiler_params=pltpu.CompilerParams(
            collective_id=4, has_side_effects=True, vmem_limit_bytes=VMEM_LIMIT),
    )(x, y, u, a)


def _lse_combine_kernel(axis, n, p_ref, q_ref, a_ref, m_ref, s_ref, o_ref,
                        part, buf, send, recv):
    me = lax.axis_index(axis)
    barrier = pltpu.get_barrier_semaphore()
    for d in range(1, n):
        pl.semaphore_signal(barrier, inc=1, device_id=_peer(axis, lax.rem(me + d, n)),
                            device_id_type=pl.DeviceIdType.MESH)

    def out_copy(c, d):
        return pltpu.make_async_remote_copy(
            src_ref=part.at[c], dst_ref=buf.at[me, c], send_sem=send.at[c, d],
            recv_sem=recv.at[c, me], device_id=_peer(axis, lax.rem(me + d, n)),
            device_id_type=pl.DeviceIdType.MESH)

    def in_copy(c, d):
        src = lax.rem(me + n - d, n)
        return pltpu.make_async_remote_copy(
            src_ref=part.at[c], dst_ref=buf.at[src, c], send_sem=send.at[c, d],
            recv_sem=recv.at[c, src], device_id=_peer(axis, src),
            device_id_type=pl.DeviceIdType.MESH)

    def send_half(c):
        for d in range(1, n):
            out_copy(c, d).start()

    half = part.shape[1]
    tile = p_ref.shape[0] // (2 * half)
    q = q_ref[...]
    a2 = _row_of(a_ref[...]) * LOG2E

    def body(i, carry):
        start = pl.multiple_of(i * tile, tile)
        cross = lax.dot_general(p_ref[pl.ds(start, tile), :], q, NT,
                                preferred_element_type=jnp.float32)
        t = a2 + SCALE2 * cross
        top = jnp.max(t, axis=1, keepdims=True)
        total = jnp.sum(jnp.exp2(t - top), axis=1, keepdims=True)
        row = _to_row(top * LN2 + jnp.log(total)) - s_ref[pl.ds(i, 1), :] * INV
        part.at[i // half][pl.ds(i % half, 1), :] = row

        @pl.when(i == half)
        def _():
            pl.semaphore_wait(barrier, n - 1)
            send_half(0)

        return carry

    lax.fori_loop(0, 2 * half, body, 0)

    def finish(c):
        for d in range(1, n):
            out_copy(c, d).wait_send()
        for d in range(1, n):
            in_copy(c, d).wait_recv()
        buf[me, c] = part[c]
        parts = buf[:, c]
        top = jnp.max(parts, axis=0)
        total = top + jnp.log(jnp.sum(jnp.exp(parts - top[None]), axis=0))
        rows = slice(c * half, (c + 1) * half)
        o_ref[rows, :] = (EPS * (m_ref[rows, :] - total) - s_ref[rows, :]) * INV

    finish(0)
    send_half(1)
    finish(1)


def lse_combine(p, q, a, log_mass, sq, axis):
    n = lax.axis_size(axis)
    m = p.shape[0] // 8
    return pl.pallas_call(
        functools.partial(_lse_combine_kernel, axis, n),
        out_shape=jax.ShapeDtypeStruct((8, m), jnp.float32),
        in_specs=[pl.BlockSpec(memory_space=pltpu.VMEM)] * 5,
        out_specs=pl.BlockSpec(memory_space=pltpu.VMEM),
        scratch_shapes=[
            pltpu.VMEM((2, 4, m), jnp.float32),
            pltpu.VMEM((n, 2, 4, m), jnp.float32),
            pltpu.SemaphoreType.DMA((2, n)),
            pltpu.SemaphoreType.DMA((2, n)),
        ],
        compiler_params=pltpu.CompilerParams(
            collective_id=5 if axis == "col" else 6, has_side_effects=True,
            vmem_limit_bytes=VMEM_LIMIT),
    )(p, q, a, log_mass, sq)


def _first_kernel(n, x_ref, q_ref, a_ref, m_ref, o_ref, rows_out, sq_out,
                  gbuf, sqs, part, buf, send, recv, gsend, grecv):
    axis = "col"
    me = lax.axis_index(axis)
    barrier = pltpu.get_barrier_semaphore()
    for d in range(1, n):
        pl.semaphore_signal(barrier, inc=1, device_id=_peer(axis, lax.rem(me + d, n)),
                            device_id_type=pl.DeviceIdType.MESH)
    pl.semaphore_wait(barrier, n - 1)

    def gather_copy(d, slot):
        return pltpu.make_async_remote_copy(
            src_ref=x_ref, dst_ref=gbuf.at[slot], send_sem=gsend.at[d], recv_sem=grecv.at[slot],
            device_id=_peer(axis, lax.rem(me + d, n)), device_id_type=pl.DeviceIdType.MESH)

    for d in range(1, n):
        gather_copy(d, me).start()
    gbuf[me] = x_ref[...]

    def out_copy(c, d):
        return pltpu.make_async_remote_copy(
            src_ref=part.at[c], dst_ref=buf.at[me, c], send_sem=send.at[c, d],
            recv_sem=recv.at[c, me], device_id=_peer(axis, lax.rem(me + d, n)),
            device_id_type=pl.DeviceIdType.MESH)

    def in_copy(c, d):
        src = lax.rem(me + n - d, n)
        return pltpu.make_async_remote_copy(
            src_ref=part.at[c], dst_ref=buf.at[src, c], send_sem=send.at[c, d],
            recv_sem=recv.at[c, src], device_id=_peer(axis, src),
            device_id_type=pl.DeviceIdType.MESH)

    def send_half(c):
        for d in range(1, n):
            out_copy(c, d).start()

    half = part.shape[1]
    m = x_ref.shape[0]
    tile = sqs.shape[1]
    per = tile // m
    q = q_ref[...]
    a2 = _row_of(a_ref[...]) * LOG2E

    def body(i, carry):
        for s in range(per):
            slot = i * per + s

            @pl.when(slot != me)
            def _():
                d = lax.rem(me + n - slot, n)
                pltpu.make_async_remote_copy(
                    src_ref=x_ref, dst_ref=gbuf.at[slot], send_sem=gsend.at[d],
                    recv_sem=grecv.at[slot], device_id=_peer(axis, slot),
                    device_id_type=pl.DeviceIdType.MESH).wait_recv()

        p = jnp.concatenate([gbuf[i * per + s] for s in range(per)], axis=0)
        v = p.astype(jnp.float32)
        sq = _to_row(jnp.sum(v * v, axis=1, keepdims=True))
        sqs[pl.ds(i, 1), :] = sq
        cross = lax.dot_general(p, q, NT, preferred_element_type=jnp.float32)
        t = a2 + SCALE2 * cross
        top = jnp.max(t, axis=1, keepdims=True)
        total = jnp.sum(jnp.exp2(t - top), axis=1, keepdims=True)
        row = _to_row(top * LN2 + jnp.log(total)) - sq * INV
        part.at[i // half][pl.ds(i % half, 1), :] = row

        @pl.when(i == half)
        def _():
            send_half(0)

        return carry

    lax.fori_loop(0, 2 * half, body, 0)

    def finish(c):
        for d in range(1, n):
            out_copy(c, d).wait_send()
        for d in range(1, n):
            in_copy(c, d).wait_recv()
        buf[me, c] = part[c]
        parts = buf[:, c]
        top = jnp.max(parts, axis=0)
        total = top + jnp.log(jnp.sum(jnp.exp(parts - top[None]), axis=0))
        rows = slice(c * half, (c + 1) * half)
        o_ref[rows, :] = (EPS * (m_ref[rows, :] - total) - sqs[rows, :]) * INV

    finish(0)
    send_half(1)
    finish(1)
    for d in range(1, n):
        gather_copy(d, me).wait_send()
    rows_out[...] = gbuf[...]
    sq_out[...] = sqs[...]


def first_lse(x, q, a, log_mass):
    n = lax.axis_size("col")
    m = x.shape[0]
    tile = n * m // 8
    return pl.pallas_call(
        functools.partial(_first_kernel, n),
        out_shape=(jax.ShapeDtypeStruct((8, tile), jnp.float32),
                   jax.ShapeDtypeStruct((n, m, D), x.dtype),
                   jax.ShapeDtypeStruct((8, tile), jnp.float32)),
        in_specs=[pl.BlockSpec(memory_space=pltpu.VMEM)] * 4,
        out_specs=(pl.BlockSpec(memory_space=pltpu.VMEM),) * 3,
        scratch_shapes=[
            pltpu.VMEM((n, m, D), x.dtype),
            pltpu.VMEM((8, tile), jnp.float32),
            pltpu.VMEM((2, 4, tile), jnp.float32),
            pltpu.VMEM((n, 2, 4, tile), jnp.float32),
            pltpu.SemaphoreType.DMA((2, n)),
            pltpu.SemaphoreType.DMA((2, n)),
            pltpu.SemaphoreType.DMA((n,)),
            pltpu.SemaphoreType.DMA((n,)),
        ],
        compiler_params=pltpu.CompilerParams(
            collective_id=7, has_side_effects=True, vmem_limit_bytes=VMEM_LIMIT),
    )(x, q, a, log_mass)


def squares(values):
    return jnp.sum(jnp.square(values.astype(jnp.float32)), axis=1)


def _peer(axis, k):
    if axis == "col":
        return (lax.axis_index("row"), k)
    return (k, lax.axis_index("col"))


def _gather_lse_kernel(axis, n, x_ref, m_ref, q_ref, o_ref, buf, send, recv):
    me = lax.axis_index(axis)
    barrier = pltpu.get_barrier_semaphore()
    for d in range(1, n):
        pl.semaphore_signal(barrier, inc=1, device_id=_peer(axis, lax.rem(me + d, n)),
                            device_id_type=pl.DeviceIdType.MESH)
    pl.semaphore_wait(barrier, n - 1)
    copies = []
    for d in range(1, n):
        copy = pltpu.make_async_remote_copy(
            src_ref=x_ref, dst_ref=buf.at[me], send_sem=send.at[d], recv_sem=recv.at[me],
            device_id=_peer(axis, lax.rem(me + d, n)), device_id_type=pl.DeviceIdType.MESH)
        copy.start()
        copies.append(copy)
    for copy in copies:
        copy.wait_send()
    for d in range(1, n):
        src = lax.rem(me + n - d, n)
        pltpu.make_async_remote_copy(
            src_ref=x_ref, dst_ref=buf.at[src], send_sem=send.at[d], recv_sem=recv.at[src],
            device_id=_peer(axis, src), device_id_type=pl.DeviceIdType.MESH).wait_recv()
    buf[me] = x_ref[...]
    parts = buf[...]
    top = jnp.max(parts, axis=0)
    total = top + jnp.log(jnp.sum(jnp.exp(parts - top[None]), axis=0))
    o_ref[...] = (EPS * (m_ref[...] - total) - q_ref[...]) * INV


def _exchange_kernel(jobs, *refs):
    count = len(jobs)
    ins, outs = refs[:count], refs[count:2 * count]
    gathers = sum(kind == "gather" for _, _, kind in jobs)
    sqs = refs[2 * count:2 * count + gathers]
    rest = refs[2 * count + gathers:]
    bufs, sends, recvs = rest[0::3], rest[1::3], rest[2::3]
    barrier = pltpu.get_barrier_semaphore()
    for axis, n, kind in jobs:
        me = lax.axis_index(axis)
        for d in range(1, n):
            pl.semaphore_signal(barrier, inc=1, device_id=_peer(axis, lax.rem(me + d, n)),
                                device_id_type=pl.DeviceIdType.MESH)
    pl.semaphore_wait(barrier, sum(n - 1 for _, n, _ in jobs))

    def copy(job, d, peer, slot):
        axis, n, kind = jobs[job]
        src = ins[job] if kind == "gather" else ins[job].at[peer]
        return pltpu.make_async_remote_copy(
            src_ref=src, dst_ref=bufs[job].at[slot], send_sem=sends[job].at[d],
            recv_sem=recvs[job].at[slot], device_id=_peer(axis, peer),
            device_id_type=pl.DeviceIdType.MESH)

    started = []
    for job, (axis, n, kind) in enumerate(jobs):
        me = lax.axis_index(axis)
        for d in range(1, n):
            started.append(copy(job, d, lax.rem(me + d, n), me))
            started[-1].start()
    for c in started:
        c.wait_send()
    for job, (axis, n, kind) in enumerate(jobs):
        me = lax.axis_index(axis)
        for d in range(1, n):
            src = lax.rem(me + n - d, n)
            copy(job, d, src, src).wait_recv()
        if kind == "gather":
            bufs[job][me] = ins[job][...]
            outs[job][...] = bufs[job][...]
            sq = sqs[job]
            m = bufs[job].shape[1]
            per = sq.shape[1] // m
            for j in range(n):
                v = bufs[job][j].astype(jnp.float32)
                row = _to_row(jnp.sum(v * v, axis=1, keepdims=True))
                sq[j // per:j // per + 1, (j % per) * m:(j % per + 1) * m] = row
        else:
            bufs[job][me] = ins[job][me]
            outs[job][...] = jnp.sum(bufs[job][...], axis=0)


def exchange(jobs, arrays, collective_id):
    shapes, scratch = [], []
    for (axis, n, kind), x in zip(jobs, arrays):
        block = x.shape if kind == "gather" else x.shape[1:]
        shapes.append(jax.ShapeDtypeStruct((n,) + block if kind == "gather" else block, x.dtype))
        scratch += [pltpu.VMEM((n,) + block, x.dtype), pltpu.SemaphoreType.DMA((n,)),
                    pltpu.SemaphoreType.DMA((n,))]
    for (axis, n, kind), x in zip(jobs, arrays):
        if kind == "gather":
            shapes.append(jax.ShapeDtypeStruct((8, n * x.shape[0] // 8), jnp.float32))
    return pl.pallas_call(
        functools.partial(_exchange_kernel, tuple(jobs)),
        out_shape=tuple(shapes),
        in_specs=[pl.BlockSpec(memory_space=pltpu.VMEM)] * len(jobs),
        out_specs=tuple(pl.BlockSpec(memory_space=pltpu.VMEM) for _ in shapes),
        scratch_shapes=scratch,
        compiler_params=pltpu.CompilerParams(
            collective_id=collective_id, has_side_effects=True, vmem_limit_bytes=VMEM_LIMIT),
    )(*arrays)


def combine(block, axis, log_mass, sq):
    n = lax.axis_size(axis)
    return pl.pallas_call(
        functools.partial(_gather_lse_kernel, axis, n),
        out_shape=jax.ShapeDtypeStruct(block.shape, jnp.float32),
        in_specs=[pl.BlockSpec(memory_space=pltpu.VMEM)] * 3,
        out_specs=pl.BlockSpec(memory_space=pltpu.VMEM),
        scratch_shapes=[
            pltpu.VMEM((n,) + block.shape, jnp.float32),
            pltpu.SemaphoreType.DMA((n,)),
            pltpu.SemaphoreType.DMA((n,)),
        ],
        compiler_params=pltpu.CompilerParams(
            collective_id=0 if axis == "col" else 1, has_side_effects=True),
    )(block, log_mass, sq)


def local(imu, camera, imu_mass, cam_mass):
    n_col, n_row = lax.axis_size("col"), lax.axis_size("row")
    cam_rows, cols_sq = exchange([("row", n_row, "gather")], [camera[0]], 3)
    cam_rows = cam_rows.reshape(-1, D)
    log_a = jnp.log(imu_mass).reshape(8, -1)
    log_b = jnp.log(cam_mass).reshape(8, -1)

    a = -cols_sq * INV
    u, imu_rows, rows_sq = first_lse(imu, cam_rows, a, log_a)
    imu_rows = imu_rows.reshape(-1, D)
    a = lse_combine(cam_rows, imu_rows, u, log_b, cols_sq, "row")
    for step in range(1, ITERS):
        u = lse_combine(imu_rows, cam_rows, a, log_a, rows_sq, "col")
        a = lse_combine(cam_rows, imu_rows, u, log_b, cols_sq, "row")

    grad_imu, grad_cam = plan_scatter(imu_rows, cam_rows, u, a, n_col, n_row)
    return (grad_imu, grad_cam[None])


def solution(mesh):
    in_specs = (P(("row", "col"), None), P("col", "row", None), P("row"), P("col"))
    out_specs = (P(("row", "col"), None), P("col", "row", None))
    return jax.shard_map(local, mesh=mesh, in_specs=in_specs, out_specs=out_specs, check_vma=False)
```

```python
import functools

import jax
import jax.numpy as jnp
from jax import lax
from jax.experimental import pallas as pl
from jax.experimental.pallas import tpu as pltpu
from jax.sharding import PartitionSpec as P

D = 128
ITERS = 3
EPS = D / 20.0
INV = 1.0 / EPS
TWO_INV = 2.0 / EPS
VMEM_LIMIT = 60 * 1024 * 1024
LOG2E = 1.4426950408889634
LN2 = 0.6931471805599453
SCALE2 = TWO_INV * LOG2E
NT = (((1,), (1,)), ((), ()))
TN = (((0,), (0,)), ((), ()))


def _params(semantics):
    return pltpu.CompilerParams(dimension_semantics=semantics, vmem_limit_bytes=VMEM_LIMIT)


def _to_row(col):
    return jnp.transpose(jnp.broadcast_to(col, (col.shape[0], D)))[0:1, :]


def _to_col(row):
    return jnp.transpose(jnp.broadcast_to(row, (D, row.shape[1])))[:, 0:1]


def _row_of(v):
    return jnp.concatenate([v[k:k + 1, :] for k in range(v.shape[0])], axis=1)


def _lse_kernel(p_ref, q_ref, a_ref, b_ref, o_ref):
    i = pl.program_id(0)
    cross = lax.dot_general(p_ref[...], q_ref[...], NT, preferred_element_type=jnp.float32)
    t = _row_of(a_ref[...]) * LOG2E + SCALE2 * cross
    top = jnp.max(t, axis=1, keepdims=True)
    total = jnp.sum(jnp.exp2(t - top), axis=1, keepdims=True)
    o_ref[pl.ds(i, 1), :] = _to_row(top * LN2 + jnp.log(total)) - b_ref[pl.ds(i, 1), :]


def lse(p, q, a, b):
    rows, cols = p.shape[0], q.shape[0]
    tile = rows // 8
    return pl.pallas_call(
        _lse_kernel,
        out_shape=jax.ShapeDtypeStruct((8, tile), jnp.float32),
        grid=(8,),
        in_specs=[
            pl.BlockSpec((tile, D), lambda i: (i, 0)),
            pl.BlockSpec((cols, D), lambda i: (0, 0)),
            pl.BlockSpec((8, cols // 8), lambda i: (0, 0)),
            pl.BlockSpec((8, tile), lambda i: (0, 0)),
        ],
        out_specs=pl.BlockSpec((8, tile), lambda i: (0, 0)),
        compiler_params=_params(("arbitrary",)),
    )(p, q, a, b)


def _plan_kernel(x_ref, y_ref, u_ref, a_ref, gi_ref, pc_ref, c_ref):
    @pl.when(pl.program_id(0) == 0)
    def _():
        pc_ref[...] = jnp.zeros_like(pc_ref)
        c_ref[...] = jnp.zeros_like(c_ref)

    i = pl.program_id(0)
    x = x_ref[...]
    cross = lax.dot_general(x, y_ref[...], NT, preferred_element_type=jnp.float32)
    u = _to_col(u_ref[pl.ds(i, 1), :] * LOG2E)
    plan = jnp.exp2(u + _row_of(a_ref[...]) * LOG2E + SCALE2 * cross).astype(jnp.bfloat16)
    wide = plan.astype(jnp.float32)
    r = jnp.sum(wide, axis=1, keepdims=True)
    c_ref[...] += jnp.sum(wide, axis=0, keepdims=True)
    pulled = jnp.dot(plan, y_ref[...], preferred_element_type=jnp.float32)
    gi_ref[...] = 2.0 * (r * x.astype(jnp.float32) - pulled)
    pc_ref[...] += lax.dot_general(plan, x, TN, preferred_element_type=jnp.float32)


def plan_grads(x, y, u, a):
    rows, cols = x.shape[0], y.shape[0]
    return pl.pallas_call(
        _plan_kernel,
        out_shape=(
            jax.ShapeDtypeStruct((rows, D), jnp.float32),
            jax.ShapeDtypeStruct((cols, D), jnp.float32),
            jax.ShapeDtypeStruct((1, cols), jnp.float32),
        ),
        grid=(8,),
        in_specs=[
            pl.BlockSpec((rows // 8, D), lambda i: (i, 0)),
            pl.BlockSpec((cols, D), lambda i: (0, 0)),
            pl.BlockSpec((8, rows // 8), lambda i: (0, 0)),
            pl.BlockSpec((8, cols // 8), lambda i: (0, 0)),
        ],
        out_specs=(
            pl.BlockSpec((rows // 8, D), lambda i: (i, 0)),
            pl.BlockSpec((cols, D), lambda i: (0, 0)),
            pl.BlockSpec((1, cols), lambda i: (0, 0)),
        ),
        compiler_params=_params(("arbitrary",)),
    )(x, y, u, a)


def _plan_scatter_kernel(n_col, n_row, x_ref, y_ref, u_ref, a_ref, gi_out, gc_out,
                         gi, pc, csum, gcs, bufi, bufc, sendi, recvi, sendc, recvc):
    me_c, me_r = lax.axis_index("col"), lax.axis_index("row")
    barrier = pltpu.get_barrier_semaphore()
    for d in range(1, n_col):
        pl.semaphore_signal(barrier, inc=1, device_id=_peer("col", lax.rem(me_c + d, n_col)),
                            device_id_type=pl.DeviceIdType.MESH)
    for d in range(1, n_row):
        pl.semaphore_signal(barrier, inc=1, device_id=_peer("row", lax.rem(me_r + d, n_row)),
                            device_id_type=pl.DeviceIdType.MESH)

    def to_col_dev(k, slot):
        return pltpu.make_async_remote_copy(
            src_ref=gi.at[k], dst_ref=bufi.at[slot], send_sem=sendi.at[k], recv_sem=recvi.at[slot],
            device_id=_peer("col", k), device_id_type=pl.DeviceIdType.MESH)

    def to_row_dev(k, slot):
        return pltpu.make_async_remote_copy(
            src_ref=gcs.at[k], dst_ref=bufc.at[slot], send_sem=sendc.at[k], recv_sem=recvc.at[slot],
            device_id=_peer("row", k), device_id_type=pl.DeviceIdType.MESH)

    def each(n, me, body):
        for k in range(n):
            pl.when(me != k)(functools.partial(body, k))

    rows, cols = x_ref.shape[0], y_ref.shape[0]
    tiles = u_ref.shape[0]
    tile, m, mc = rows // tiles, rows // n_col, cols // n_row
    per = tile // m
    y = y_ref[...]
    a2 = _row_of(a_ref[...]) * LOG2E
    pc[...] = jnp.zeros_like(pc)
    csum[...] = jnp.zeros_like(csum)
    for i in range(tiles):
        x = x_ref[i * tile:(i + 1) * tile, :]
        cross = lax.dot_general(x, y, NT, preferred_element_type=jnp.float32)
        u = _to_col(u_ref[i:i + 1, :] * LOG2E)
        plan = jnp.exp2(u + a2 + SCALE2 * cross).astype(jnp.bfloat16)
        wide = plan.astype(jnp.float32)
        r = jnp.sum(wide, axis=1, keepdims=True)
        csum[...] += jnp.sum(wide, axis=0, keepdims=True)
        pulled = jnp.dot(plan, y, preferred_element_type=jnp.float32)
        g = 2.0 * (r * x.astype(jnp.float32) - pulled)
        for s in range(per):
            gi[i * per + s] = g[s * m:(s + 1) * m]
        pc[...] += lax.dot_general(plan, x, TN, preferred_element_type=jnp.float32)
        if i == 1:
            pl.semaphore_wait(barrier, n_col + n_row - 2)
        if i >= 1:
            for s in range((i - 1) * per, i * per):
                pl.when(me_c != s)(functools.partial(lambda k: to_col_dev(k, me_c).start(), s))
    for s in range((tiles - 1) * per, tiles * per):
        pl.when(me_c != s)(functools.partial(lambda k: to_col_dev(k, me_c).start(), s))
    gcv = 2.0 * (_to_col(csum[...]) * y.astype(jnp.float32) - pc[...])
    for k in range(n_row):
        gcs[k] = gcv[k * mc:(k + 1) * mc]
    each(n_row, me_r, lambda k: to_row_dev(k, me_r).start())
    each(n_col, me_c, lambda k: to_col_dev(k, me_c).wait_send())
    each(n_row, me_r, lambda k: to_row_dev(k, me_r).wait_send())
    each(n_col, me_c, lambda k: to_col_dev(k, k).wait_recv())
    each(n_row, me_r, lambda k: to_row_dev(k, k).wait_recv())
    bufi[me_c] = gi[me_c]
    bufc[me_r] = gcs[me_r]
    gi_out[...] = jnp.sum(bufi[...], axis=0)
    gc_out[...] = jnp.sum(bufc[...], axis=0)


def plan_scatter(x, y, u, a, n_col, n_row):
    rows, cols = x.shape[0], y.shape[0]
    m, mc = rows // n_col, cols // n_row
    return pl.pallas_call(
        functools.partial(_plan_scatter_kernel, n_col, n_row),
        out_shape=(jax.ShapeDtypeStruct((m, D), jnp.float32),
                   jax.ShapeDtypeStruct((mc, D), jnp.float32)),
        in_specs=[pl.BlockSpec(memory_space=pltpu.VMEM)] * 4,
        out_specs=(pl.BlockSpec(memory_space=pltpu.VMEM),) * 2,
        scratch_shapes=[
            pltpu.VMEM((n_col, m, D), jnp.float32),
            pltpu.VMEM((cols, D), jnp.float32),
            pltpu.VMEM((1, cols), jnp.float32),
            pltpu.VMEM((n_row, mc, D), jnp.float32),
            pltpu.VMEM((n_col, m, D), jnp.float32),
            pltpu.VMEM((n_row, mc, D), jnp.float32),
            pltpu.SemaphoreType.DMA((n_col,)),
            pltpu.SemaphoreType.DMA((n_col,)),
            pltpu.SemaphoreType.DMA((n_row,)),
            pltpu.SemaphoreType.DMA((n_row,)),
        ],
        compiler_params=pltpu.CompilerParams(
            collective_id=4, has_side_effects=True, vmem_limit_bytes=VMEM_LIMIT),
    )(x, y, u, a)


def _lse_combine_kernel(axis, n, p_ref, q_ref, a_ref, m_ref, s_ref, o_ref,
                        part, buf, send, recv):
    me = lax.axis_index(axis)
    barrier = pltpu.get_barrier_semaphore()
    for d in range(1, n):
        pl.semaphore_signal(barrier, inc=1, device_id=_peer(axis, lax.rem(me + d, n)),
                            device_id_type=pl.DeviceIdType.MESH)

    def out_copy(c, d):
        return pltpu.make_async_remote_copy(
            src_ref=part.at[c], dst_ref=buf.at[me, c], send_sem=send.at[c, d],
            recv_sem=recv.at[c, me], device_id=_peer(axis, lax.rem(me + d, n)),
            device_id_type=pl.DeviceIdType.MESH)

    def in_copy(c, d):
        src = lax.rem(me + n - d, n)
        return pltpu.make_async_remote_copy(
            src_ref=part.at[c], dst_ref=buf.at[src, c], send_sem=send.at[c, d],
            recv_sem=recv.at[c, src], device_id=_peer(axis, src),
            device_id_type=pl.DeviceIdType.MESH)

    def send_half(c):
        for d in range(1, n):
            out_copy(c, d).start()

    half = part.shape[1]
    tile = p_ref.shape[0] // (2 * half)
    q = q_ref[...]
    a2 = _row_of(a_ref[...]) * LOG2E

    def body(i, carry):
        start = pl.multiple_of(i * tile, tile)
        cross = lax.dot_general(p_ref[pl.ds(start, tile), :], q, NT,
                                preferred_element_type=jnp.float32)
        t = a2 + SCALE2 * cross
        top = jnp.max(t, axis=1, keepdims=True)
        total = jnp.sum(jnp.exp2(t - top), axis=1, keepdims=True)
        row = _to_row(top * LN2 + jnp.log(total)) - s_ref[pl.ds(i, 1), :] * INV
        part.at[i // half][pl.ds(i % half, 1), :] = row

        @pl.when(i == half)
        def _():
            pl.semaphore_wait(barrier, n - 1)
            send_half(0)

        return carry

    lax.fori_loop(0, 2 * half, body, 0)

    def finish(c):
        for d in range(1, n):
            out_copy(c, d).wait_send()
        for d in range(1, n):
            in_copy(c, d).wait_recv()
        buf[me, c] = part[c]
        parts = buf[:, c]
        top = jnp.max(parts, axis=0)
        total = top + jnp.log(jnp.sum(jnp.exp(parts - top[None]), axis=0))
        rows = slice(c * half, (c + 1) * half)
        o_ref[rows, :] = (EPS * (jnp.log(m_ref[rows, :]) - total) - s_ref[rows, :]) * INV

    finish(0)
    send_half(1)
    finish(1)


def lse_combine(p, q, a, mass, sq, axis):
    n = lax.axis_size(axis)
    m = p.shape[0] // 8
    return pl.pallas_call(
        functools.partial(_lse_combine_kernel, axis, n),
        out_shape=jax.ShapeDtypeStruct((8, m), jnp.float32),
        in_specs=[pl.BlockSpec(memory_space=pltpu.VMEM)] * 5,
        out_specs=pl.BlockSpec(memory_space=pltpu.VMEM),
        scratch_shapes=[
            pltpu.VMEM((2, 4, m), jnp.float32),
            pltpu.VMEM((n, 2, 4, m), jnp.float32),
            pltpu.SemaphoreType.DMA((2, n)),
            pltpu.SemaphoreType.DMA((2, n)),
        ],
        compiler_params=pltpu.CompilerParams(
            collective_id=5 if axis == "col" else 6, has_side_effects=True,
            vmem_limit_bytes=VMEM_LIMIT),
    )(p, q, a, mass, sq)


def squares(values):
    return jnp.sum(jnp.square(values.astype(jnp.float32)), axis=1)


def _peer(axis, k):
    if axis == "col":
        return (lax.axis_index("row"), k)
    return (k, lax.axis_index("col"))


def _gather_lse_kernel(axis, n, x_ref, m_ref, q_ref, o_ref, buf, send, recv):
    me = lax.axis_index(axis)
    barrier = pltpu.get_barrier_semaphore()
    for d in range(1, n):
        pl.semaphore_signal(barrier, inc=1, device_id=_peer(axis, lax.rem(me + d, n)),
                            device_id_type=pl.DeviceIdType.MESH)
    pl.semaphore_wait(barrier, n - 1)
    copies = []
    for d in range(1, n):
        copy = pltpu.make_async_remote_copy(
            src_ref=x_ref, dst_ref=buf.at[me], send_sem=send.at[d], recv_sem=recv.at[me],
            device_id=_peer(axis, lax.rem(me + d, n)), device_id_type=pl.DeviceIdType.MESH)
        copy.start()
        copies.append(copy)
    for copy in copies:
        copy.wait_send()
    for d in range(1, n):
        src = lax.rem(me + n - d, n)
        pltpu.make_async_remote_copy(
            src_ref=x_ref, dst_ref=buf.at[src], send_sem=send.at[d], recv_sem=recv.at[src],
            device_id=_peer(axis, src), device_id_type=pl.DeviceIdType.MESH).wait_recv()
    buf[me] = x_ref[...]
    parts = buf[...]
    top = jnp.max(parts, axis=0)
    total = top + jnp.log(jnp.sum(jnp.exp(parts - top[None]), axis=0))
    o_ref[...] = (EPS * (m_ref[...] - total) - q_ref[...]) * INV


def _exchange_kernel(jobs, *refs):
    count = len(jobs)
    ins, outs = refs[:count], refs[count:2 * count]
    gathers = sum(kind == "gather" for _, _, kind in jobs)
    sqs = refs[2 * count:2 * count + gathers]
    rest = refs[2 * count + gathers:]
    bufs, sends, recvs = rest[0::3], rest[1::3], rest[2::3]
    barrier = pltpu.get_barrier_semaphore()
    for axis, n, kind in jobs:
        me = lax.axis_index(axis)
        for d in range(1, n):
            pl.semaphore_signal(barrier, inc=1, device_id=_peer(axis, lax.rem(me + d, n)),
                                device_id_type=pl.DeviceIdType.MESH)
    pl.semaphore_wait(barrier, sum(n - 1 for _, n, _ in jobs))

    def copy(job, d, peer, slot):
        axis, n, kind = jobs[job]
        src = ins[job] if kind == "gather" else ins[job].at[peer]
        return pltpu.make_async_remote_copy(
            src_ref=src, dst_ref=bufs[job].at[slot], send_sem=sends[job].at[d],
            recv_sem=recvs[job].at[slot], device_id=_peer(axis, peer),
            device_id_type=pl.DeviceIdType.MESH)

    started = []
    for job, (axis, n, kind) in enumerate(jobs):
        me = lax.axis_index(axis)
        for d in range(1, n):
            started.append(copy(job, d, lax.rem(me + d, n), me))
            started[-1].start()
    for c in started:
        c.wait_send()
    for job, (axis, n, kind) in enumerate(jobs):
        me = lax.axis_index(axis)
        for d in range(1, n):
            src = lax.rem(me + n - d, n)
            copy(job, d, src, src).wait_recv()
        if kind == "gather":
            bufs[job][me] = ins[job][...]
            outs[job][...] = bufs[job][...]
            sq = sqs[job]
            m = bufs[job].shape[1]
            per = sq.shape[1] // m
            for j in range(n):
                v = bufs[job][j].astype(jnp.float32)
                row = _to_row(jnp.sum(v * v, axis=1, keepdims=True))
                sq[j // per:j // per + 1, (j % per) * m:(j % per + 1) * m] = row
        else:
            bufs[job][me] = ins[job][me]
            outs[job][...] = jnp.sum(bufs[job][...], axis=0)


def exchange(jobs, arrays, collective_id):
    shapes, scratch = [], []
    for (axis, n, kind), x in zip(jobs, arrays):
        block = x.shape if kind == "gather" else x.shape[1:]
        shapes.append(jax.ShapeDtypeStruct((n,) + block if kind == "gather" else block, x.dtype))
        scratch += [pltpu.VMEM((n,) + block, x.dtype), pltpu.SemaphoreType.DMA((n,)),
                    pltpu.SemaphoreType.DMA((n,))]
    for (axis, n, kind), x in zip(jobs, arrays):
        if kind == "gather":
            shapes.append(jax.ShapeDtypeStruct((8, n * x.shape[0] // 8), jnp.float32))
    return pl.pallas_call(
        functools.partial(_exchange_kernel, tuple(jobs)),
        out_shape=tuple(shapes),
        in_specs=[pl.BlockSpec(memory_space=pltpu.VMEM)] * len(jobs),
        out_specs=tuple(pl.BlockSpec(memory_space=pltpu.VMEM) for _ in shapes),
        scratch_shapes=scratch,
        compiler_params=pltpu.CompilerParams(
            collective_id=collective_id, has_side_effects=True, vmem_limit_bytes=VMEM_LIMIT),
    )(*arrays)


def combine(block, axis, log_mass, sq):
    n = lax.axis_size(axis)
    return pl.pallas_call(
        functools.partial(_gather_lse_kernel, axis, n),
        out_shape=jax.ShapeDtypeStruct(block.shape, jnp.float32),
        in_specs=[pl.BlockSpec(memory_space=pltpu.VMEM)] * 3,
        out_specs=pl.BlockSpec(memory_space=pltpu.VMEM),
        scratch_shapes=[
            pltpu.VMEM((n,) + block.shape, jnp.float32),
            pltpu.SemaphoreType.DMA((n,)),
            pltpu.SemaphoreType.DMA((n,)),
        ],
        compiler_params=pltpu.CompilerParams(
            collective_id=0 if axis == "col" else 1, has_side_effects=True),
    )(block, log_mass, sq)


def local(imu, camera, imu_mass, cam_mass):
    n_col, n_row = lax.axis_size("col"), lax.axis_size("row")
    imu_rows, cam_rows, rows_sq, cols_sq = exchange(
        [("col", n_col, "gather"), ("row", n_row, "gather")], [imu, camera[0]], 3)
    imu_rows = imu_rows.reshape(-1, D)
    cam_rows = cam_rows.reshape(-1, D)
    log_a = imu_mass.reshape(8, -1)
    log_b = cam_mass.reshape(8, -1)

    a = -cols_sq * INV
    for step in range(ITERS):
        u = lse_combine(imu_rows, cam_rows, a, log_a, rows_sq, "col")
        a = lse_combine(cam_rows, imu_rows, u, log_b, cols_sq, "row")

    grad_imu, grad_cam = plan_scatter(imu_rows, cam_rows, u, a, n_col, n_row)
    return (grad_imu, grad_cam[None])


def solution(mesh):
    in_specs = (P(("row", "col"), None), P("col", "row", None), P("row"), P("col"))
    out_specs = (P(("row", "col"), None), P("col", "row", None))
    return jax.shard_map(local, mesh=mesh, in_specs=in_specs, out_specs=out_specs, check_vma=False)
```

```python
import functools

import jax
import jax.numpy as jnp
from jax import lax
from jax.experimental import pallas as pl
from jax.experimental.pallas import tpu as pltpu
from jax.sharding import PartitionSpec as P

D = 128
ITERS = 3
EPS = D / 20.0
INV = 1.0 / EPS
TWO_INV = 2.0 / EPS
VMEM_LIMIT = 60 * 1024 * 1024
LOG2E = 1.4426950408889634
LN2 = 0.6931471805599453
SCALE2 = TWO_INV * LOG2E
NT = (((1,), (1,)), ((), ()))
TN = (((0,), (0,)), ((), ()))


def _params(semantics):
    return pltpu.CompilerParams(dimension_semantics=semantics, vmem_limit_bytes=VMEM_LIMIT)


def _to_row(col):
    return jnp.transpose(jnp.broadcast_to(col, (col.shape[0], D)))[0:1, :]


def _to_col(row):
    return jnp.transpose(jnp.broadcast_to(row, (D, row.shape[1])))[:, 0:1]


def _row_of(v):
    return jnp.concatenate([v[k:k + 1, :] for k in range(v.shape[0])], axis=1)


def _lse_kernel(p_ref, q_ref, a_ref, b_ref, o_ref):
    i = pl.program_id(0)
    cross = lax.dot_general(p_ref[...], q_ref[...], NT, preferred_element_type=jnp.float32)
    t = _row_of(a_ref[...]) * LOG2E + SCALE2 * cross
    top = jnp.max(t, axis=1, keepdims=True)
    total = jnp.sum(jnp.exp2(t - top), axis=1, keepdims=True)
    o_ref[pl.ds(i, 1), :] = _to_row(top * LN2 + jnp.log(total)) - b_ref[pl.ds(i, 1), :]


def lse(p, q, a, b):
    rows, cols = p.shape[0], q.shape[0]
    tile = rows // 8
    return pl.pallas_call(
        _lse_kernel,
        out_shape=jax.ShapeDtypeStruct((8, tile), jnp.float32),
        grid=(8,),
        in_specs=[
            pl.BlockSpec((tile, D), lambda i: (i, 0)),
            pl.BlockSpec((cols, D), lambda i: (0, 0)),
            pl.BlockSpec((8, cols // 8), lambda i: (0, 0)),
            pl.BlockSpec((8, tile), lambda i: (0, 0)),
        ],
        out_specs=pl.BlockSpec((8, tile), lambda i: (0, 0)),
        compiler_params=_params(("arbitrary",)),
    )(p, q, a, b)


def _plan_kernel(x_ref, y_ref, u_ref, a_ref, gi_ref, pc_ref, c_ref):
    @pl.when(pl.program_id(0) == 0)
    def _():
        pc_ref[...] = jnp.zeros_like(pc_ref)
        c_ref[...] = jnp.zeros_like(c_ref)

    i = pl.program_id(0)
    x = x_ref[...]
    cross = lax.dot_general(x, y_ref[...], NT, preferred_element_type=jnp.float32)
    u = _to_col(u_ref[pl.ds(i, 1), :] * LOG2E)
    plan = jnp.exp2(u + _row_of(a_ref[...]) * LOG2E + SCALE2 * cross).astype(jnp.bfloat16)
    wide = plan.astype(jnp.float32)
    r = jnp.sum(wide, axis=1, keepdims=True)
    c_ref[...] += jnp.sum(wide, axis=0, keepdims=True)
    pulled = jnp.dot(plan, y_ref[...], preferred_element_type=jnp.float32)
    gi_ref[...] = 2.0 * (r * x.astype(jnp.float32) - pulled)
    pc_ref[...] += lax.dot_general(plan, x, TN, preferred_element_type=jnp.float32)


def plan_grads(x, y, u, a):
    rows, cols = x.shape[0], y.shape[0]
    return pl.pallas_call(
        _plan_kernel,
        out_shape=(
            jax.ShapeDtypeStruct((rows, D), jnp.float32),
            jax.ShapeDtypeStruct((cols, D), jnp.float32),
            jax.ShapeDtypeStruct((1, cols), jnp.float32),
        ),
        grid=(8,),
        in_specs=[
            pl.BlockSpec((rows // 8, D), lambda i: (i, 0)),
            pl.BlockSpec((cols, D), lambda i: (0, 0)),
            pl.BlockSpec((8, rows // 8), lambda i: (0, 0)),
            pl.BlockSpec((8, cols // 8), lambda i: (0, 0)),
        ],
        out_specs=(
            pl.BlockSpec((rows // 8, D), lambda i: (i, 0)),
            pl.BlockSpec((cols, D), lambda i: (0, 0)),
            pl.BlockSpec((1, cols), lambda i: (0, 0)),
        ),
        compiler_params=_params(("arbitrary",)),
    )(x, y, u, a)


def _plan_scatter_kernel(n_col, n_row, x_ref, y_ref, u_ref, a_ref, gi_out, gc_out,
                         gi, pc, csum, gcs, bufi, bufc, sendi, recvi, sendc, recvc):
    me_c, me_r = lax.axis_index("col"), lax.axis_index("row")
    barrier = pltpu.get_barrier_semaphore()
    for d in range(1, n_col):
        pl.semaphore_signal(barrier, inc=1, device_id=_peer("col", lax.rem(me_c + d, n_col)),
                            device_id_type=pl.DeviceIdType.MESH)
    for d in range(1, n_row):
        pl.semaphore_signal(barrier, inc=1, device_id=_peer("row", lax.rem(me_r + d, n_row)),
                            device_id_type=pl.DeviceIdType.MESH)

    def to_col_dev(k, slot):
        return pltpu.make_async_remote_copy(
            src_ref=gi.at[k], dst_ref=bufi.at[slot], send_sem=sendi.at[k], recv_sem=recvi.at[slot],
            device_id=_peer("col", k), device_id_type=pl.DeviceIdType.MESH)

    def to_row_dev(k, slot):
        return pltpu.make_async_remote_copy(
            src_ref=gcs.at[k], dst_ref=bufc.at[slot], send_sem=sendc.at[k], recv_sem=recvc.at[slot],
            device_id=_peer("row", k), device_id_type=pl.DeviceIdType.MESH)

    def each(n, me, body):
        for k in range(n):
            pl.when(me != k)(functools.partial(body, k))

    rows, cols = x_ref.shape[0], y_ref.shape[0]
    tiles = u_ref.shape[0]
    tile, m, mc = rows // tiles, rows // n_col, cols // n_row
    per = tile // m
    y = y_ref[...]
    a2 = _row_of(a_ref[...]) * LOG2E
    pc[...] = jnp.zeros_like(pc)
    csum[...] = jnp.zeros_like(csum)
    for i in range(tiles):
        x = x_ref[i * tile:(i + 1) * tile, :]
        cross = lax.dot_general(x, y, NT, preferred_element_type=jnp.float32)
        u = _to_col(u_ref[i:i + 1, :] * LOG2E)
        plan = jnp.exp2(u + a2 + SCALE2 * cross).astype(jnp.bfloat16)
        wide = plan.astype(jnp.float32)
        r = jnp.sum(wide, axis=1, keepdims=True)
        csum[...] += jnp.sum(wide, axis=0, keepdims=True)
        pulled = jnp.dot(plan, y, preferred_element_type=jnp.float32)
        g = 2.0 * (r * x.astype(jnp.float32) - pulled)
        for s in range(per):
            gi[i * per + s] = g[s * m:(s + 1) * m]
        pc[...] += lax.dot_general(plan, x, TN, preferred_element_type=jnp.float32)
        if i == 1:
            pl.semaphore_wait(barrier, n_col + n_row - 2)
        if i >= 1:
            for s in range((i - 1) * per, i * per):
                pl.when(me_c != s)(functools.partial(lambda k: to_col_dev(k, me_c).start(), s))
    for s in range((tiles - 1) * per, tiles * per):
        pl.when(me_c != s)(functools.partial(lambda k: to_col_dev(k, me_c).start(), s))
    gcv = 2.0 * (_to_col(csum[...]) * y.astype(jnp.float32) - pc[...])
    for k in range(n_row):
        gcs[k] = gcv[k * mc:(k + 1) * mc]
    each(n_row, me_r, lambda k: to_row_dev(k, me_r).start())
    each(n_col, me_c, lambda k: to_col_dev(k, me_c).wait_send())
    each(n_row, me_r, lambda k: to_row_dev(k, me_r).wait_send())
    each(n_col, me_c, lambda k: to_col_dev(k, k).wait_recv())
    each(n_row, me_r, lambda k: to_row_dev(k, k).wait_recv())
    bufi[me_c] = gi[me_c]
    bufc[me_r] = gcs[me_r]
    gi_out[...] = jnp.sum(bufi[...], axis=0)
    gc_out[...] = jnp.sum(bufc[...], axis=0)


def plan_scatter(x, y, u, a, n_col, n_row):
    rows, cols = x.shape[0], y.shape[0]
    m, mc = rows // n_col, cols // n_row
    return pl.pallas_call(
        functools.partial(_plan_scatter_kernel, n_col, n_row),
        out_shape=(jax.ShapeDtypeStruct((m, D), jnp.float32),
                   jax.ShapeDtypeStruct((mc, D), jnp.float32)),
        in_specs=[pl.BlockSpec(memory_space=pltpu.VMEM)] * 4,
        out_specs=(pl.BlockSpec(memory_space=pltpu.VMEM),) * 2,
        scratch_shapes=[
            pltpu.VMEM((n_col, m, D), jnp.float32),
            pltpu.VMEM((cols, D), jnp.float32),
            pltpu.VMEM((1, cols), jnp.float32),
            pltpu.VMEM((n_row, mc, D), jnp.float32),
            pltpu.VMEM((n_col, m, D), jnp.float32),
            pltpu.VMEM((n_row, mc, D), jnp.float32),
            pltpu.SemaphoreType.DMA((n_col,)),
            pltpu.SemaphoreType.DMA((n_col,)),
            pltpu.SemaphoreType.DMA((n_row,)),
            pltpu.SemaphoreType.DMA((n_row,)),
        ],
        compiler_params=pltpu.CompilerParams(
            collective_id=4, has_side_effects=True, vmem_limit_bytes=VMEM_LIMIT),
    )(x, y, u, a)


def _lse_combine_kernel(axis, n, p_ref, q_ref, a_ref, m_ref, s_ref, o_ref,
                        part, buf, send, recv):
    me = lax.axis_index(axis)
    barrier = pltpu.get_barrier_semaphore()
    for d in range(1, n):
        pl.semaphore_signal(barrier, inc=1, device_id=_peer(axis, lax.rem(me + d, n)),
                            device_id_type=pl.DeviceIdType.MESH)

    def out_copy(c, d):
        return pltpu.make_async_remote_copy(
            src_ref=part.at[c], dst_ref=buf.at[me, c], send_sem=send.at[c, d],
            recv_sem=recv.at[c, me], device_id=_peer(axis, lax.rem(me + d, n)),
            device_id_type=pl.DeviceIdType.MESH)

    def in_copy(c, d):
        src = lax.rem(me + n - d, n)
        return pltpu.make_async_remote_copy(
            src_ref=part.at[c], dst_ref=buf.at[src, c], send_sem=send.at[c, d],
            recv_sem=recv.at[c, src], device_id=_peer(axis, src),
            device_id_type=pl.DeviceIdType.MESH)

    def send_half(c):
        for d in range(1, n):
            out_copy(c, d).start()

    half = part.shape[1]
    tile = p_ref.shape[0] // (2 * half)
    cq = q_ref.shape[0]
    wide = jnp.transpose(jnp.broadcast_to(_row_of(a_ref[...]) * (EPS / 2.0), (D, cq)))
    hi = wide.astype(jnp.bfloat16)
    rest = wide - hi.astype(jnp.float32)
    mid = rest.astype(jnp.bfloat16)
    low = (rest - mid.astype(jnp.float32)).astype(jnp.bfloat16)
    lane = lax.broadcasted_iota(jnp.int32, (cq, D), 1)
    zero = jnp.zeros_like(hi)
    extra = jnp.where(lane == 0, hi, jnp.where(lane == 1, mid, jnp.where(lane == 2, low, zero)))
    q = jnp.concatenate([q_ref[...], extra], axis=1)
    ones = jnp.where(lax.broadcasted_iota(jnp.int32, (tile, D), 1) < 3, 1.0, 0.0).astype(jnp.bfloat16)

    def body(i, carry):
        start = pl.multiple_of(i * tile, tile)
        p = jnp.concatenate([p_ref[pl.ds(start, tile), :], ones], axis=1)
        shifted = lax.dot_general(p, q, NT, preferred_element_type=jnp.float32)
        top = jnp.max(shifted, axis=1, keepdims=True)
        total = jnp.sum(jnp.exp2((shifted - top) * SCALE2), axis=1, keepdims=True)
        row = _to_row(top * TWO_INV + jnp.log(total)) - s_ref[pl.ds(i, 1), :] * INV
        part.at[i // half][pl.ds(i % half, 1), :] = row

        @pl.when(i == half)
        def _():
            pl.semaphore_wait(barrier, n - 1)
            send_half(0)

        return carry

    lax.fori_loop(0, 2 * half, body, 0)

    def finish(c):
        for d in range(1, n):
            out_copy(c, d).wait_send()
        for d in range(1, n):
            in_copy(c, d).wait_recv()
        buf[me, c] = part[c]
        parts = buf[:, c]
        top = jnp.max(parts, axis=0)
        total = top + jnp.log(jnp.sum(jnp.exp(parts - top[None]), axis=0))
        rows = slice(c * half, (c + 1) * half)
        o_ref[rows, :] = (EPS * (jnp.log(m_ref[rows, :]) - total) - s_ref[rows, :]) * INV

    finish(0)
    send_half(1)
    finish(1)


def lse_combine(p, q, a, mass, sq, axis):
    n = lax.axis_size(axis)
    m = p.shape[0] // 8
    return pl.pallas_call(
        functools.partial(_lse_combine_kernel, axis, n),
        out_shape=jax.ShapeDtypeStruct((8, m), jnp.float32),
        in_specs=[pl.BlockSpec(memory_space=pltpu.VMEM)] * 5,
        out_specs=pl.BlockSpec(memory_space=pltpu.VMEM),
        scratch_shapes=[
            pltpu.VMEM((2, 4, m), jnp.float32),
            pltpu.VMEM((n, 2, 4, m), jnp.float32),
            pltpu.SemaphoreType.DMA((2, n)),
            pltpu.SemaphoreType.DMA((2, n)),
        ],
        compiler_params=pltpu.CompilerParams(
            collective_id=5 if axis == "col" else 6, has_side_effects=True,
            vmem_limit_bytes=VMEM_LIMIT),
    )(p, q, a, mass, sq)


def squares(values):
    return jnp.sum(jnp.square(values.astype(jnp.float32)), axis=1)


def _peer(axis, k):
    if axis == "col":
        return (lax.axis_index("row"), k)
    return (k, lax.axis_index("col"))


def _gather_lse_kernel(axis, n, x_ref, m_ref, q_ref, o_ref, buf, send, recv):
    me = lax.axis_index(axis)
    barrier = pltpu.get_barrier_semaphore()
    for d in range(1, n):
        pl.semaphore_signal(barrier, inc=1, device_id=_peer(axis, lax.rem(me + d, n)),
                            device_id_type=pl.DeviceIdType.MESH)
    pl.semaphore_wait(barrier, n - 1)
    copies = []
    for d in range(1, n):
        copy = pltpu.make_async_remote_copy(
            src_ref=x_ref, dst_ref=buf.at[me], send_sem=send.at[d], recv_sem=recv.at[me],
            device_id=_peer(axis, lax.rem(me + d, n)), device_id_type=pl.DeviceIdType.MESH)
        copy.start()
        copies.append(copy)
    for copy in copies:
        copy.wait_send()
    for d in range(1, n):
        src = lax.rem(me + n - d, n)
        pltpu.make_async_remote_copy(
            src_ref=x_ref, dst_ref=buf.at[src], send_sem=send.at[d], recv_sem=recv.at[src],
            device_id=_peer(axis, src), device_id_type=pl.DeviceIdType.MESH).wait_recv()
    buf[me] = x_ref[...]
    parts = buf[...]
    top = jnp.max(parts, axis=0)
    total = top + jnp.log(jnp.sum(jnp.exp(parts - top[None]), axis=0))
    o_ref[...] = (EPS * (m_ref[...] - total) - q_ref[...]) * INV


def _exchange_kernel(jobs, *refs):
    count = len(jobs)
    ins, outs = refs[:count], refs[count:2 * count]
    gathers = sum(kind == "gather" for _, _, kind in jobs)
    sqs = refs[2 * count:2 * count + gathers]
    rest = refs[2 * count + gathers:]
    bufs, sends, recvs = rest[0::3], rest[1::3], rest[2::3]
    barrier = pltpu.get_barrier_semaphore()
    for axis, n, kind in jobs:
        me = lax.axis_index(axis)
        for d in range(1, n):
            pl.semaphore_signal(barrier, inc=1, device_id=_peer(axis, lax.rem(me + d, n)),
                                device_id_type=pl.DeviceIdType.MESH)
    pl.semaphore_wait(barrier, sum(n - 1 for _, n, _ in jobs))

    def copy(job, d, peer, slot):
        axis, n, kind = jobs[job]
        src = ins[job] if kind == "gather" else ins[job].at[peer]
        return pltpu.make_async_remote_copy(
            src_ref=src, dst_ref=bufs[job].at[slot], send_sem=sends[job].at[d],
            recv_sem=recvs[job].at[slot], device_id=_peer(axis, peer),
            device_id_type=pl.DeviceIdType.MESH)

    started = []
    for job, (axis, n, kind) in enumerate(jobs):
        me = lax.axis_index(axis)
        for d in range(1, n):
            started.append(copy(job, d, lax.rem(me + d, n), me))
            started[-1].start()
    for c in started:
        c.wait_send()
    for job, (axis, n, kind) in enumerate(jobs):
        me = lax.axis_index(axis)
        for d in range(1, n):
            src = lax.rem(me + n - d, n)
            copy(job, d, src, src).wait_recv()
        if kind == "gather":
            bufs[job][me] = ins[job][...]
            outs[job][...] = bufs[job][...]
            sq = sqs[job]
            m = bufs[job].shape[1]
            per = sq.shape[1] // m
            for j in range(n):
                v = bufs[job][j].astype(jnp.float32)
                row = _to_row(jnp.sum(v * v, axis=1, keepdims=True))
                sq[j // per:j // per + 1, (j % per) * m:(j % per + 1) * m] = row
        else:
            bufs[job][me] = ins[job][me]
            outs[job][...] = jnp.sum(bufs[job][...], axis=0)


def exchange(jobs, arrays, collective_id):
    shapes, scratch = [], []
    for (axis, n, kind), x in zip(jobs, arrays):
        block = x.shape if kind == "gather" else x.shape[1:]
        shapes.append(jax.ShapeDtypeStruct((n,) + block if kind == "gather" else block, x.dtype))
        scratch += [pltpu.VMEM((n,) + block, x.dtype), pltpu.SemaphoreType.DMA((n,)),
                    pltpu.SemaphoreType.DMA((n,))]
    for (axis, n, kind), x in zip(jobs, arrays):
        if kind == "gather":
            shapes.append(jax.ShapeDtypeStruct((8, n * x.shape[0] // 8), jnp.float32))
    return pl.pallas_call(
        functools.partial(_exchange_kernel, tuple(jobs)),
        out_shape=tuple(shapes),
        in_specs=[pl.BlockSpec(memory_space=pltpu.VMEM)] * len(jobs),
        out_specs=tuple(pl.BlockSpec(memory_space=pltpu.VMEM) for _ in shapes),
        scratch_shapes=scratch,
        compiler_params=pltpu.CompilerParams(
            collective_id=collective_id, has_side_effects=True, vmem_limit_bytes=VMEM_LIMIT),
    )(*arrays)


def combine(block, axis, log_mass, sq):
    n = lax.axis_size(axis)
    return pl.pallas_call(
        functools.partial(_gather_lse_kernel, axis, n),
        out_shape=jax.ShapeDtypeStruct(block.shape, jnp.float32),
        in_specs=[pl.BlockSpec(memory_space=pltpu.VMEM)] * 3,
        out_specs=pl.BlockSpec(memory_space=pltpu.VMEM),
        scratch_shapes=[
            pltpu.VMEM((n,) + block.shape, jnp.float32),
            pltpu.SemaphoreType.DMA((n,)),
            pltpu.SemaphoreType.DMA((n,)),
        ],
        compiler_params=pltpu.CompilerParams(
            collective_id=0 if axis == "col" else 1, has_side_effects=True),
    )(block, log_mass, sq)


def local(imu, camera, imu_mass, cam_mass):
    n_col, n_row = lax.axis_size("col"), lax.axis_size("row")
    imu_rows, cam_rows, rows_sq, cols_sq = exchange(
        [("col", n_col, "gather"), ("row", n_row, "gather")], [imu, camera[0]], 3)
    imu_rows = imu_rows.reshape(-1, D)
    cam_rows = cam_rows.reshape(-1, D)
    log_a = imu_mass.reshape(8, -1)
    log_b = cam_mass.reshape(8, -1)

    a = -cols_sq * INV
    for step in range(ITERS):
        u = lse_combine(imu_rows, cam_rows, a, log_a, rows_sq, "col")
        a = lse_combine(cam_rows, imu_rows, u, log_b, cols_sq, "row")

    grad_imu, grad_cam = plan_scatter(imu_rows, cam_rows, u, a, n_col, n_row)
    return (grad_imu, grad_cam[None])


def solution(mesh):
    in_specs = (P(("row", "col"), None), P("col", "row", None), P("row"), P("col"))
    out_specs = (P(("row", "col"), None), P("col", "row", None))
    return jax.shard_map(local, mesh=mesh, in_specs=in_specs, out_specs=out_specs, check_vma=False)
```

```python
import functools

import jax
import jax.numpy as jnp
from jax import lax
from jax.experimental import pallas as pl
from jax.experimental.pallas import tpu as pltpu
from jax.sharding import PartitionSpec as P

D = 128
ITERS = 3
EPS = D / 20.0
INV = 1.0 / EPS
TWO_INV = 2.0 / EPS
VMEM_LIMIT = 60 * 1024 * 1024
LOG2E = 1.4426950408889634
LN2 = 0.6931471805599453
SCALE2 = TWO_INV * LOG2E
NT = (((1,), (1,)), ((), ()))
TN = (((0,), (0,)), ((), ()))


def _params(semantics):
    return pltpu.CompilerParams(dimension_semantics=semantics, vmem_limit_bytes=VMEM_LIMIT)


def _to_row(col):
    return jnp.transpose(jnp.broadcast_to(col, (col.shape[0], D)))[0:1, :]


def _to_col(row):
    return jnp.transpose(jnp.broadcast_to(row, (D, row.shape[1])))[:, 0:1]


def _row_of(v):
    return jnp.concatenate([v[k:k + 1, :] for k in range(v.shape[0])], axis=1)


def _lse_kernel(p_ref, q_ref, a_ref, b_ref, o_ref):
    i = pl.program_id(0)
    cross = lax.dot_general(p_ref[...], q_ref[...], NT, preferred_element_type=jnp.float32)
    t = _row_of(a_ref[...]) * LOG2E + SCALE2 * cross
    top = jnp.max(t, axis=1, keepdims=True)
    total = jnp.sum(jnp.exp2(t - top), axis=1, keepdims=True)
    o_ref[pl.ds(i, 1), :] = _to_row(top * LN2 + jnp.log(total)) - b_ref[pl.ds(i, 1), :]


def lse(p, q, a, b):
    rows, cols = p.shape[0], q.shape[0]
    tile = rows // 8
    return pl.pallas_call(
        _lse_kernel,
        out_shape=jax.ShapeDtypeStruct((8, tile), jnp.float32),
        grid=(8,),
        in_specs=[
            pl.BlockSpec((tile, D), lambda i: (i, 0)),
            pl.BlockSpec((cols, D), lambda i: (0, 0)),
            pl.BlockSpec((8, cols // 8), lambda i: (0, 0)),
            pl.BlockSpec((8, tile), lambda i: (0, 0)),
        ],
        out_specs=pl.BlockSpec((8, tile), lambda i: (0, 0)),
        compiler_params=_params(("arbitrary",)),
    )(p, q, a, b)


def _plan_kernel(x_ref, y_ref, u_ref, a_ref, gi_ref, pc_ref, c_ref):
    @pl.when(pl.program_id(0) == 0)
    def _():
        pc_ref[...] = jnp.zeros_like(pc_ref)
        c_ref[...] = jnp.zeros_like(c_ref)

    i = pl.program_id(0)
    x = x_ref[...]
    cross = lax.dot_general(x, y_ref[...], NT, preferred_element_type=jnp.float32)
    u = _to_col(u_ref[pl.ds(i, 1), :] * LOG2E)
    plan = jnp.exp2(u + _row_of(a_ref[...]) * LOG2E + SCALE2 * cross).astype(jnp.bfloat16)
    wide = plan.astype(jnp.float32)
    r = jnp.sum(wide, axis=1, keepdims=True)
    c_ref[...] += jnp.sum(wide, axis=0, keepdims=True)
    pulled = jnp.dot(plan, y_ref[...], preferred_element_type=jnp.float32)
    gi_ref[...] = 2.0 * (r * x.astype(jnp.float32) - pulled)
    pc_ref[...] += lax.dot_general(plan, x, TN, preferred_element_type=jnp.float32)


def plan_grads(x, y, u, a):
    rows, cols = x.shape[0], y.shape[0]
    return pl.pallas_call(
        _plan_kernel,
        out_shape=(
            jax.ShapeDtypeStruct((rows, D), jnp.float32),
            jax.ShapeDtypeStruct((cols, D), jnp.float32),
            jax.ShapeDtypeStruct((1, cols), jnp.float32),
        ),
        grid=(8,),
        in_specs=[
            pl.BlockSpec((rows // 8, D), lambda i: (i, 0)),
            pl.BlockSpec((cols, D), lambda i: (0, 0)),
            pl.BlockSpec((8, rows // 8), lambda i: (0, 0)),
            pl.BlockSpec((8, cols // 8), lambda i: (0, 0)),
        ],
        out_specs=(
            pl.BlockSpec((rows // 8, D), lambda i: (i, 0)),
            pl.BlockSpec((cols, D), lambda i: (0, 0)),
            pl.BlockSpec((1, cols), lambda i: (0, 0)),
        ),
        compiler_params=_params(("arbitrary",)),
    )(x, y, u, a)


def _plan_scatter_kernel(n_col, n_row, x_ref, y_ref, u_ref, a_ref, gi_out, gc_out,
                         gi, pc, csum, gcs, bufi, bufc, sendi, recvi, sendc, recvc):
    me_c, me_r = lax.axis_index("col"), lax.axis_index("row")
    barrier = pltpu.get_barrier_semaphore()
    for d in range(1, n_col):
        pl.semaphore_signal(barrier, inc=1, device_id=_peer("col", lax.rem(me_c + d, n_col)),
                            device_id_type=pl.DeviceIdType.MESH)
    for d in range(1, n_row):
        pl.semaphore_signal(barrier, inc=1, device_id=_peer("row", lax.rem(me_r + d, n_row)),
                            device_id_type=pl.DeviceIdType.MESH)

    def to_col_dev(k, slot):
        return pltpu.make_async_remote_copy(
            src_ref=gi.at[k], dst_ref=bufi.at[slot], send_sem=sendi.at[k], recv_sem=recvi.at[slot],
            device_id=_peer("col", k), device_id_type=pl.DeviceIdType.MESH)

    def to_row_dev(k, slot):
        return pltpu.make_async_remote_copy(
            src_ref=gcs.at[k], dst_ref=bufc.at[slot], send_sem=sendc.at[k], recv_sem=recvc.at[slot],
            device_id=_peer("row", k), device_id_type=pl.DeviceIdType.MESH)

    def each(n, me, body):
        for k in range(n):
            pl.when(me != k)(functools.partial(body, k))

    rows, cols = x_ref.shape[0], y_ref.shape[0]
    tiles = u_ref.shape[0]
    tile, m, mc = rows // tiles, rows // n_col, cols // n_row
    per = tile // m
    y = y_ref[...]
    a2 = _row_of(a_ref[...]) * LOG2E
    pc[...] = jnp.zeros_like(pc)
    csum[...] = jnp.zeros_like(csum)
    for i in range(tiles):
        x = x_ref[i * tile:(i + 1) * tile, :]
        cross = lax.dot_general(x, y, NT, preferred_element_type=jnp.float32)
        u = _to_col(u_ref[i:i + 1, :] * LOG2E)
        plan = jnp.exp2(u + a2 + SCALE2 * cross).astype(jnp.bfloat16)
        wide = plan.astype(jnp.float32)
        r = jnp.sum(wide, axis=1, keepdims=True)
        csum[...] += jnp.sum(wide, axis=0, keepdims=True)
        pulled = jnp.dot(plan, y, preferred_element_type=jnp.float32)
        g = 2.0 * (r * x.astype(jnp.float32) - pulled)
        for s in range(per):
            gi[i * per + s] = g[s * m:(s + 1) * m]
        pc[...] += lax.dot_general(plan, x, TN, preferred_element_type=jnp.float32)
        if i == 1:
            pl.semaphore_wait(barrier, n_col + n_row - 2)
        if i >= 1:
            for s in range((i - 1) * per, i * per):
                pl.when(me_c != s)(functools.partial(lambda k: to_col_dev(k, me_c).start(), s))
    for s in range((tiles - 1) * per, tiles * per):
        pl.when(me_c != s)(functools.partial(lambda k: to_col_dev(k, me_c).start(), s))
    gcv = 2.0 * (_to_col(csum[...]) * y.astype(jnp.float32) - pc[...])
    for k in range(n_row):
        gcs[k] = gcv[k * mc:(k + 1) * mc]
    each(n_row, me_r, lambda k: to_row_dev(k, me_r).start())
    each(n_col, me_c, lambda k: to_col_dev(k, me_c).wait_send())
    each(n_row, me_r, lambda k: to_row_dev(k, me_r).wait_send())
    each(n_col, me_c, lambda k: to_col_dev(k, k).wait_recv())
    each(n_row, me_r, lambda k: to_row_dev(k, k).wait_recv())
    bufi[me_c] = gi[me_c]
    bufc[me_r] = gcs[me_r]
    gi_out[...] = jnp.sum(bufi[...], axis=0)
    gc_out[...] = jnp.sum(bufc[...], axis=0)


def plan_scatter(x, y, u, a, n_col, n_row):
    rows, cols = x.shape[0], y.shape[0]
    m, mc = rows // n_col, cols // n_row
    return pl.pallas_call(
        functools.partial(_plan_scatter_kernel, n_col, n_row),
        out_shape=(jax.ShapeDtypeStruct((m, D), jnp.float32),
                   jax.ShapeDtypeStruct((mc, D), jnp.float32)),
        in_specs=[pl.BlockSpec(memory_space=pltpu.VMEM)] * 4,
        out_specs=(pl.BlockSpec(memory_space=pltpu.VMEM),) * 2,
        scratch_shapes=[
            pltpu.VMEM((n_col, m, D), jnp.float32),
            pltpu.VMEM((cols, D), jnp.float32),
            pltpu.VMEM((1, cols), jnp.float32),
            pltpu.VMEM((n_row, mc, D), jnp.float32),
            pltpu.VMEM((n_col, m, D), jnp.float32),
            pltpu.VMEM((n_row, mc, D), jnp.float32),
            pltpu.SemaphoreType.DMA((n_col,)),
            pltpu.SemaphoreType.DMA((n_col,)),
            pltpu.SemaphoreType.DMA((n_row,)),
            pltpu.SemaphoreType.DMA((n_row,)),
        ],
        compiler_params=pltpu.CompilerParams(
            collective_id=4, has_side_effects=True, vmem_limit_bytes=VMEM_LIMIT),
    )(x, y, u, a)


def _lse_combine_kernel(axis, n, scale, p_ref, q_ref, a_ref, m_ref, s_ref, o_ref,
                        part, buf, send, recv):
    me = lax.axis_index(axis)
    barrier = pltpu.get_barrier_semaphore()
    for d in range(1, n):
        pl.semaphore_signal(barrier, inc=1, device_id=_peer(axis, lax.rem(me + d, n)),
                            device_id_type=pl.DeviceIdType.MESH)

    def out_copy(c, d):
        return pltpu.make_async_remote_copy(
            src_ref=part.at[c], dst_ref=buf.at[me, c], send_sem=send.at[c, d],
            recv_sem=recv.at[c, me], device_id=_peer(axis, lax.rem(me + d, n)),
            device_id_type=pl.DeviceIdType.MESH)

    def in_copy(c, d):
        src = lax.rem(me + n - d, n)
        return pltpu.make_async_remote_copy(
            src_ref=part.at[c], dst_ref=buf.at[src, c], send_sem=send.at[c, d],
            recv_sem=recv.at[c, src], device_id=_peer(axis, src),
            device_id_type=pl.DeviceIdType.MESH)

    def send_half(c):
        for d in range(1, n):
            out_copy(c, d).start()

    half = part.shape[1]
    tile = p_ref.shape[0] // (2 * half)
    cq = q_ref.shape[0]
    wide = jnp.transpose(jnp.broadcast_to(_row_of(a_ref[...]) * scale, (D, cq)))
    hi = wide.astype(jnp.bfloat16)
    rest = wide - hi.astype(jnp.float32)
    mid = rest.astype(jnp.bfloat16)
    low = (rest - mid.astype(jnp.float32)).astype(jnp.bfloat16)
    lane = lax.broadcasted_iota(jnp.int32, (cq, D), 1)
    zero = jnp.zeros_like(hi)
    extra = jnp.where(lane == 0, hi, jnp.where(lane == 1, mid, jnp.where(lane == 2, low, zero)))
    q = jnp.concatenate([q_ref[...], extra], axis=1)
    ones = jnp.where(lax.broadcasted_iota(jnp.int32, (tile, D), 1) < 3, 1.0, 0.0).astype(jnp.bfloat16)

    def body(i, carry):
        start = pl.multiple_of(i * tile, tile)
        p = jnp.concatenate([p_ref[pl.ds(start, tile), :], ones], axis=1)
        shifted = lax.dot_general(p, q, NT, preferred_element_type=jnp.float32)
        top = jnp.max(shifted, axis=1, keepdims=True)
        total = jnp.sum(jnp.exp2((shifted - top) * SCALE2), axis=1, keepdims=True)
        row = _to_row(top * TWO_INV + jnp.log(total)) - s_ref[pl.ds(i, 1), :] * INV
        part.at[i // half][pl.ds(i % half, 1), :] = row

        @pl.when(i == half)
        def _():
            pl.semaphore_wait(barrier, n - 1)
            send_half(0)

        return carry

    lax.fori_loop(0, 2 * half, body, 0)

    def finish(c):
        for d in range(1, n):
            out_copy(c, d).wait_send()
        for d in range(1, n):
            in_copy(c, d).wait_recv()
        buf[me, c] = part[c]
        parts = buf[:, c]
        top = jnp.max(parts, axis=0)
        total = top + jnp.log(jnp.sum(jnp.exp(parts - top[None]), axis=0))
        rows = slice(c * half, (c + 1) * half)
        mass = m_ref[...].reshape(2 * half, -1)[rows, :]
        o_ref[rows, :] = (EPS * (jnp.log(mass) - total) - s_ref[rows, :]) * INV

    finish(0)
    send_half(1)
    finish(1)


def lse_combine(p, q, a, mass, sq, axis, scale=EPS / 2.0):
    n = lax.axis_size(axis)
    m = p.shape[0] // 8
    return pl.pallas_call(
        functools.partial(_lse_combine_kernel, axis, n, scale),
        out_shape=jax.ShapeDtypeStruct((8, m), jnp.float32),
        in_specs=[pl.BlockSpec(memory_space=pltpu.VMEM)] * 5,
        out_specs=pl.BlockSpec(memory_space=pltpu.VMEM),
        scratch_shapes=[
            pltpu.VMEM((2, 4, m), jnp.float32),
            pltpu.VMEM((n, 2, 4, m), jnp.float32),
            pltpu.SemaphoreType.DMA((2, n)),
            pltpu.SemaphoreType.DMA((2, n)),
        ],
        compiler_params=pltpu.CompilerParams(
            collective_id=(5 if axis == "col" else 6) + (0 if scale == EPS / 2.0 else 3),
            has_side_effects=True,
            vmem_limit_bytes=VMEM_LIMIT),
    )(p, q, a, mass, sq)


def squares(values):
    return jnp.sum(jnp.square(values.astype(jnp.float32)), axis=1)


def _peer(axis, k):
    if axis == "col":
        return (lax.axis_index("row"), k)
    return (k, lax.axis_index("col"))


def _gather_lse_kernel(axis, n, x_ref, m_ref, q_ref, o_ref, buf, send, recv):
    me = lax.axis_index(axis)
    barrier = pltpu.get_barrier_semaphore()
    for d in range(1, n):
        pl.semaphore_signal(barrier, inc=1, device_id=_peer(axis, lax.rem(me + d, n)),
                            device_id_type=pl.DeviceIdType.MESH)
    pl.semaphore_wait(barrier, n - 1)
    copies = []
    for d in range(1, n):
        copy = pltpu.make_async_remote_copy(
            src_ref=x_ref, dst_ref=buf.at[me], send_sem=send.at[d], recv_sem=recv.at[me],
            device_id=_peer(axis, lax.rem(me + d, n)), device_id_type=pl.DeviceIdType.MESH)
        copy.start()
        copies.append(copy)
    for copy in copies:
        copy.wait_send()
    for d in range(1, n):
        src = lax.rem(me + n - d, n)
        pltpu.make_async_remote_copy(
            src_ref=x_ref, dst_ref=buf.at[src], send_sem=send.at[d], recv_sem=recv.at[src],
            device_id=_peer(axis, src), device_id_type=pl.DeviceIdType.MESH).wait_recv()
    buf[me] = x_ref[...]
    parts = buf[...]
    top = jnp.max(parts, axis=0)
    total = top + jnp.log(jnp.sum(jnp.exp(parts - top[None]), axis=0))
    o_ref[...] = (EPS * (m_ref[...] - total) - q_ref[...]) * INV


def _exchange_kernel(jobs, *refs):
    count = len(jobs)
    ins, outs = refs[:count], refs[count:2 * count]
    gathers = sum(kind == "gather" for _, _, kind in jobs)
    sqs = refs[2 * count:2 * count + gathers]
    rest = refs[2 * count + gathers:]
    bufs, sends, recvs = rest[0::3], rest[1::3], rest[2::3]
    barrier = pltpu.get_barrier_semaphore()
    for axis, n, kind in jobs:
        me = lax.axis_index(axis)
        for d in range(1, n):
            pl.semaphore_signal(barrier, inc=1, device_id=_peer(axis, lax.rem(me + d, n)),
                                device_id_type=pl.DeviceIdType.MESH)
    pl.semaphore_wait(barrier, sum(n - 1 for _, n, _ in jobs))

    def copy(job, d, peer, slot):
        axis, n, kind = jobs[job]
        src = ins[job] if kind == "gather" else ins[job].at[peer]
        return pltpu.make_async_remote_copy(
            src_ref=src, dst_ref=bufs[job].at[slot], send_sem=sends[job].at[d],
            recv_sem=recvs[job].at[slot], device_id=_peer(axis, peer),
            device_id_type=pl.DeviceIdType.MESH)

    started = []
    for job, (axis, n, kind) in enumerate(jobs):
        me = lax.axis_index(axis)
        for d in range(1, n):
            started.append(copy(job, d, lax.rem(me + d, n), me))
            started[-1].start()
    for c in started:
        c.wait_send()
    for job, (axis, n, kind) in enumerate(jobs):
        me = lax.axis_index(axis)
        for d in range(1, n):
            src = lax.rem(me + n - d, n)
            copy(job, d, src, src).wait_recv()
        if kind == "gather":
            bufs[job][me] = ins[job][...]
            outs[job][...] = bufs[job][...]
            sq = sqs[job]
            m = bufs[job].shape[1]
            per = sq.shape[1] // m
            for j in range(n):
                v = bufs[job][j].astype(jnp.float32)
                row = _to_row(jnp.sum(v * v, axis=1, keepdims=True))
                sq[j // per:j // per + 1, (j % per) * m:(j % per + 1) * m] = row
        else:
            bufs[job][me] = ins[job][me]
            outs[job][...] = jnp.sum(bufs[job][...], axis=0)


def exchange(jobs, arrays, collective_id):
    shapes, scratch = [], []
    for (axis, n, kind), x in zip(jobs, arrays):
        block = x.shape if kind == "gather" else x.shape[1:]
        shapes.append(jax.ShapeDtypeStruct((n,) + block if kind == "gather" else block, x.dtype))
        scratch += [pltpu.VMEM((n,) + block, x.dtype), pltpu.SemaphoreType.DMA((n,)),
                    pltpu.SemaphoreType.DMA((n,))]
    for (axis, n, kind), x in zip(jobs, arrays):
        if kind == "gather":
            shapes.append(jax.ShapeDtypeStruct((8, n * x.shape[0] // 8), jnp.float32))
    return pl.pallas_call(
        functools.partial(_exchange_kernel, tuple(jobs)),
        out_shape=tuple(shapes),
        in_specs=[pl.BlockSpec(memory_space=pltpu.VMEM)] * len(jobs),
        out_specs=tuple(pl.BlockSpec(memory_space=pltpu.VMEM) for _ in shapes),
        scratch_shapes=scratch,
        compiler_params=pltpu.CompilerParams(
            collective_id=collective_id, has_side_effects=True, vmem_limit_bytes=VMEM_LIMIT),
    )(*arrays)


def combine(block, axis, log_mass, sq):
    n = lax.axis_size(axis)
    return pl.pallas_call(
        functools.partial(_gather_lse_kernel, axis, n),
        out_shape=jax.ShapeDtypeStruct(block.shape, jnp.float32),
        in_specs=[pl.BlockSpec(memory_space=pltpu.VMEM)] * 3,
        out_specs=pl.BlockSpec(memory_space=pltpu.VMEM),
        scratch_shapes=[
            pltpu.VMEM((n,) + block.shape, jnp.float32),
            pltpu.SemaphoreType.DMA((n,)),
            pltpu.SemaphoreType.DMA((n,)),
        ],
        compiler_params=pltpu.CompilerParams(
            collective_id=0 if axis == "col" else 1, has_side_effects=True),
    )(block, log_mass, sq)


def local(imu, camera, imu_mass, cam_mass):
    n_col, n_row = lax.axis_size("col"), lax.axis_size("row")
    imu_rows, cam_rows, rows_sq, cols_sq = exchange(
        [("col", n_col, "gather"), ("row", n_row, "gather")], [imu, camera[0]], 3)
    imu_rows = imu_rows.reshape(-1, D)
    cam_rows = cam_rows.reshape(-1, D)
    a, scale = cols_sq, -INV * EPS / 2.0
    for step in range(ITERS):
        u = lse_combine(imu_rows, cam_rows, a, imu_mass, rows_sq, "col", scale)
        a = lse_combine(cam_rows, imu_rows, u, cam_mass, cols_sq, "row")
        scale = EPS / 2.0

    grad_imu, grad_cam = plan_scatter(imu_rows, cam_rows, u, a, n_col, n_row)
    return (grad_imu, grad_cam[None])


def solution(mesh):
    in_specs = (P(("row", "col"), None), P("col", "row", None), P("row"), P("col"))
    out_specs = (P(("row", "col"), None), P("col", "row", None))
    return jax.shard_map(local, mesh=mesh, in_specs=in_specs, out_specs=out_specs, check_vma=False)
```

```python
import functools

import jax
import jax.numpy as jnp
from jax import lax
from jax.experimental import pallas as pl
from jax.experimental.pallas import tpu as pltpu
from jax.sharding import PartitionSpec as P

D = 128
ITERS = 3
EPS = D / 20.0
INV = 1.0 / EPS
TWO_INV = 2.0 / EPS
VMEM_LIMIT = 60 * 1024 * 1024
LOG2E = 1.4426950408889634
LN2 = 0.6931471805599453
SCALE2 = TWO_INV * LOG2E
NT = (((1,), (1,)), ((), ()))
TN = (((0,), (0,)), ((), ()))


def _params(semantics):
    return pltpu.CompilerParams(dimension_semantics=semantics, vmem_limit_bytes=VMEM_LIMIT)


def _to_row(col):
    return jnp.transpose(jnp.broadcast_to(col, (col.shape[0], D)))[0:1, :]


def _to_col(row):
    return jnp.transpose(jnp.broadcast_to(row, (D, row.shape[1])))[:, 0:1]


def _row_of(v):
    return jnp.concatenate([v[k:k + 1, :] for k in range(v.shape[0])], axis=1)


def _lse_kernel(p_ref, q_ref, a_ref, b_ref, o_ref):
    i = pl.program_id(0)
    cross = lax.dot_general(p_ref[...], q_ref[...], NT, preferred_element_type=jnp.float32)
    t = _row_of(a_ref[...]) * LOG2E + SCALE2 * cross
    top = jnp.max(t, axis=1, keepdims=True)
    total = jnp.sum(jnp.exp2(t - top), axis=1, keepdims=True)
    o_ref[pl.ds(i, 1), :] = _to_row(top * LN2 + jnp.log(total)) - b_ref[pl.ds(i, 1), :]


def lse(p, q, a, b):
    rows, cols = p.shape[0], q.shape[0]
    tile = rows // 8
    return pl.pallas_call(
        _lse_kernel,
        out_shape=jax.ShapeDtypeStruct((8, tile), jnp.float32),
        grid=(8,),
        in_specs=[
            pl.BlockSpec((tile, D), lambda i: (i, 0)),
            pl.BlockSpec((cols, D), lambda i: (0, 0)),
            pl.BlockSpec((8, cols // 8), lambda i: (0, 0)),
            pl.BlockSpec((8, tile), lambda i: (0, 0)),
        ],
        out_specs=pl.BlockSpec((8, tile), lambda i: (0, 0)),
        compiler_params=_params(("arbitrary",)),
    )(p, q, a, b)


def _plan_kernel(x_ref, y_ref, u_ref, a_ref, gi_ref, pc_ref, c_ref):
    @pl.when(pl.program_id(0) == 0)
    def _():
        pc_ref[...] = jnp.zeros_like(pc_ref)
        c_ref[...] = jnp.zeros_like(c_ref)

    i = pl.program_id(0)
    x = x_ref[...]
    cross = lax.dot_general(x, y_ref[...], NT, preferred_element_type=jnp.float32)
    u = _to_col(u_ref[pl.ds(i, 1), :] * LOG2E)
    plan = jnp.exp2(u + _row_of(a_ref[...]) * LOG2E + SCALE2 * cross).astype(jnp.bfloat16)
    wide = plan.astype(jnp.float32)
    r = jnp.sum(wide, axis=1, keepdims=True)
    c_ref[...] += jnp.sum(wide, axis=0, keepdims=True)
    pulled = jnp.dot(plan, y_ref[...], preferred_element_type=jnp.float32)
    gi_ref[...] = 2.0 * (r * x.astype(jnp.float32) - pulled)
    pc_ref[...] += lax.dot_general(plan, x, TN, preferred_element_type=jnp.float32)


def plan_grads(x, y, u, a):
    rows, cols = x.shape[0], y.shape[0]
    return pl.pallas_call(
        _plan_kernel,
        out_shape=(
            jax.ShapeDtypeStruct((rows, D), jnp.float32),
            jax.ShapeDtypeStruct((cols, D), jnp.float32),
            jax.ShapeDtypeStruct((1, cols), jnp.float32),
        ),
        grid=(8,),
        in_specs=[
            pl.BlockSpec((rows // 8, D), lambda i: (i, 0)),
            pl.BlockSpec((cols, D), lambda i: (0, 0)),
            pl.BlockSpec((8, rows // 8), lambda i: (0, 0)),
            pl.BlockSpec((8, cols // 8), lambda i: (0, 0)),
        ],
        out_specs=(
            pl.BlockSpec((rows // 8, D), lambda i: (i, 0)),
            pl.BlockSpec((cols, D), lambda i: (0, 0)),
            pl.BlockSpec((1, cols), lambda i: (0, 0)),
        ),
        compiler_params=_params(("arbitrary",)),
    )(x, y, u, a)


def _plan_scatter_kernel(n_col, n_row, x_ref, y_ref, u_ref, a_ref, gi_out, gc_out,
                         gi, pc, csum, gcs, bufi, bufc, sendi, recvi, sendc, recvc):
    me_c, me_r = lax.axis_index("col"), lax.axis_index("row")
    barrier = pltpu.get_barrier_semaphore()
    for d in range(1, n_col):
        pl.semaphore_signal(barrier, inc=1, device_id=_peer("col", lax.rem(me_c + d, n_col)),
                            device_id_type=pl.DeviceIdType.MESH)
    for d in range(1, n_row):
        pl.semaphore_signal(barrier, inc=1, device_id=_peer("row", lax.rem(me_r + d, n_row)),
                            device_id_type=pl.DeviceIdType.MESH)

    def to_col_dev(k, slot):
        return pltpu.make_async_remote_copy(
            src_ref=gi.at[k], dst_ref=bufi.at[slot], send_sem=sendi.at[k], recv_sem=recvi.at[slot],
            device_id=_peer("col", k), device_id_type=pl.DeviceIdType.MESH)

    def to_row_dev(k, slot):
        return pltpu.make_async_remote_copy(
            src_ref=gcs.at[k], dst_ref=bufc.at[slot], send_sem=sendc.at[k], recv_sem=recvc.at[slot],
            device_id=_peer("row", k), device_id_type=pl.DeviceIdType.MESH)

    def send_tile(t):
        for s in range(per):
            k = t * per + s
            pl.when(me_c != k)(functools.partial(lambda k: to_col_dev(k, me_c).start(), k))

    def each(n, me, body):
        for k in range(n):
            pl.when(me != k)(functools.partial(body, k))

    rows, cols = x_ref.shape[0], y_ref.shape[0]
    tiles = u_ref.shape[0]
    tile, m, mc = rows // tiles, rows // n_col, cols // n_row
    per = tile // m
    y = y_ref[...]
    a2 = _row_of(a_ref[...]) * LOG2E
    pc[...] = jnp.zeros_like(pc)
    csum[...] = jnp.zeros_like(csum)
    order = [lax.rem(me_c // per + 1 + i, tiles) for i in range(tiles)]
    for i in range(tiles):
        t = order[i]
        x = x_ref[pl.ds(pl.multiple_of(t * tile, tile), tile), :]
        cross = lax.dot_general(x, y, NT, preferred_element_type=jnp.float32)
        u = _to_col(u_ref[pl.ds(t, 1), :] * LOG2E)
        plan = jnp.exp2(u + a2 + SCALE2 * cross).astype(jnp.bfloat16)
        wide = plan.astype(jnp.float32)
        r = jnp.sum(wide, axis=1, keepdims=True)
        csum[...] += jnp.sum(wide, axis=0, keepdims=True)
        pulled = jnp.dot(plan, y, preferred_element_type=jnp.float32)
        g = 2.0 * (r * x.astype(jnp.float32) - pulled)
        for s in range(per):
            gi[t * per + s] = g[s * m:(s + 1) * m]
        pc[...] += lax.dot_general(plan, x, TN, preferred_element_type=jnp.float32)
        if i == 1:
            pl.semaphore_wait(barrier, n_col + n_row - 2)
        if i >= 1:
            send_tile(order[i - 1])
    send_tile(order[tiles - 1])
    gcv = 2.0 * (_to_col(csum[...]) * y.astype(jnp.float32) - pc[...])
    for k in range(n_row):
        gcs[k] = gcv[k * mc:(k + 1) * mc]
    each(n_row, me_r, lambda k: to_row_dev(k, me_r).start())
    each(n_col, me_c, lambda k: to_col_dev(k, me_c).wait_send())
    each(n_row, me_r, lambda k: to_row_dev(k, me_r).wait_send())
    each(n_col, me_c, lambda k: to_col_dev(k, k).wait_recv())
    each(n_row, me_r, lambda k: to_row_dev(k, k).wait_recv())
    bufi[me_c] = gi[me_c]
    bufc[me_r] = gcs[me_r]
    gi_out[...] = jnp.sum(bufi[...], axis=0)
    gc_out[...] = jnp.sum(bufc[...], axis=0)


def plan_scatter(x, y, u, a, n_col, n_row):
    rows, cols = x.shape[0], y.shape[0]
    m, mc = rows // n_col, cols // n_row
    return pl.pallas_call(
        functools.partial(_plan_scatter_kernel, n_col, n_row),
        out_shape=(jax.ShapeDtypeStruct((m, D), jnp.float32),
                   jax.ShapeDtypeStruct((mc, D), jnp.float32)),
        in_specs=[pl.BlockSpec(memory_space=pltpu.VMEM)] * 4,
        out_specs=(pl.BlockSpec(memory_space=pltpu.VMEM),) * 2,
        scratch_shapes=[
            pltpu.VMEM((n_col, m, D), jnp.float32),
            pltpu.VMEM((cols, D), jnp.float32),
            pltpu.VMEM((1, cols), jnp.float32),
            pltpu.VMEM((n_row, mc, D), jnp.float32),
            pltpu.VMEM((n_col, m, D), jnp.float32),
            pltpu.VMEM((n_row, mc, D), jnp.float32),
            pltpu.SemaphoreType.DMA((n_col,)),
            pltpu.SemaphoreType.DMA((n_col,)),
            pltpu.SemaphoreType.DMA((n_row,)),
            pltpu.SemaphoreType.DMA((n_row,)),
        ],
        compiler_params=pltpu.CompilerParams(
            collective_id=4, has_side_effects=True, vmem_limit_bytes=VMEM_LIMIT),
    )(x, y, u, a)


def _lse_combine_kernel(axis, n, scale, p_ref, q_ref, a_ref, m_ref, s_ref, o_ref,
                        part, buf, send, recv):
    me = lax.axis_index(axis)
    barrier = pltpu.get_barrier_semaphore()
    for d in range(1, n):
        pl.semaphore_signal(barrier, inc=1, device_id=_peer(axis, lax.rem(me + d, n)),
                            device_id_type=pl.DeviceIdType.MESH)

    def out_copy(c, d):
        return pltpu.make_async_remote_copy(
            src_ref=part.at[c], dst_ref=buf.at[me, c], send_sem=send.at[c, d],
            recv_sem=recv.at[c, me], device_id=_peer(axis, lax.rem(me + d, n)),
            device_id_type=pl.DeviceIdType.MESH)

    def in_copy(c, d):
        src = lax.rem(me + n - d, n)
        return pltpu.make_async_remote_copy(
            src_ref=part.at[c], dst_ref=buf.at[src, c], send_sem=send.at[c, d],
            recv_sem=recv.at[c, src], device_id=_peer(axis, src),
            device_id_type=pl.DeviceIdType.MESH)

    def send_half(c):
        for d in range(1, n):
            out_copy(c, d).start()

    half = part.shape[1]
    tile = p_ref.shape[0] // (2 * half)
    cq = q_ref.shape[0]
    wide = jnp.transpose(jnp.broadcast_to(_row_of(a_ref[...]) * scale, (D, cq)))
    hi = wide.astype(jnp.bfloat16)
    rest = wide - hi.astype(jnp.float32)
    mid = rest.astype(jnp.bfloat16)
    low = (rest - mid.astype(jnp.float32)).astype(jnp.bfloat16)
    lane = lax.broadcasted_iota(jnp.int32, (cq, D), 1)
    zero = jnp.zeros_like(hi)
    extra = jnp.where(lane == 0, hi, jnp.where(lane == 1, mid, jnp.where(lane == 2, low, zero)))
    q = jnp.concatenate([q_ref[...], extra], axis=1)
    ones = jnp.where(lax.broadcasted_iota(jnp.int32, (tile, D), 1) < 3, 1.0, 0.0).astype(jnp.bfloat16)

    def body(i, carry):
        start = pl.multiple_of(i * tile, tile)
        p = jnp.concatenate([p_ref[pl.ds(start, tile), :], ones], axis=1)
        shifted = lax.dot_general(p, q, NT, preferred_element_type=jnp.float32)
        top = jnp.max(shifted, axis=1, keepdims=True)
        total = jnp.sum(jnp.exp2((shifted - top) * SCALE2), axis=1, keepdims=True)
        row = _to_row(top * TWO_INV + jnp.log(total)) - s_ref[pl.ds(i, 1), :] * INV
        part.at[i // half][pl.ds(i % half, 1), :] = row

        @pl.when(i == half)
        def _():
            pl.semaphore_wait(barrier, n - 1)
            send_half(0)

        return carry

    lax.fori_loop(0, 2 * half, body, 0)

    def finish(c):
        for d in range(1, n):
            out_copy(c, d).wait_send()
        for d in range(1, n):
            in_copy(c, d).wait_recv()
        buf[me, c] = part[c]
        parts = buf[:, c]
        top = jnp.max(parts, axis=0)
        total = top + jnp.log(jnp.sum(jnp.exp(parts - top[None]), axis=0))
        rows = slice(c * half, (c + 1) * half)
        mass = m_ref[...].reshape(2 * half, -1)[rows, :]
        o_ref[rows, :] = (EPS * (jnp.log(mass) - total) - s_ref[rows, :]) * INV

    finish(0)
    send_half(1)
    finish(1)


def lse_combine(p, q, a, mass, sq, axis, scale=EPS / 2.0):
    n = lax.axis_size(axis)
    m = p.shape[0] // 8
    return pl.pallas_call(
        functools.partial(_lse_combine_kernel, axis, n, scale),
        out_shape=jax.ShapeDtypeStruct((8, m), jnp.float32),
        in_specs=[pl.BlockSpec(memory_space=pltpu.VMEM)] * 5,
        out_specs=pl.BlockSpec(memory_space=pltpu.VMEM),
        scratch_shapes=[
            pltpu.VMEM((2, 4, m), jnp.float32),
            pltpu.VMEM((n, 2, 4, m), jnp.float32),
            pltpu.SemaphoreType.DMA((2, n)),
            pltpu.SemaphoreType.DMA((2, n)),
        ],
        compiler_params=pltpu.CompilerParams(
            collective_id=(5 if axis == "col" else 6) + (0 if scale == EPS / 2.0 else 3),
            has_side_effects=True,
            vmem_limit_bytes=VMEM_LIMIT),
    )(p, q, a, mass, sq)


def squares(values):
    return jnp.sum(jnp.square(values.astype(jnp.float32)), axis=1)


def _peer(axis, k):
    if axis == "col":
        return (lax.axis_index("row"), k)
    return (k, lax.axis_index("col"))


def _gather_lse_kernel(axis, n, x_ref, m_ref, q_ref, o_ref, buf, send, recv):
    me = lax.axis_index(axis)
    barrier = pltpu.get_barrier_semaphore()
    for d in range(1, n):
        pl.semaphore_signal(barrier, inc=1, device_id=_peer(axis, lax.rem(me + d, n)),
                            device_id_type=pl.DeviceIdType.MESH)
    pl.semaphore_wait(barrier, n - 1)
    copies = []
    for d in range(1, n):
        copy = pltpu.make_async_remote_copy(
            src_ref=x_ref, dst_ref=buf.at[me], send_sem=send.at[d], recv_sem=recv.at[me],
            device_id=_peer(axis, lax.rem(me + d, n)), device_id_type=pl.DeviceIdType.MESH)
        copy.start()
        copies.append(copy)
    for copy in copies:
        copy.wait_send()
    for d in range(1, n):
        src = lax.rem(me + n - d, n)
        pltpu.make_async_remote_copy(
            src_ref=x_ref, dst_ref=buf.at[src], send_sem=send.at[d], recv_sem=recv.at[src],
            device_id=_peer(axis, src), device_id_type=pl.DeviceIdType.MESH).wait_recv()
    buf[me] = x_ref[...]
    parts = buf[...]
    top = jnp.max(parts, axis=0)
    total = top + jnp.log(jnp.sum(jnp.exp(parts - top[None]), axis=0))
    o_ref[...] = (EPS * (m_ref[...] - total) - q_ref[...]) * INV


def _exchange_kernel(jobs, *refs):
    count = len(jobs)
    ins, outs = refs[:count], refs[count:2 * count]
    gathers = sum(kind == "gather" for _, _, kind in jobs)
    sqs = refs[2 * count:2 * count + gathers]
    rest = refs[2 * count + gathers:]
    bufs, sends, recvs = rest[0::3], rest[1::3], rest[2::3]
    barrier = pltpu.get_barrier_semaphore()
    for axis, n, kind in jobs:
        me = lax.axis_index(axis)
        for d in range(1, n):
            pl.semaphore_signal(barrier, inc=1, device_id=_peer(axis, lax.rem(me + d, n)),
                                device_id_type=pl.DeviceIdType.MESH)
    pl.semaphore_wait(barrier, sum(n - 1 for _, n, _ in jobs))

    def copy(job, d, peer, slot):
        axis, n, kind = jobs[job]
        src = ins[job] if kind == "gather" else ins[job].at[peer]
        return pltpu.make_async_remote_copy(
            src_ref=src, dst_ref=bufs[job].at[slot], send_sem=sends[job].at[d],
            recv_sem=recvs[job].at[slot], device_id=_peer(axis, peer),
            device_id_type=pl.DeviceIdType.MESH)

    started = []
    for job, (axis, n, kind) in enumerate(jobs):
        me = lax.axis_index(axis)
        for d in range(1, n):
            started.append(copy(job, d, lax.rem(me + d, n), me))
            started[-1].start()
    for c in started:
        c.wait_send()
    for job, (axis, n, kind) in enumerate(jobs):
        me = lax.axis_index(axis)
        for d in range(1, n):
            src = lax.rem(me + n - d, n)
            copy(job, d, src, src).wait_recv()
        if kind == "gather":
            bufs[job][me] = ins[job][...]
            outs[job][...] = bufs[job][...]
            sq = sqs[job]
            m = bufs[job].shape[1]
            per = sq.shape[1] // m
            for j in range(n):
                v = bufs[job][j].astype(jnp.float32)
                row = _to_row(jnp.sum(v * v, axis=1, keepdims=True))
                sq[j // per:j // per + 1, (j % per) * m:(j % per + 1) * m] = row
        else:
            bufs[job][me] = ins[job][me]
            outs[job][...] = jnp.sum(bufs[job][...], axis=0)


def exchange(jobs, arrays, collective_id):
    shapes, scratch = [], []
    for (axis, n, kind), x in zip(jobs, arrays):
        block = x.shape if kind == "gather" else x.shape[1:]
        shapes.append(jax.ShapeDtypeStruct((n,) + block if kind == "gather" else block, x.dtype))
        scratch += [pltpu.VMEM((n,) + block, x.dtype), pltpu.SemaphoreType.DMA((n,)),
                    pltpu.SemaphoreType.DMA((n,))]
    for (axis, n, kind), x in zip(jobs, arrays):
        if kind == "gather":
            shapes.append(jax.ShapeDtypeStruct((8, n * x.shape[0] // 8), jnp.float32))
    return pl.pallas_call(
        functools.partial(_exchange_kernel, tuple(jobs)),
        out_shape=tuple(shapes),
        in_specs=[pl.BlockSpec(memory_space=pltpu.VMEM)] * len(jobs),
        out_specs=tuple(pl.BlockSpec(memory_space=pltpu.VMEM) for _ in shapes),
        scratch_shapes=scratch,
        compiler_params=pltpu.CompilerParams(
            collective_id=collective_id, has_side_effects=True, vmem_limit_bytes=VMEM_LIMIT),
    )(*arrays)


def combine(block, axis, log_mass, sq):
    n = lax.axis_size(axis)
    return pl.pallas_call(
        functools.partial(_gather_lse_kernel, axis, n),
        out_shape=jax.ShapeDtypeStruct(block.shape, jnp.float32),
        in_specs=[pl.BlockSpec(memory_space=pltpu.VMEM)] * 3,
        out_specs=pl.BlockSpec(memory_space=pltpu.VMEM),
        scratch_shapes=[
            pltpu.VMEM((n,) + block.shape, jnp.float32),
            pltpu.SemaphoreType.DMA((n,)),
            pltpu.SemaphoreType.DMA((n,)),
        ],
        compiler_params=pltpu.CompilerParams(
            collective_id=0 if axis == "col" else 1, has_side_effects=True),
    )(block, log_mass, sq)


def local(imu, camera, imu_mass, cam_mass):
    n_col, n_row = lax.axis_size("col"), lax.axis_size("row")
    imu_rows, cam_rows, rows_sq, cols_sq = exchange(
        [("col", n_col, "gather"), ("row", n_row, "gather")], [imu, camera[0]], 3)
    imu_rows = imu_rows.reshape(-1, D)
    cam_rows = cam_rows.reshape(-1, D)
    a, scale = cols_sq, -INV * EPS / 2.0
    for step in range(ITERS):
        u = lse_combine(imu_rows, cam_rows, a, imu_mass, rows_sq, "col", scale)
        a = lse_combine(cam_rows, imu_rows, u, cam_mass, cols_sq, "row")
        scale = EPS / 2.0

    grad_imu, grad_cam = plan_scatter(imu_rows, cam_rows, u, a, n_col, n_row)
    return (grad_imu, grad_cam[None])


def solution(mesh):
    in_specs = (P(("row", "col"), None), P("col", "row", None), P("row"), P("col"))
    out_specs = (P(("row", "col"), None), P("col", "row", None))
    return jax.shard_map(local, mesh=mesh, in_specs=in_specs, out_specs=out_specs, check_vma=False)
```

```python
import functools

import jax
import jax.numpy as jnp
from jax import lax
from jax.experimental import pallas as pl
from jax.experimental.pallas import tpu as pltpu
from jax.sharding import PartitionSpec as P

D = 128
ITERS = 3
EPS = D / 20.0
INV = 1.0 / EPS
TWO_INV = 2.0 / EPS
VMEM_LIMIT = 60 * 1024 * 1024
LOG2E = 1.4426950408889634
LN2 = 0.6931471805599453
SCALE2 = TWO_INV * LOG2E
NT = (((1,), (1,)), ((), ()))
TN = (((0,), (0,)), ((), ()))


def _params(semantics):
    return pltpu.CompilerParams(dimension_semantics=semantics, vmem_limit_bytes=VMEM_LIMIT)


def _to_row(col):
    return jnp.transpose(jnp.broadcast_to(col, (col.shape[0], D)))[0:1, :]


def _to_col(row):
    return jnp.transpose(jnp.broadcast_to(row, (D, row.shape[1])))[:, 0:1]


def _row_of(v):
    return jnp.concatenate([v[k:k + 1, :] for k in range(v.shape[0])], axis=1)


def _lse_kernel(p_ref, q_ref, a_ref, b_ref, o_ref):
    i = pl.program_id(0)
    cross = lax.dot_general(p_ref[...], q_ref[...], NT, preferred_element_type=jnp.float32)
    t = _row_of(a_ref[...]) * LOG2E + SCALE2 * cross
    top = jnp.max(t, axis=1, keepdims=True)
    total = jnp.sum(jnp.exp2(t - top), axis=1, keepdims=True)
    o_ref[pl.ds(i, 1), :] = _to_row(top * LN2 + jnp.log(total)) - b_ref[pl.ds(i, 1), :]


def lse(p, q, a, b):
    rows, cols = p.shape[0], q.shape[0]
    tile = rows // 8
    return pl.pallas_call(
        _lse_kernel,
        out_shape=jax.ShapeDtypeStruct((8, tile), jnp.float32),
        grid=(8,),
        in_specs=[
            pl.BlockSpec((tile, D), lambda i: (i, 0)),
            pl.BlockSpec((cols, D), lambda i: (0, 0)),
            pl.BlockSpec((8, cols // 8), lambda i: (0, 0)),
            pl.BlockSpec((8, tile), lambda i: (0, 0)),
        ],
        out_specs=pl.BlockSpec((8, tile), lambda i: (0, 0)),
        compiler_params=_params(("arbitrary",)),
    )(p, q, a, b)


def _plan_kernel(x_ref, y_ref, u_ref, a_ref, gi_ref, pc_ref, c_ref):
    @pl.when(pl.program_id(0) == 0)
    def _():
        pc_ref[...] = jnp.zeros_like(pc_ref)
        c_ref[...] = jnp.zeros_like(c_ref)

    i = pl.program_id(0)
    x = x_ref[...]
    cross = lax.dot_general(x, y_ref[...], NT, preferred_element_type=jnp.float32)
    u = _to_col(u_ref[pl.ds(i, 1), :] * LOG2E)
    plan = jnp.exp2(u + _row_of(a_ref[...]) * LOG2E + SCALE2 * cross).astype(jnp.bfloat16)
    wide = plan.astype(jnp.float32)
    r = jnp.sum(wide, axis=1, keepdims=True)
    c_ref[...] += jnp.sum(wide, axis=0, keepdims=True)
    pulled = jnp.dot(plan, y_ref[...], preferred_element_type=jnp.float32)
    gi_ref[...] = 2.0 * (r * x.astype(jnp.float32) - pulled)
    pc_ref[...] += lax.dot_general(plan, x, TN, preferred_element_type=jnp.float32)


def plan_grads(x, y, u, a):
    rows, cols = x.shape[0], y.shape[0]
    return pl.pallas_call(
        _plan_kernel,
        out_shape=(
            jax.ShapeDtypeStruct((rows, D), jnp.float32),
            jax.ShapeDtypeStruct((cols, D), jnp.float32),
            jax.ShapeDtypeStruct((1, cols), jnp.float32),
        ),
        grid=(8,),
        in_specs=[
            pl.BlockSpec((rows // 8, D), lambda i: (i, 0)),
            pl.BlockSpec((cols, D), lambda i: (0, 0)),
            pl.BlockSpec((8, rows // 8), lambda i: (0, 0)),
            pl.BlockSpec((8, cols // 8), lambda i: (0, 0)),
        ],
        out_specs=(
            pl.BlockSpec((rows // 8, D), lambda i: (i, 0)),
            pl.BlockSpec((cols, D), lambda i: (0, 0)),
            pl.BlockSpec((1, cols), lambda i: (0, 0)),
        ),
        compiler_params=_params(("arbitrary",)),
    )(x, y, u, a)


def _plan_scatter_kernel(n_col, n_row, x_ref, y_ref, u_ref, a_ref, gi_out, gc_out,
                         gi, pc, csum, gcs, bufi, bufc, sendi, recvi, sendc, recvc):
    me_c, me_r = lax.axis_index("col"), lax.axis_index("row")
    barrier = pltpu.get_barrier_semaphore()
    for d in range(1, n_col):
        pl.semaphore_signal(barrier, inc=1, device_id=_peer("col", lax.rem(me_c + d, n_col)),
                            device_id_type=pl.DeviceIdType.MESH)
    for d in range(1, n_row):
        pl.semaphore_signal(barrier, inc=1, device_id=_peer("row", lax.rem(me_r + d, n_row)),
                            device_id_type=pl.DeviceIdType.MESH)

    def to_col_dev(k, slot):
        return pltpu.make_async_remote_copy(
            src_ref=gi.at[k], dst_ref=bufi.at[slot], send_sem=sendi.at[k], recv_sem=recvi.at[slot],
            device_id=_peer("col", k), device_id_type=pl.DeviceIdType.MESH)

    def to_row_dev(k, slot):
        return pltpu.make_async_remote_copy(
            src_ref=gcs.at[k], dst_ref=bufc.at[slot], send_sem=sendc.at[k], recv_sem=recvc.at[slot],
            device_id=_peer("row", k), device_id_type=pl.DeviceIdType.MESH)

    def send_tile(t):
        for s in range(per):
            k = t * per + s
            pl.when(me_c != k)(functools.partial(lambda k: to_col_dev(k, me_c).start(), k))

    def each(n, me, body):
        for k in range(n):
            pl.when(me != k)(functools.partial(body, k))

    rows, cols = x_ref.shape[0], y_ref.shape[0]
    tiles = u_ref.shape[0]
    tile, m, mc = rows // tiles, rows // n_col, cols // n_row
    per = tile // m
    y = y_ref[...]
    a2 = _row_of(a_ref[...]) * LOG2E
    pc[...] = jnp.zeros_like(pc)
    csum[...] = jnp.zeros_like(csum)
    order = [lax.rem(me_c // per + 1 + i, tiles) for i in range(tiles)]
    for i in range(tiles):
        t = order[i]
        x = x_ref[pl.ds(pl.multiple_of(t * tile, tile), tile), :]
        cross = lax.dot_general(x, y, NT, preferred_element_type=jnp.float32)
        u = _to_col(u_ref[pl.ds(t, 1), :] * LOG2E)
        plan = jnp.exp2(u + a2 + SCALE2 * cross).astype(jnp.bfloat16)
        wide = plan.astype(jnp.float32)
        r = jnp.sum(wide, axis=1, keepdims=True)
        csum[...] += jnp.sum(wide, axis=0, keepdims=True)
        pulled = jnp.dot(plan, y, preferred_element_type=jnp.float32)
        g = 2.0 * (r * x.astype(jnp.float32) - pulled)
        for s in range(per):
            gi[t * per + s] = g[s * m:(s + 1) * m]
        pc[...] += lax.dot_general(plan, x, TN, preferred_element_type=jnp.float32)
        if i == 1:
            pl.semaphore_wait(barrier, n_col + n_row - 2)
        if i >= 1:
            send_tile(order[i - 1])
    send_tile(order[tiles - 1])
    gcv = 2.0 * (_to_col(csum[...]) * y.astype(jnp.float32) - pc[...])
    for k in range(n_row):
        gcs[k] = gcv[k * mc:(k + 1) * mc]
    for d in range(1, n_row):
        to_row_dev(lax.rem(me_r + d, n_row), me_r).start()
    each(n_col, me_c, lambda k: to_col_dev(k, me_c).wait_send())
    each(n_row, me_r, lambda k: to_row_dev(k, me_r).wait_send())
    each(n_col, me_c, lambda k: to_col_dev(k, k).wait_recv())
    each(n_row, me_r, lambda k: to_row_dev(k, k).wait_recv())
    bufi[me_c] = gi[me_c]
    bufc[me_r] = gcs[me_r]
    gi_out[...] = jnp.sum(bufi[...], axis=0)
    gc_out[...] = jnp.sum(bufc[...], axis=0)


def plan_scatter(x, y, u, a, n_col, n_row):
    rows, cols = x.shape[0], y.shape[0]
    m, mc = rows // n_col, cols // n_row
    return pl.pallas_call(
        functools.partial(_plan_scatter_kernel, n_col, n_row),
        out_shape=(jax.ShapeDtypeStruct((m, D), jnp.float32),
                   jax.ShapeDtypeStruct((mc, D), jnp.float32)),
        in_specs=[pl.BlockSpec(memory_space=pltpu.VMEM)] * 4,
        out_specs=(pl.BlockSpec(memory_space=pltpu.VMEM),) * 2,
        scratch_shapes=[
            pltpu.VMEM((n_col, m, D), jnp.float32),
            pltpu.VMEM((cols, D), jnp.float32),
            pltpu.VMEM((1, cols), jnp.float32),
            pltpu.VMEM((n_row, mc, D), jnp.float32),
            pltpu.VMEM((n_col, m, D), jnp.float32),
            pltpu.VMEM((n_row, mc, D), jnp.float32),
            pltpu.SemaphoreType.DMA((n_col,)),
            pltpu.SemaphoreType.DMA((n_col,)),
            pltpu.SemaphoreType.DMA((n_row,)),
            pltpu.SemaphoreType.DMA((n_row,)),
        ],
        compiler_params=pltpu.CompilerParams(
            collective_id=4, has_side_effects=True, vmem_limit_bytes=VMEM_LIMIT),
    )(x, y, u, a)


def _lse_combine_kernel(axis, n, scale, p_ref, q_ref, a_ref, m_ref, s_ref, o_ref,
                        part, buf, send, recv):
    me = lax.axis_index(axis)
    barrier = pltpu.get_barrier_semaphore()
    for d in range(1, n):
        pl.semaphore_signal(barrier, inc=1, device_id=_peer(axis, lax.rem(me + d, n)),
                            device_id_type=pl.DeviceIdType.MESH)

    def out_copy(c, d):
        return pltpu.make_async_remote_copy(
            src_ref=part.at[c], dst_ref=buf.at[me, c], send_sem=send.at[c, d],
            recv_sem=recv.at[c, me], device_id=_peer(axis, lax.rem(me + d, n)),
            device_id_type=pl.DeviceIdType.MESH)

    def in_copy(c, d):
        src = lax.rem(me + n - d, n)
        return pltpu.make_async_remote_copy(
            src_ref=part.at[c], dst_ref=buf.at[src, c], send_sem=send.at[c, d],
            recv_sem=recv.at[c, src], device_id=_peer(axis, src),
            device_id_type=pl.DeviceIdType.MESH)

    def send_half(c):
        for d in range(1, n):
            out_copy(c, d).start()

    half = part.shape[1]
    tile = p_ref.shape[0] // (2 * half)
    cq = q_ref.shape[0]
    wide = jnp.transpose(jnp.broadcast_to(_row_of(a_ref[...]) * scale, (D, cq)))
    hi = wide.astype(jnp.bfloat16)
    rest = wide - hi.astype(jnp.float32)
    mid = rest.astype(jnp.bfloat16)
    low = (rest - mid.astype(jnp.float32)).astype(jnp.bfloat16)
    lane = lax.broadcasted_iota(jnp.int32, (cq, D), 1)
    zero = jnp.zeros_like(hi)
    extra = jnp.where(lane == 0, hi, jnp.where(lane == 1, mid, jnp.where(lane == 2, low, zero)))
    q = jnp.concatenate([q_ref[...], extra], axis=1)
    ones = jnp.where(lax.broadcasted_iota(jnp.int32, (tile, D), 1) < 3, 1.0, 0.0).astype(jnp.bfloat16)

    def body(i, carry):
        start = pl.multiple_of(i * tile, tile)
        p = jnp.concatenate([p_ref[pl.ds(start, tile), :], ones], axis=1)
        shifted = lax.dot_general(p, q, NT, preferred_element_type=jnp.float32)
        top = jnp.max(shifted, axis=1, keepdims=True)
        total = jnp.sum(jnp.exp2((shifted - top) * SCALE2), axis=1, keepdims=True)
        row = _to_row(top * TWO_INV + jnp.log(total)) - s_ref[pl.ds(i, 1), :] * INV
        part.at[i // half][pl.ds(i % half, 1), :] = row

        @pl.when(i == half)
        def _():
            pl.semaphore_wait(barrier, n - 1)
            send_half(0)

        return carry

    lax.fori_loop(0, 2 * half, body, 0)

    def finish(c):
        for d in range(1, n):
            out_copy(c, d).wait_send()
        for d in range(1, n):
            in_copy(c, d).wait_recv()
        buf[me, c] = part[c]
        parts = buf[:, c]
        top = jnp.max(parts, axis=0)
        total = top + jnp.log(jnp.sum(jnp.exp(parts - top[None]), axis=0))
        rows = slice(c * half, (c + 1) * half)
        mass = m_ref[...].reshape(2 * half, -1)[rows, :]
        o_ref[rows, :] = (EPS * (jnp.log(mass) - total) - s_ref[rows, :]) * INV

    finish(0)
    send_half(1)
    finish(1)


def lse_combine(p, q, a, mass, sq, axis, scale=EPS / 2.0):
    n = lax.axis_size(axis)
    m = p.shape[0] // 8
    return pl.pallas_call(
        functools.partial(_lse_combine_kernel, axis, n, scale),
        out_shape=jax.ShapeDtypeStruct((8, m), jnp.float32),
        in_specs=[pl.BlockSpec(memory_space=pltpu.VMEM)] * 5,
        out_specs=pl.BlockSpec(memory_space=pltpu.VMEM),
        scratch_shapes=[
            pltpu.VMEM((2, 4, m), jnp.float32),
            pltpu.VMEM((n, 2, 4, m), jnp.float32),
            pltpu.SemaphoreType.DMA((2, n)),
            pltpu.SemaphoreType.DMA((2, n)),
        ],
        compiler_params=pltpu.CompilerParams(
            collective_id=(5 if axis == "col" else 6) + (0 if scale == EPS / 2.0 else 3),
            has_side_effects=True,
            vmem_limit_bytes=VMEM_LIMIT),
    )(p, q, a, mass, sq)


def squares(values):
    return jnp.sum(jnp.square(values.astype(jnp.float32)), axis=1)


def _peer(axis, k):
    if axis == "col":
        return (lax.axis_index("row"), k)
    return (k, lax.axis_index("col"))


def _gather_lse_kernel(axis, n, x_ref, m_ref, q_ref, o_ref, buf, send, recv):
    me = lax.axis_index(axis)
    barrier = pltpu.get_barrier_semaphore()
    for d in range(1, n):
        pl.semaphore_signal(barrier, inc=1, device_id=_peer(axis, lax.rem(me + d, n)),
                            device_id_type=pl.DeviceIdType.MESH)
    pl.semaphore_wait(barrier, n - 1)
    copies = []
    for d in range(1, n):
        copy = pltpu.make_async_remote_copy(
            src_ref=x_ref, dst_ref=buf.at[me], send_sem=send.at[d], recv_sem=recv.at[me],
            device_id=_peer(axis, lax.rem(me + d, n)), device_id_type=pl.DeviceIdType.MESH)
        copy.start()
        copies.append(copy)
    for copy in copies:
        copy.wait_send()
    for d in range(1, n):
        src = lax.rem(me + n - d, n)
        pltpu.make_async_remote_copy(
            src_ref=x_ref, dst_ref=buf.at[src], send_sem=send.at[d], recv_sem=recv.at[src],
            device_id=_peer(axis, src), device_id_type=pl.DeviceIdType.MESH).wait_recv()
    buf[me] = x_ref[...]
    parts = buf[...]
    top = jnp.max(parts, axis=0)
    total = top + jnp.log(jnp.sum(jnp.exp(parts - top[None]), axis=0))
    o_ref[...] = (EPS * (m_ref[...] - total) - q_ref[...]) * INV


def _exchange_kernel(jobs, *refs):
    count = len(jobs)
    ins, outs = refs[:count], refs[count:2 * count]
    gathers = sum(kind == "gather" for _, _, kind in jobs)
    sqs = refs[2 * count:2 * count + gathers]
    rest = refs[2 * count + gathers:]
    bufs, sends, recvs = rest[0::3], rest[1::3], rest[2::3]
    barrier = pltpu.get_barrier_semaphore()
    for axis, n, kind in jobs:
        me = lax.axis_index(axis)
        for d in range(1, n):
            pl.semaphore_signal(barrier, inc=1, device_id=_peer(axis, lax.rem(me + d, n)),
                                device_id_type=pl.DeviceIdType.MESH)
    pl.semaphore_wait(barrier, sum(n - 1 for _, n, _ in jobs))

    def copy(job, d, peer, slot):
        axis, n, kind = jobs[job]
        src = ins[job] if kind == "gather" else ins[job].at[peer]
        return pltpu.make_async_remote_copy(
            src_ref=src, dst_ref=bufs[job].at[slot], send_sem=sends[job].at[d],
            recv_sem=recvs[job].at[slot], device_id=_peer(axis, peer),
            device_id_type=pl.DeviceIdType.MESH)

    started = []
    for job, (axis, n, kind) in enumerate(jobs):
        me = lax.axis_index(axis)
        for d in range(1, n):
            started.append(copy(job, d, lax.rem(me + d, n), me))
            started[-1].start()
    for c in started:
        c.wait_send()
    for job, (axis, n, kind) in enumerate(jobs):
        me = lax.axis_index(axis)
        for d in range(1, n):
            src = lax.rem(me + n - d, n)
            copy(job, d, src, src).wait_recv()
        if kind == "gather":
            bufs[job][me] = ins[job][...]
            outs[job][...] = bufs[job][...]
            sq = sqs[job]
            m = bufs[job].shape[1]
            per = sq.shape[1] // m
            for j in range(n):
                v = bufs[job][j].astype(jnp.float32)
                row = _to_row(jnp.sum(v * v, axis=1, keepdims=True))
                sq[j // per:j // per + 1, (j % per) * m:(j % per + 1) * m] = row
        else:
            bufs[job][me] = ins[job][me]
            outs[job][...] = jnp.sum(bufs[job][...], axis=0)


def exchange(jobs, arrays, collective_id):
    shapes, scratch = [], []
    for (axis, n, kind), x in zip(jobs, arrays):
        block = x.shape if kind == "gather" else x.shape[1:]
        shapes.append(jax.ShapeDtypeStruct((n,) + block if kind == "gather" else block, x.dtype))
        scratch += [pltpu.VMEM((n,) + block, x.dtype), pltpu.SemaphoreType.DMA((n,)),
                    pltpu.SemaphoreType.DMA((n,))]
    for (axis, n, kind), x in zip(jobs, arrays):
        if kind == "gather":
            shapes.append(jax.ShapeDtypeStruct((8, n * x.shape[0] // 8), jnp.float32))
    return pl.pallas_call(
        functools.partial(_exchange_kernel, tuple(jobs)),
        out_shape=tuple(shapes),
        in_specs=[pl.BlockSpec(memory_space=pltpu.VMEM)] * len(jobs),
        out_specs=tuple(pl.BlockSpec(memory_space=pltpu.VMEM) for _ in shapes),
        scratch_shapes=scratch,
        compiler_params=pltpu.CompilerParams(
            collective_id=collective_id, has_side_effects=True, vmem_limit_bytes=VMEM_LIMIT),
    )(*arrays)


def combine(block, axis, log_mass, sq):
    n = lax.axis_size(axis)
    return pl.pallas_call(
        functools.partial(_gather_lse_kernel, axis, n),
        out_shape=jax.ShapeDtypeStruct(block.shape, jnp.float32),
        in_specs=[pl.BlockSpec(memory_space=pltpu.VMEM)] * 3,
        out_specs=pl.BlockSpec(memory_space=pltpu.VMEM),
        scratch_shapes=[
            pltpu.VMEM((n,) + block.shape, jnp.float32),
            pltpu.SemaphoreType.DMA((n,)),
            pltpu.SemaphoreType.DMA((n,)),
        ],
        compiler_params=pltpu.CompilerParams(
            collective_id=0 if axis == "col" else 1, has_side_effects=True),
    )(block, log_mass, sq)


def local(imu, camera, imu_mass, cam_mass):
    n_col, n_row = lax.axis_size("col"), lax.axis_size("row")
    imu_rows, cam_rows, rows_sq, cols_sq = exchange(
        [("col", n_col, "gather"), ("row", n_row, "gather")], [imu, camera[0]], 3)
    imu_rows = imu_rows.reshape(-1, D)
    cam_rows = cam_rows.reshape(-1, D)
    a, scale = cols_sq, -INV * EPS / 2.0
    for step in range(ITERS):
        u = lse_combine(imu_rows, cam_rows, a, imu_mass, rows_sq, "col", scale)
        a = lse_combine(cam_rows, imu_rows, u, cam_mass, cols_sq, "row")
        scale = EPS / 2.0

    grad_imu, grad_cam = plan_scatter(imu_rows, cam_rows, u, a, n_col, n_row)
    return (grad_imu, grad_cam[None])


def solution(mesh):
    in_specs = (P(("row", "col"), None), P("col", "row", None), P("row"), P("col"))
    out_specs = (P(("row", "col"), None), P("col", "row", None))
    return jax.shard_map(local, mesh=mesh, in_specs=in_specs, out_specs=out_specs, check_vma=False)
```
